32 devices in a mesh: grp: 2 (over y), seq: 4 (over z), head: 4 (over x, core).
Axes of the slice: x: 2, y: 2, z: 4, core: 2. Of those that a mesh axis runs over, the one named last changes fastest.
Arguments:
- queries: bfloat16 [3072, 4096], P(('grp', 'seq'), 'head'), parts along dimension 0, may hold values from -6 to 6
- keys: bfloat16 [3072, 2048], P(('grp', 'seq'), 'head'), parts along dimension 0, may hold values from -6 to 6
- values: bfloat16 [3072, 2048], P(('grp', 'seq'), 'head'), parts along dimension 0, may hold values from -16 to 16
- out_weight: bfloat16 [4096, 5376], P('head'), may hold values from -0.5 to 0.5
Outputs:
- mixed: bfloat16 [3072, 5376], P(('grp', 'seq', 'head')), parts along dimension 0
The draws below stay inside these ranges and needn't reach their ends.
There are 2 independent parts, one for each index of `grp`. The reference program is written for one: setup_inputs(seed, part) draws one part's arguments, and reference() takes and returns one part's arrays. A program takes and returns all parts, laid end to end along the dimension named above; an argument that names none is the same for every part. Nothing has to cross between parts.
All inputs are finite; a program needn't handle non-finite values.
Results may differ from the reference program's by a relative error of at most 0.02.
Values may be sent and summed in bfloat16 or wider, within the bound.
No kernel may reach another device: no remote copies, remote signals or barrier semaphores. Data moves between devices by JAX's collectives and lax.ppermute only.
A program may use at most 64 MiB of HBM per device.

```python
import jax
import jax.numpy as jnp
from jax import lax

D = 5376
QUERY_HEADS = 32
KEY_VALUE_HEADS = 16
HEAD_SIZE = 128
BLOCK_TOKENS = 384
SEQUENCE_TOKENS = 1536
N_SEQ = 4
N_HEAD = 4


def paired_draw(key):
    base = jax.random.fold_in(key, 11)
    query_seed, key_random_seed = jax.random.split(base, 2)
    query_drawn = jnp.clip(jax.random.normal(query_seed, (SEQUENCE_TOKENS, QUERY_HEADS * HEAD_SIZE), jnp.float32), -4.0, 4.0)
    sampled_keys = jnp.clip(jax.random.normal(key_random_seed, (SEQUENCE_TOKENS, KEY_VALUE_HEADS * HEAD_SIZE), jnp.float32), -4.0, 4.0)
    return (query_drawn, sampled_keys)


def draw_queries(key, part):
    return paired_draw(key)[0].astype(jnp.bfloat16)


def draw_keys(key, part):
    return paired_draw(key)[1].astype(jnp.bfloat16)


def steps_of(stream_key, shape, cuts, smallest, high):
    loudness, own = 1.0, jax.random.fold_in(stream_key, 6)
    for position, blocks in cuts:
        steps = jnp.exp(jax.random.uniform(jax.random.fold_in(own, position), (blocks,), jnp.float32, smallest / len(cuts), high / len(cuts)))
        loudness = loudness * jnp.repeat(steps, shape[position] // blocks).reshape([-1 if axis == position else 1 for axis in range(len(shape))])
    return loudness


def gaussian(rng, dims, deviation, bound, cuts=(), held_as=jnp.bfloat16):
    drawn = deviation * jax.random.normal(rng, dims, jnp.float32)
    if cuts:
        drawn = drawn * steps_of(rng, dims, cuts, -0.22, 0.18)
    return jnp.clip(drawn, -bound, bound).astype(held_as)


def setup_inputs(seed: int = 0, part: int = 0) -> dict:
    seeds = jax.random.split(jax.random.key(seed), 5)
    part_splits = jax.random.split(jax.random.fold_in(seeds[4], part), 5)
    return {
        "queries": draw_queries(jax.random.fold_in(jax.random.fold_in(seeds[4], part), 71), part),
        "keys": draw_keys(jax.random.fold_in(jax.random.fold_in(seeds[4], part), 71), part),
        "values": gaussian(part_splits[2], (SEQUENCE_TOKENS, KEY_VALUE_HEADS * HEAD_SIZE), 4.0, 16.0, ((0, 4), (1, 4))),
        "out_weight": gaussian(seeds[3], (QUERY_HEADS * HEAD_SIZE, D), HEAD_SIZE ** -0.5, 0.5, ((0, 4),)),
    }


attn_scale = 168.0 ** -0.5


def block_attention(block, queries, keys, values):
    distances = [0] + [1 << step_level for step_level in range(N_SEQ.bit_length() - 1)]
    begin = (block * BLOCK_TOKENS).astype(jnp.int32)
    query_row_block = lax.dynamic_slice_in_dim(queries, begin, BLOCK_TOKENS, 0).astype(jnp.float32)
    causal = jnp.arange(BLOCK_TOKENS)[:, None] >= jnp.arange(BLOCK_TOKENS)[None, :]
    key_parts = []
    value_parts = []
    mask_parts = []
    for distance in distances:
        source = (jnp.maximum(block - distance, 0) * BLOCK_TOKENS).astype(jnp.int32)
        key_parts.append(lax.dynamic_slice_in_dim(keys, source, BLOCK_TOKENS, 0))
        value_parts.append(lax.dynamic_slice_in_dim(values, source, BLOCK_TOKENS, 0))
        if distance == 0:
            mask_parts.append(causal)
        else:
            mask_parts.append(jnp.broadcast_to(block >= distance, (BLOCK_TOKENS, BLOCK_TOKENS)))
    full_keys = jnp.concatenate(key_parts, axis=0).astype(jnp.float32)
    full_values = jnp.concatenate(value_parts, axis=0).astype(jnp.float32)
    visible = jnp.concatenate(mask_parts, axis=1)
    group_width = QUERY_HEADS // KEY_VALUE_HEADS
    query_head_stack = query_row_block.reshape(BLOCK_TOKENS, KEY_VALUE_HEADS, group_width, HEAD_SIZE)
    key_head_stack = full_keys.reshape(-1, KEY_VALUE_HEADS, HEAD_SIZE)
    value_head_stack = full_values.reshape(-1, KEY_VALUE_HEADS, HEAD_SIZE)
    scores = jnp.einsum("tkgd,skd->kgts", query_head_stack, key_head_stack) * attn_scale
    masked = jnp.where(visible, scores, -jnp.inf)
    row_max = jnp.max(masked, axis=-1, keepdims=True)
    shifted = jnp.exp(masked - row_max)
    row_sum = jnp.sum(shifted, axis=-1, keepdims=True)
    weights = (shifted / row_sum).astype(jnp.bfloat16).astype(jnp.float32)
    attended = jnp.einsum("kgts,skd->tkgd", weights, value_head_stack)
    return attended.astype(jnp.bfloat16).reshape(BLOCK_TOKENS, QUERY_HEADS * HEAD_SIZE)


def reference(queries, keys, values, out_weight):
    blocks = jnp.arange(N_SEQ, dtype=jnp.int32)
    attended = lax.map(lambda block: block_attention(block, queries, keys, values), blocks)
    attended = attended.reshape(SEQUENCE_TOKENS, QUERY_HEADS * HEAD_SIZE)
    band = QUERY_HEADS * HEAD_SIZE // N_HEAD

    def add_group(carry, group_index):
        start_col = (group_index * band).astype(jnp.int32)
        picked = lax.dynamic_slice_in_dim(attended, start_col, band, 1)
        weight_rows = lax.dynamic_slice_in_dim(out_weight, start_col, band, 0)
        partial_value = jnp.dot(picked, weight_rows, preferred_element_type=jnp.float32)
        partial_value = lax.optimization_barrier(partial_value.astype(jnp.bfloat16)).astype(jnp.float32)
        return carry + partial_value, None

    summed, _ = lax.scan(add_group, jnp.zeros((SEQUENCE_TOKENS, D), jnp.float32), jnp.arange(N_HEAD, dtype=jnp.int32))
    return summed.astype(jnp.bfloat16)
```

```python
import functools
import math

import jax
import jax.numpy as jnp
from jax import lax
from jax.experimental import pallas as pl
from jax.experimental.pallas import tpu as pltpu
from jax.sharding import PartitionSpec as P

QUERY_HEADS = 32
KEY_VALUE_HEADS = 16
HEAD_SIZE = 128
GROUP = QUERY_HEADS // KEY_VALUE_HEADS
CORES = 2

SCALE2 = 168.0**-0.5 * math.log2(math.e)


def pass_on(value, distance):
    count = lax.axis_size("seq")
    return lax.ppermute(value, "seq", [(s, s + distance) for s in range(distance, count - distance)])


def shifted(value):
    count = lax.axis_size("seq")
    return lax.ppermute(value, "seq", [(s, s + 1) for s in range(count - 1)])


def stacked(q_ref):
    return jnp.concatenate([q_ref[:, g * HEAD_SIZE : (g + 1) * HEAD_SIZE] for g in range(GROUP)], axis=0)


def scores_of(q, k):
    return lax.dot_general(q, k, (((1,), (1,)), ((), ())), preferred_element_type=jnp.float32) * SCALE2


def near_kernel(sources, place_ref, pos_ref, q_ref, *refs):
    k_refs, v_refs = refs[: len(sources)], refs[len(sources) : 2 * len(sources)]
    stat_ref, o_ref = refs[2 * len(sources) :]
    rows = q_ref.shape[0]
    q = stacked(q_ref)
    pos = jnp.concatenate([pos_ref[...]] * GROUP, axis=0)
    place = place_ref[0]
    parts = []
    for distance, k_ref in zip(sources, k_refs):
        s = scores_of(q, k_ref[...])
        if distance == 0:
            s = jnp.where(pos >= lax.broadcasted_iota(jnp.int32, s.shape, 1), s, -jnp.inf)
        else:
            s = s + jnp.where(place >= distance, 0.0, -jnp.inf)
        parts.append(s)
    top = functools.reduce(jnp.maximum, [jnp.max(s, axis=1, keepdims=True) for s in parts])
    total, acc = 0.0, 0.0
    for s, v_ref in zip(parts, v_refs):
        p = jnp.exp2(s - top)
        total = total + jnp.sum(p, axis=1, keepdims=True)
        acc = acc + jnp.dot(p.astype(jnp.bfloat16), v_ref[...], preferred_element_type=jnp.float32)
    stat_ref[0] = jnp.concatenate([top, total], axis=1)
    for g in range(GROUP):
        o_ref[:, g * HEAD_SIZE : (g + 1) * HEAD_SIZE] = acc[g * rows : (g + 1) * rows]


def far_scores_kernel(distance, place_ref, q_ref, k_ref, stat_ref, o_ref, w_ref, os_ref):
    rows = q_ref.shape[0]
    s = scores_of(stacked(q_ref), k_ref[...])
    s = s + jnp.where(place_ref[0] >= distance, 0.0, -jnp.inf)
    top, total = stat_ref[0, :, 0:1], stat_ref[0, :, 1:2]
    new_top = jnp.maximum(top, jnp.max(s, axis=1, keepdims=True))
    p = jnp.exp2(s - new_top)
    keep = jnp.exp2(top - new_top)
    inverse = 1.0 / (total * keep + jnp.sum(p, axis=1, keepdims=True))
    w_ref[0] = (p * inverse).astype(jnp.bfloat16)
    factor = keep * inverse
    for g in range(GROUP):
        columns = slice(g * HEAD_SIZE, (g + 1) * HEAD_SIZE)
        os_ref[:, columns] = o_ref[:, columns] * factor[g * rows : (g + 1) * rows]


def far_values_kernel(os_ref, w_ref, v_ref, att_ref):
    rows = os_ref.shape[0]
    acc = jnp.dot(w_ref[0], v_ref[...], preferred_element_type=jnp.float32)
    for g in range(GROUP):
        columns = slice(g * HEAD_SIZE, (g + 1) * HEAD_SIZE)
        att_ref[:, columns] = (os_ref[:, columns] + acc[g * rows : (g + 1) * rows]).astype(jnp.bfloat16)


def project_kernel(att_ref, w_ref, *out_refs):
    part = out_refs[0].shape[0]
    product = jnp.dot(att_ref[...], w_ref[...], preferred_element_type=jnp.float32)
    for i, out_ref in enumerate(out_refs):
        out_ref[...] = product[i * part : (i + 1) * part].astype(jnp.bfloat16)


def attend(place, pos, queries, keys, values, far_keys_of):
    rows = queries.shape[0]
    kv_local = keys.shape[1] // HEAD_SIZE
    wide = GROUP * HEAD_SIZE
    smem = pl.BlockSpec(memory_space=pltpu.SMEM)
    q_spec = pl.BlockSpec((rows, wide), lambda i: (0, i))
    kv_spec = pl.BlockSpec((rows, HEAD_SIZE), lambda i: (0, i))
    stat_spec = pl.BlockSpec((1, GROUP * rows, 2), lambda i: (i, 0, 0))
    w_spec = pl.BlockSpec((1, GROUP * rows, rows), lambda i: (i, 0, 0))
    stat_shape = jax.ShapeDtypeStruct((kv_local, GROUP * rows, 2), jnp.float32)
    o_shape = jax.ShapeDtypeStruct((rows, kv_local * wide), jnp.float32)

    sources, near_keys, near_values, far = far_keys_of(keys, values)
    stat, o = pl.pallas_call(
        functools.partial(near_kernel, sources),
        grid=(kv_local,),
        in_specs=[smem, pl.BlockSpec((rows, 1), lambda i: (0, 0)), q_spec] + [kv_spec] * (2 * len(sources)),
        out_specs=[stat_spec, q_spec],
        out_shape=[stat_shape, o_shape],
        name="near",
    )(place, pos, queries, *near_keys, *near_values)
    distance, k_far, v_far = far
    weights, scaled = pl.pallas_call(
        functools.partial(far_scores_kernel, distance),
        grid=(kv_local,),
        in_specs=[smem, q_spec, kv_spec, stat_spec, q_spec],
        out_specs=[w_spec, q_spec],
        out_shape=[jax.ShapeDtypeStruct((kv_local, GROUP * rows, rows), jnp.bfloat16), o_shape],
        name="far_scores",
    )(place, queries, k_far, stat, o)
    return pl.pallas_call(
        far_values_kernel,
        grid=(kv_local,),
        in_specs=[q_spec, w_spec, kv_spec],
        out_specs=q_spec,
        out_shape=jax.ShapeDtypeStruct(o_shape.shape, jnp.bfloat16),
        name="far_values",
    )(scaled, weights, v_far)


def project(att, out_weight, part, start, count, tile):
    parts = att.shape[0] // part
    return pl.pallas_call(
        project_kernel,
        grid=(count,),
        in_specs=[
            pl.BlockSpec(att.shape, lambda j: (0, 0)),
            pl.BlockSpec((out_weight.shape[0], tile), lambda j: (0, start + j)),
        ],
        out_specs=[pl.BlockSpec((part, tile), lambda j: (0, j))] * parts,
        out_shape=[jax.ShapeDtypeStruct((part, count * tile), jnp.bfloat16)] * parts,
        name="project",
    )(att, out_weight)


def tile_of(width):
    return max(t for t in range(128, 1024, 128) if width % t == 0 and (t % 256 == 0 or width % 256))


def on_device(queries, keys, values, out_weight):
    rows = queries.shape[0]
    heads = lax.axis_size("head")
    seq_count = lax.axis_size("seq")
    place = lax.axis_index("seq")
    me = lax.axis_index("head")
    chips = heads // CORES
    part = rows // heads
    reaches = [1 << level for level in range(seq_count.bit_length() - 1)]

    chip, core = me // CORES, me % CORES
    owners = []
    for step in range(1, chips + 1):
        base = ((chip + step) % chips) * CORES
        owners += [base + 1 - core, base + core]
    q_blocks = [lax.dynamic_slice_in_dim(queries, owner * part, part, 0) for owner in owners]
    queries = jnp.concatenate(q_blocks, axis=0)
    pos = jnp.concatenate([owner * part + jnp.arange(part, dtype=jnp.int32) for owner in owners])[:, None]

    def arrivals(keys, values):
        k_now, v_now = shifted(keys), shifted(values)
        sources, near_k, near_v = [0], [keys], [values]
        for distance in reaches[:-1]:
            sources.append(distance)
            near_k.append(k_now)
            near_v.append(v_now)
            k_now, v_now = pass_on(k_now, distance), pass_on(v_now, distance)
        return sources, near_k, near_v, (reaches[-1], k_now, v_now)

    att = attend(place.astype(jnp.int32)[None], pos, queries, keys, values, arrivals)

    width = out_weight.shape[1]
    tile = tile_of(width)
    tiles = width // tile
    counts = [1] + [2] * ((tiles - 1) // 2) + [1] * ((tiles - 1) % 2)
    across = [(h, h ^ 1) for h in range(heads)]
    start = 0
    pieces = []
    for count in counts:
        parts = project(att, out_weight, part, start, count, tile)
        start += count
        total = None
        for step in range(1, chips + 1):
            theirs, mine = parts[2 * (step - 1)], parts[2 * (step - 1) + 1]
            got = lax.ppermute(theirs, "head", across)
            both = mine.astype(jnp.float32) + got.astype(jnp.float32)
            if step < chips:
                moves = [(h, (h + step * CORES) % heads) for h in range(heads)]
                both = lax.ppermute(both.astype(jnp.bfloat16), "head", moves).astype(jnp.float32)
            total = both if total is None else total + both
        pieces.append(total.astype(jnp.bfloat16))
    return jnp.concatenate(pieces, axis=1)


def solution(mesh):
    in_specs = (
        P(("grp", "seq"), "head"),
        P(("grp", "seq"), "head"),
        P(("grp", "seq"), "head"),
        P("head", None),
    )
    out_specs = P(("grp", "seq", "head"), None)
    return jax.shard_map(
        on_device, mesh=mesh, in_specs=in_specs, out_specs=out_specs, check_vma=False
    )
```

```python
import functools
import math

import jax
import jax.numpy as jnp
from jax import lax
from jax.experimental import pallas as pl
from jax.experimental.pallas import tpu as pltpu
from jax.sharding import PartitionSpec as P

QUERY_HEADS = 32
KEY_VALUE_HEADS = 16
HEAD_SIZE = 128
GROUP = QUERY_HEADS // KEY_VALUE_HEADS
CORES = 2

SCALE2 = 168.0**-0.5 * math.log2(math.e)


VMEM = pl.BlockSpec(memory_space=pltpu.VMEM)
SMEM = pl.BlockSpec(memory_space=pltpu.SMEM)


def in_vmem(value):
    return pltpu.with_memory_space_constraint(value, pltpu.VMEM)


def call(kernel, outs, *operands, scalars=0):
    operands = [value if i < scalars else in_vmem(value) for i, value in enumerate(operands)]
    return pl.pallas_call(
        kernel,
        in_specs=[SMEM] * scalars + [VMEM] * (len(operands) - scalars),
        out_specs=[VMEM] * len(outs),
        out_shape=[pltpu.VMEM(shape, dtype) for shape, dtype in outs],
        compiler_params=pltpu.CompilerParams(vmem_limit_bytes=20 << 20),
    )(*operands)


def stacked(q_ref, i):
    first = i * GROUP
    return jnp.concatenate(
        [q_ref[:, (first + g) * HEAD_SIZE : (first + g + 1) * HEAD_SIZE] for g in range(GROUP)], axis=0
    )


def head_of(ref, i):
    return ref[:, i * HEAD_SIZE : (i + 1) * HEAD_SIZE]


def scores_of(k, q):
    return lax.dot_general(k, q, (((1,), (1,)), ((), ())), preferred_element_type=jnp.float32) * SCALE2


def weigh(v, p):
    return lax.dot_general(v, p, (((0,), (0,)), ((), ())), preferred_element_type=jnp.float32)


def local_kernel(place_ref, pos_ref, q_ref, k_ref, v_ref, top_ref, total_ref, o_ref):
    for i in range(o_ref.shape[0]):
        s = scores_of(head_of(k_ref, i), stacked(q_ref, i))
        s = jnp.where(pos_ref[...] >= lax.broadcasted_iota(jnp.int32, s.shape, 0), s, -jnp.inf)
        top = jnp.max(s, axis=0, keepdims=True)
        p = jnp.exp2(s - top)
        top_ref[i] = top
        total_ref[i] = jnp.sum(p, axis=0, keepdims=True)
        o_ref[i] = weigh(head_of(v_ref, i), p.astype(jnp.bfloat16))


def seen(place_ref, distance):
    return jnp.where(place_ref[0] >= distance, 0.0, -jnp.inf).astype(jnp.float32)


def middle_kernel(distance, place_ref, q_ref, k_ref, v_ref, top_ref, total_ref, o_ref, top_out, total_out, o_out):
    for i in range(o_ref.shape[0]):
        s = scores_of(head_of(k_ref, i), stacked(q_ref, i)) + seen(place_ref, distance)
        old = top_ref[i]
        top = jnp.maximum(old, jnp.max(s, axis=0, keepdims=True))
        p = jnp.exp2(s - top)
        keep = jnp.exp2(old - top)
        top_out[i] = top
        total_out[i] = total_ref[i] * keep + jnp.sum(p, axis=0, keepdims=True)
        o_out[i] = o_ref[i] * keep + weigh(head_of(v_ref, i), p.astype(jnp.bfloat16))


def last_scores_kernel(distance, place_ref, q_ref, k_ref, top_ref, total_ref, o_ref, w_out, o_out):
    for i in range(o_ref.shape[0]):
        s = scores_of(head_of(k_ref, i), stacked(q_ref, i)) + seen(place_ref, distance)
        old = top_ref[i]
        top = jnp.maximum(old, jnp.max(s, axis=0, keepdims=True))
        p = jnp.exp2(s - top)
        keep = jnp.exp2(old - top)
        inverse = 1.0 / (total_ref[i] * keep + jnp.sum(p, axis=0, keepdims=True))
        w_out[i] = (p * inverse).astype(jnp.bfloat16)
        o_out[i] = o_ref[i] * (keep * inverse)


def put_product(att, w_ref, columns, out_refs):
    product = jnp.dot(att, w_ref[:, columns[0] : columns[1]], preferred_element_type=jnp.float32)
    part = out_refs[0].shape[0]
    for i, out_ref in enumerate(out_refs):
        out_ref[...] = product[i * part : (i + 1) * part].astype(jnp.bfloat16)


def last_values_kernel(columns, w_ref, o_ref, v_ref, weight_ref, att_ref, *out_refs):
    rows = att_ref.shape[0]
    for i in range(o_ref.shape[0]):
        o = (o_ref[i] + weigh(head_of(v_ref, i), w_ref[i])).T.astype(jnp.bfloat16)
        for g in range(GROUP):
            head = i * GROUP + g
            att_ref[:, head * HEAD_SIZE : (head + 1) * HEAD_SIZE] = o[g * rows : (g + 1) * rows]
    far = len(out_refs) * out_refs[0].shape[0]
    put_product(att_ref[0:far, :], weight_ref, columns, out_refs)


def project_kernel(first, columns, att_ref, weight_ref, *out_refs):
    count = len(out_refs) * out_refs[0].shape[0]
    put_product(att_ref[first : first + count, :], weight_ref, columns, out_refs)


def load_kernel(weight_ref, out_ref, sems):
    count = sems.shape[0]
    rows = weight_ref.shape[0] // count
    copies = []
    for i in range(count):
        block = pl.ds(i * rows, rows)
        copies.append(pltpu.make_async_copy(weight_ref.at[block], out_ref.at[block], sems.at[i]))
        copies[-1].start()
    for copy in copies:
        copy.wait()


def load(weight):
    return pl.pallas_call(
        load_kernel,
        in_specs=[pl.BlockSpec(memory_space=pltpu.HBM)],
        out_specs=VMEM,
        out_shape=pltpu.VMEM(weight.shape, weight.dtype),
        scratch_shapes=[pltpu.SemaphoreType.DMA((4,))],
        compiler_params=pltpu.CompilerParams(vmem_limit_bytes=1 << 20),
        name="load",
    )(pltpu.with_memory_space_constraint(weight, pltpu.HBM))


def finish_kernel(columns, first, mine_ref, got_ref, *refs):
    far_refs, (out_ref, staged, sem) = refs[: len(refs) - 3], refs[len(refs) - 3 :]
    if not first:
        far_refs = far_refs[:-1]
    total = mine_ref[:, columns[0] : columns[1]].astype(jnp.float32)
    total = total + got_ref[:, columns[0] : columns[1]].astype(jnp.float32)
    for far_ref in far_refs:
        total = total + far_ref[...].astype(jnp.float32)
    staged[...] = total.astype(jnp.bfloat16)
    copy = pltpu.make_async_copy(staged, out_ref.at[:, columns[0] : columns[1]], sem)
    copy.start()
    copy.wait()


def finish(columns, width, mine, got, far, out):
    operands = [in_vmem(value) for value in (mine, got, *far)]
    specs = [VMEM] * len(operands)
    aliases = {}
    if out is not None:
        aliases = {len(operands): 0}
        operands.append(out)
        specs.append(pl.BlockSpec(memory_space=pltpu.HBM))
    rows = mine.shape[0]
    return pl.pallas_call(
        functools.partial(finish_kernel, columns, out is None),
        in_specs=specs,
        out_specs=pl.BlockSpec(memory_space=pltpu.HBM),
        out_shape=jax.ShapeDtypeStruct((rows, width), jnp.bfloat16),
        scratch_shapes=[pltpu.VMEM((rows, columns[1] - columns[0]), jnp.bfloat16), pltpu.SemaphoreType.DMA],
        input_output_aliases=aliases,
        compiler_params=pltpu.CompilerParams(vmem_limit_bytes=8 << 20),
        name="finish",
    )(*operands)


def ring(value, axis, distance):
    count = lax.axis_size(axis)
    return lax.ppermute(value, axis, [(s, (s + distance) % count) for s in range(count)])


def swap(value):
    count = lax.axis_size("head")
    return lax.ppermute(value, "head", [(h, h ^ 1) for h in range(count)])


def tile_of(width):
    return max(t for t in range(128, 1024, 128) if width % t == 0 and (t % 256 == 0 or width % 256))


def on_device(queries, keys, values, out_weight):
    rows = queries.shape[0]
    heads = lax.axis_size("head")
    seq_count = lax.axis_size("seq")
    place = lax.axis_index("seq").astype(jnp.int32)[None]
    me = lax.axis_index("head")
    chips = heads // CORES
    part = rows // heads
    kv_local = keys.shape[1] // HEAD_SIZE
    reaches = [1 << level for level in range(seq_count.bit_length() - 1)]
    f32, bf16 = jnp.float32, jnp.bfloat16

    k_now, v_now = ring(keys, "seq", 1), ring(values, "seq", 1)

    chip, core = me // CORES, me % CORES
    owners = []
    for step in range(1, chips + 1):
        base = ((chip + step) % chips) * CORES
        owners += [base + 1 - core, base + core]
    q = jnp.concatenate([lax.dynamic_slice_in_dim(queries, owner * part, part, 0) for owner in owners], axis=0)
    pos = jnp.concatenate([owner * part + jnp.arange(part, dtype=jnp.int32) for owner in owners])
    pos = jnp.concatenate([pos] * GROUP)[None]
    q = in_vmem(q)

    line = (kv_local, 1, GROUP * rows)
    block = (kv_local, HEAD_SIZE, GROUP * rows)
    state = [(line, f32), (line, f32), (block, f32)]
    carried = call(local_kernel, state, place, pos, q, keys, values, scalars=1)
    for distance in reaches[:-1]:
        k_here, v_here = k_now, v_now
        k_now = ring(k_here, "seq", distance)
        v_now = ring(v_here, "seq", distance)
        carried = call(functools.partial(middle_kernel, distance), state, place, q, k_here, v_here, *carried, scalars=1)
    weights, scaled = call(
        functools.partial(last_scores_kernel, reaches[-1]),
        [((kv_local, rows, GROUP * rows), bf16), (block, f32)],
        place,
        q,
        k_now,
        *carried,
        scalars=1,
    )

    width = out_weight.shape[1]
    tile = tile_of(width)
    tiles = width // tile
    bounds = [0] + [tile * t for t in range(1, tiles + 1, 2)]
    if bounds[-1] != width:
        bounds.append(width)
    chunks = list(zip(bounds[:-1], bounds[1:]))
    far_parts = 2 * (chips - 1)
    out_weight = load(out_weight)

    def parts_of(count, columns):
        return [((part, columns[1] - columns[0]), bf16)] * count

    att, *first_far = call(
        functools.partial(last_values_kernel, chunks[0]),
        [(queries.shape, bf16)] + parts_of(far_parts, chunks[0]),
        weights,
        scaled,
        v_now,
        out_weight,
    )
    arrived = []
    for index, columns in enumerate(chunks):
        far = first_far
        if index:
            kernel = functools.partial(project_kernel, 0, columns)
            far = call(kernel, parts_of(far_parts, columns), att, out_weight)
        here = []
        for step in range(1, chips):
            theirs, mine = far[2 * step - 2], far[2 * step - 1]
            got = swap(theirs)
            both = (mine.astype(f32) + got.astype(f32)).astype(bf16)
            here.append(ring(both, "head", step * CORES))
        arrived.append(here)
    whole = (0, width)
    theirs, mine = call(functools.partial(project_kernel, far_parts * part, whole), parts_of(2, whole), att, out_weight)
    got = swap(theirs)
    out = None
    for columns, here in zip(chunks, arrived):
        out = finish(columns, width, mine, got, here, out)
    return out


def solution(mesh):
    in_specs = (
        P(("grp", "seq"), "head"),
        P(("grp", "seq"), "head"),
        P(("grp", "seq"), "head"),
        P("head", None),
    )
    out_specs = P(("grp", "seq", "head"), None)

    return jax.shard_map(on_device, mesh=mesh, in_specs=in_specs, out_specs=out_specs, check_vma=False)
```

```python
import functools
import math

import jax
import jax.numpy as jnp
from jax import lax
from jax.experimental import pallas as pl
from jax.experimental.pallas import tpu as pltpu
from jax.sharding import PartitionSpec as P

QUERY_HEADS = 32
KEY_VALUE_HEADS = 16
HEAD_SIZE = 128
GROUP = QUERY_HEADS // KEY_VALUE_HEADS
CORES = 2

SCALE2 = 168.0**-0.5 * math.log2(math.e)


VMEM = pl.BlockSpec(memory_space=pltpu.VMEM)
SMEM = pl.BlockSpec(memory_space=pltpu.SMEM)


def in_vmem(value):
    return pltpu.with_memory_space_constraint(value, pltpu.VMEM)


def loading(kernel, columns, *refs):
    source, (out_ref, sem), refs = refs[0], refs[-2:], refs[1:-2]
    copy = pltpu.make_async_copy(source.at[:, columns[0] : columns[1]], out_ref, sem)
    copy.start()
    kernel(*refs)
    copy.wait()


def call(kernel, outs, *operands, scalars=0, load=None):
    operands = [value if i < scalars else in_vmem(value) for i, value in enumerate(operands)]
    specs = [SMEM] * scalars + [VMEM] * (len(operands) - scalars)
    outs = [pltpu.VMEM(shape, dtype) for shape, dtype in outs]
    scratch = []
    if load is not None:
        source, columns = load
        kernel = functools.partial(loading, kernel, columns)
        operands = [pltpu.with_memory_space_constraint(source, pltpu.HBM)] + operands
        specs = [pl.BlockSpec(memory_space=pltpu.HBM)] + specs
        outs.append(pltpu.VMEM((source.shape[0], columns[1] - columns[0]), source.dtype))
        scratch = [pltpu.SemaphoreType.DMA]
    return pl.pallas_call(
        kernel,
        in_specs=specs,
        out_specs=[VMEM] * len(outs),
        out_shape=outs,
        scratch_shapes=scratch,
        compiler_params=pltpu.CompilerParams(vmem_limit_bytes=20 << 20),
    )(*operands)


def stacked(q_ref, i):
    first = i * GROUP
    return jnp.concatenate(
        [q_ref[:, (first + g) * HEAD_SIZE : (first + g + 1) * HEAD_SIZE] for g in range(GROUP)], axis=0
    )


def head_of(ref, i):
    return ref[:, i * HEAD_SIZE : (i + 1) * HEAD_SIZE]


def scores_of(k, q):
    return lax.dot_general(k, q, (((1,), (1,)), ((), ())), preferred_element_type=jnp.float32) * SCALE2


def weigh(v, p):
    return lax.dot_general(v, p, (((0,), (0,)), ((), ())), preferred_element_type=jnp.float32)


def local_kernel(place_ref, pos_ref, q_ref, k_ref, v_ref, top_ref, total_ref, o_ref):
    for i in range(o_ref.shape[0]):
        s = scores_of(head_of(k_ref, i), stacked(q_ref, i))
        s = jnp.where(pos_ref[...] >= lax.broadcasted_iota(jnp.int32, s.shape, 0), s, -jnp.inf)
        top = jnp.max(s, axis=0, keepdims=True)
        p = jnp.exp2(s - top)
        top_ref[i] = top
        total_ref[i] = jnp.sum(p, axis=0, keepdims=True)
        o_ref[i] = weigh(head_of(v_ref, i), p.astype(jnp.bfloat16))


def seen(place_ref, distance):
    return jnp.where(place_ref[0] >= distance, 0.0, -jnp.inf).astype(jnp.float32)


def middle_kernel(distance, place_ref, q_ref, k_ref, v_ref, top_ref, total_ref, o_ref, top_out, total_out, o_out):
    for i in range(o_ref.shape[0]):
        s = scores_of(head_of(k_ref, i), stacked(q_ref, i)) + seen(place_ref, distance)
        old = top_ref[i]
        top = jnp.maximum(old, jnp.max(s, axis=0, keepdims=True))
        p = jnp.exp2(s - top)
        keep = jnp.exp2(old - top)
        top_out[i] = top
        total_out[i] = total_ref[i] * keep + jnp.sum(p, axis=0, keepdims=True)
        o_out[i] = o_ref[i] * keep + weigh(head_of(v_ref, i), p.astype(jnp.bfloat16))


def last_scores_kernel(distance, place_ref, q_ref, k_ref, top_ref, total_ref, o_ref, w_out, o_out):
    for i in range(o_ref.shape[0]):
        s = scores_of(head_of(k_ref, i), stacked(q_ref, i)) + seen(place_ref, distance)
        old = top_ref[i]
        top = jnp.maximum(old, jnp.max(s, axis=0, keepdims=True))
        p = jnp.exp2(s - top)
        keep = jnp.exp2(old - top)
        inverse = 1.0 / (total_ref[i] * keep + jnp.sum(p, axis=0, keepdims=True))
        w_out[i] = (p * inverse).astype(jnp.bfloat16)
        o_out[i] = o_ref[i] * (keep * inverse)


def put_product(att, w_ref, columns, out_refs, out_first=0):
    product = jnp.dot(att, w_ref[:, columns[0] : columns[1]], preferred_element_type=jnp.float32)
    part = out_refs[0].shape[0]
    for i, out_ref in enumerate(out_refs):
        out_ref[:, out_first : out_first + columns[1] - columns[0]] = product[i * part : (i + 1) * part].astype(
            jnp.bfloat16
        )


def last_values_kernel(columns, w_ref, o_ref, v_ref, weight_ref, att_ref, *out_refs):
    rows = att_ref.shape[0]
    for i in range(o_ref.shape[0]):
        o = (o_ref[i] + weigh(head_of(v_ref, i), w_ref[i])).T.astype(jnp.bfloat16)
        for g in range(GROUP):
            head = i * GROUP + g
            att_ref[:, head * HEAD_SIZE : (head + 1) * HEAD_SIZE] = o[g * rows : (g + 1) * rows]
    far = len(out_refs) * out_refs[0].shape[0]
    put_product(att_ref[0:far, :], weight_ref, columns, out_refs)


def project_kernel(first, columns, att_ref, weight_ref, *out_refs):
    count = len(out_refs) * out_refs[0].shape[0]
    put_product(att_ref[first : first + count, :], weight_ref, columns, out_refs)


def project_whole_kernel(first, att_ref, left_ref, right_ref, *out_refs):
    count = len(out_refs) * out_refs[0].shape[0]
    att = att_ref[first : first + count, :]
    left, right = left_ref.shape[1], right_ref.shape[1]
    put_product(att, left_ref, (0, left), out_refs)
    put_product(att, right_ref, (0, right), out_refs, left)


def finish_kernel(columns, first, mine_ref, got_ref, *refs):
    far_refs, (out_ref, staged, sem) = refs[: len(refs) - 3], refs[len(refs) - 3 :]
    if not first:
        far_refs = far_refs[:-1]
    total = mine_ref[:, columns[0] : columns[1]].astype(jnp.float32)
    total = total + got_ref[:, columns[0] : columns[1]].astype(jnp.float32)
    for far_ref in far_refs:
        total = total + far_ref[...].astype(jnp.float32)
    staged[...] = total.astype(jnp.bfloat16)
    copy = pltpu.make_async_copy(staged, out_ref.at[:, columns[0] : columns[1]], sem)
    copy.start()
    copy.wait()


def finish(columns, width, mine, got, far, out):
    operands = [in_vmem(value) for value in (mine, got, *far)]
    specs = [VMEM] * len(operands)
    aliases = {}
    if out is not None:
        aliases = {len(operands): 0}
        operands.append(out)
        specs.append(pl.BlockSpec(memory_space=pltpu.HBM))
    rows = mine.shape[0]
    return pl.pallas_call(
        functools.partial(finish_kernel, columns, out is None),
        in_specs=specs,
        out_specs=pl.BlockSpec(memory_space=pltpu.HBM),
        out_shape=jax.ShapeDtypeStruct((rows, width), jnp.bfloat16),
        scratch_shapes=[pltpu.VMEM((rows, columns[1] - columns[0]), jnp.bfloat16), pltpu.SemaphoreType.DMA],
        input_output_aliases=aliases,
        compiler_params=pltpu.CompilerParams(vmem_limit_bytes=8 << 20),
        name="finish",
    )(*operands)


def ring(value, axis, distance):
    count = lax.axis_size(axis)
    return lax.ppermute(value, axis, [(s, (s + distance) % count) for s in range(count)])


def swap(value):
    count = lax.axis_size("head")
    return lax.ppermute(value, "head", [(h, h ^ 1) for h in range(count)])


def tile_of(width):
    return max(t for t in range(128, 1024, 128) if width % t == 0 and (t % 256 == 0 or width % 256))


def on_device(queries, keys, values, out_weight):
    rows = queries.shape[0]
    heads = lax.axis_size("head")
    seq_count = lax.axis_size("seq")
    place = lax.axis_index("seq").astype(jnp.int32)[None]
    me = lax.axis_index("head")
    chips = heads // CORES
    part = rows // heads
    kv_local = keys.shape[1] // HEAD_SIZE
    reaches = [1 << level for level in range(seq_count.bit_length() - 1)]
    f32, bf16 = jnp.float32, jnp.bfloat16

    k_now, v_now = ring(keys, "seq", 1), ring(values, "seq", 1)

    chip, core = me // CORES, me % CORES
    owners = []
    for step in range(1, chips + 1):
        base = ((chip + step) % chips) * CORES
        owners += [base + 1 - core, base + core]
    q = jnp.concatenate([lax.dynamic_slice_in_dim(queries, owner * part, part, 0) for owner in owners], axis=0)
    pos = jnp.concatenate([owner * part + jnp.arange(part, dtype=jnp.int32) for owner in owners])
    pos = jnp.concatenate([pos] * GROUP)[None]
    q = in_vmem(q)

    width = out_weight.shape[1]
    tile = tile_of(width)
    tiles = width // tile
    bounds = [0] + [tile * t for t in range(1, tiles + 1, 2)]
    if bounds[-1] != width:
        bounds.append(width)
    chunks = list(zip(bounds[:-1], bounds[1:]))
    far_parts = 2 * (chips - 1)
    border = bounds[len(bounds) // 2]
    halves = [(0, border), (border, width)]

    line = (kv_local, 1, GROUP * rows)
    block = (kv_local, HEAD_SIZE, GROUP * rows)
    state = [(line, f32), (line, f32), (block, f32)]
    *carried, left = call(local_kernel, state, place, pos, q, keys, values, scalars=1, load=(out_weight, halves[0]))
    right = None
    for distance in reaches[:-1]:
        k_here, v_here = k_now, v_now
        k_now = ring(k_here, "seq", distance)
        v_now = ring(v_here, "seq", distance)
        carried = call(
            functools.partial(middle_kernel, distance),
            state,
            place,
            q,
            k_here,
            v_here,
            *carried,
            scalars=1,
            load=(out_weight, halves[1]) if right is None else None,
        )
        if right is None:
            *carried, right = carried
    weights, scaled = call(
        functools.partial(last_scores_kernel, reaches[-1]),
        [((kv_local, rows, GROUP * rows), bf16), (block, f32)],
        place,
        q,
        k_now,
        *carried,
        scalars=1,
    )

    def weight_of(columns):
        side = int(columns[0] >= border)
        return (left, right)[side], (columns[0] - halves[side][0], columns[1] - halves[side][0])

    def parts_of(count, columns):
        return [((part, columns[1] - columns[0]), bf16)] * count

    weight, inner = weight_of(chunks[0])
    att, *first_far = call(
        functools.partial(last_values_kernel, inner),
        [(queries.shape, bf16)] + parts_of(far_parts, chunks[0]),
        weights,
        scaled,
        v_now,
        weight,
    )
    arrived = []
    for index, columns in enumerate(chunks):
        far = first_far
        if index:
            weight, inner = weight_of(columns)
            kernel = functools.partial(project_kernel, 0, inner)
            far = call(kernel, parts_of(far_parts, columns), att, weight)
        here = []
        for step in range(1, chips):
            theirs, mine = far[2 * step - 2], far[2 * step - 1]
            got = swap(theirs)
            both = (mine.astype(f32) + got.astype(f32)).astype(bf16)
            here.append(ring(both, "head", step * CORES))
        arrived.append(here)
    whole = (0, width)
    theirs, mine = call(functools.partial(project_whole_kernel, far_parts * part), parts_of(2, whole), att, left, right)
    got = swap(theirs)
    out = None
    for columns, here in zip(chunks, arrived):
        out = finish(columns, width, mine, got, here, out)
    return out


def solution(mesh):
    in_specs = (
        P(("grp", "seq"), "head"),
        P(("grp", "seq"), "head"),
        P(("grp", "seq"), "head"),
        P("head", None),
    )
    out_specs = P(("grp", "seq", "head"), None)

    return jax.shard_map(on_device, mesh=mesh, in_specs=in_specs, out_specs=out_specs, check_vma=False)
```

```python
import functools
import math

import jax
import jax.numpy as jnp
from jax import lax
from jax.experimental import pallas as pl
from jax.experimental.pallas import tpu as pltpu
from jax.sharding import PartitionSpec as P

QUERY_HEADS = 32
KEY_VALUE_HEADS = 16
HEAD_SIZE = 128
GROUP = QUERY_HEADS // KEY_VALUE_HEADS
CORES = 2

SCALE2 = 168.0**-0.5 * math.log2(math.e)


VMEM = pl.BlockSpec(memory_space=pltpu.VMEM)
SMEM = pl.BlockSpec(memory_space=pltpu.SMEM)


def in_vmem(value):
    return pltpu.with_memory_space_constraint(value, pltpu.VMEM)


def loading(kernel, columns, *refs):
    source, (out_ref, sems), refs = refs[0], refs[-2:], refs[1:-2]
    count = sems.shape[0]
    rows = source.shape[0] // count
    copies = []
    for i in range(count):
        block = pl.ds(i * rows, rows)
        copies.append(
            pltpu.make_async_copy(source.at[block, columns[0] : columns[1]], out_ref.at[block], sems.at[i])
        )
        copies[-1].start()
    kernel(*refs)
    for copy in copies:
        copy.wait()


def call(kernel, outs, *operands, scalars=0, load=None):
    operands = [value if i < scalars else in_vmem(value) for i, value in enumerate(operands)]
    specs = [SMEM] * scalars + [VMEM] * (len(operands) - scalars)
    outs = [pltpu.VMEM(shape, dtype) for shape, dtype in outs]
    scratch = []
    if load is not None:
        source, columns = load
        kernel = functools.partial(loading, kernel, columns)
        operands = [pltpu.with_memory_space_constraint(source, pltpu.HBM)] + operands
        specs = [pl.BlockSpec(memory_space=pltpu.HBM)] + specs
        outs.append(pltpu.VMEM((source.shape[0], columns[1] - columns[0]), source.dtype))
        scratch = [pltpu.SemaphoreType.DMA((8,))]
    return pl.pallas_call(
        kernel,
        in_specs=specs,
        out_specs=[VMEM] * len(outs),
        out_shape=outs,
        scratch_shapes=scratch,
        compiler_params=pltpu.CompilerParams(vmem_limit_bytes=20 << 20),
    )(*operands)


def stacked(q_ref, i):
    first = i * GROUP
    return jnp.concatenate(
        [q_ref[:, (first + g) * HEAD_SIZE : (first + g + 1) * HEAD_SIZE] for g in range(GROUP)], axis=0
    )


def head_of(ref, i):
    return ref[:, i * HEAD_SIZE : (i + 1) * HEAD_SIZE]


def scores_of(k, q):
    return lax.dot_general(k, q, (((1,), (1,)), ((), ())), preferred_element_type=jnp.float32) * SCALE2


def weigh(v, p):
    return lax.dot_general(v, p, (((0,), (0,)), ((), ())), preferred_element_type=jnp.float32)


def local_kernel(place_ref, pos_ref, q_ref, k_ref, v_ref, top_ref, total_ref, o_ref):
    for i in range(o_ref.shape[0]):
        s = scores_of(head_of(k_ref, i), stacked(q_ref, i))
        s = jnp.where(pos_ref[...] >= lax.broadcasted_iota(jnp.int32, s.shape, 0), s, -jnp.inf)
        top = jnp.max(s, axis=0, keepdims=True)
        p = jnp.exp2(s - top)
        top_ref[i] = top
        total_ref[i] = jnp.sum(p, axis=0, keepdims=True)
        o_ref[i] = weigh(head_of(v_ref, i), p.astype(jnp.bfloat16))


def seen(place_ref, distance):
    return jnp.where(place_ref[0] >= distance, 0.0, -jnp.inf).astype(jnp.float32)


def middle_kernel(distance, place_ref, q_ref, k_ref, v_ref, top_ref, total_ref, o_ref, top_out, total_out, o_out):
    for i in range(o_ref.shape[0]):
        s = scores_of(head_of(k_ref, i), stacked(q_ref, i)) + seen(place_ref, distance)
        old = top_ref[i]
        top = jnp.maximum(old, jnp.max(s, axis=0, keepdims=True))
        p = jnp.exp2(s - top)
        keep = jnp.exp2(old - top)
        top_out[i] = top
        total_out[i] = total_ref[i] * keep + jnp.sum(p, axis=0, keepdims=True)
        o_out[i] = o_ref[i] * keep + weigh(head_of(v_ref, i), p.astype(jnp.bfloat16))


def last_scores_kernel(distance, place_ref, q_ref, k_ref, top_ref, total_ref, o_ref, w_out, o_out):
    for i in range(o_ref.shape[0]):
        s = scores_of(head_of(k_ref, i), stacked(q_ref, i)) + seen(place_ref, distance)
        old = top_ref[i]
        top = jnp.maximum(old, jnp.max(s, axis=0, keepdims=True))
        p = jnp.exp2(s - top)
        keep = jnp.exp2(old - top)
        inverse = 1.0 / (total_ref[i] * keep + jnp.sum(p, axis=0, keepdims=True))
        w_out[i] = (p * inverse).astype(jnp.bfloat16)
        o_out[i] = o_ref[i] * (keep * inverse)


def put_product(att, w_ref, columns, out_refs, out_first=0):
    product = jnp.dot(att, w_ref[:, columns[0] : columns[1]], preferred_element_type=jnp.float32)
    part = out_refs[0].shape[0]
    for i, out_ref in enumerate(out_refs):
        out_ref[:, out_first : out_first + columns[1] - columns[0]] = product[i * part : (i + 1) * part].astype(
            jnp.bfloat16
        )


def last_values_kernel(columns, w_ref, o_ref, v_ref, weight_ref, att_ref, *out_refs):
    rows = att_ref.shape[0]
    for i in range(o_ref.shape[0]):
        o = (o_ref[i] + weigh(head_of(v_ref, i), w_ref[i])).T.astype(jnp.bfloat16)
        for g in range(GROUP):
            head = i * GROUP + g
            att_ref[:, head * HEAD_SIZE : (head + 1) * HEAD_SIZE] = o[g * rows : (g + 1) * rows]
    far = len(out_refs) * out_refs[0].shape[0]
    put_product(att_ref[0:far, :], weight_ref, columns, out_refs)


def project_kernel(first, columns, att_ref, weight_ref, *out_refs):
    count = len(out_refs) * out_refs[0].shape[0]
    put_product(att_ref[first : first + count, :], weight_ref, columns, out_refs)


def project_whole_kernel(first, att_ref, left_ref, right_ref, *out_refs):
    count = len(out_refs) * out_refs[0].shape[0]
    att = att_ref[first : first + count, :]
    left, right = left_ref.shape[1], right_ref.shape[1]
    put_product(att, left_ref, (0, left), out_refs)
    put_product(att, right_ref, (0, right), out_refs, left)


def finish_kernel(columns, first, mine_ref, got_ref, *refs):
    far_refs, (out_ref, staged, sem) = refs[: len(refs) - 3], refs[len(refs) - 3 :]
    if not first:
        far_refs = far_refs[:-1]
    total = mine_ref[:, columns[0] : columns[1]].astype(jnp.float32)
    total = total + got_ref[:, columns[0] : columns[1]].astype(jnp.float32)
    for far_ref in far_refs:
        total = total + far_ref[...].astype(jnp.float32)
    staged[...] = total.astype(jnp.bfloat16)
    copy = pltpu.make_async_copy(staged, out_ref.at[:, columns[0] : columns[1]], sem)
    copy.start()
    copy.wait()


def finish(columns, width, mine, got, far, out):
    operands = [in_vmem(value) for value in (mine, got, *far)]
    specs = [VMEM] * len(operands)
    aliases = {}
    if out is not None:
        aliases = {len(operands): 0}
        operands.append(out)
        specs.append(pl.BlockSpec(memory_space=pltpu.HBM))
    rows = mine.shape[0]
    return pl.pallas_call(
        functools.partial(finish_kernel, columns, out is None),
        in_specs=specs,
        out_specs=pl.BlockSpec(memory_space=pltpu.HBM),
        out_shape=jax.ShapeDtypeStruct((rows, width), jnp.bfloat16),
        scratch_shapes=[pltpu.VMEM((rows, columns[1] - columns[0]), jnp.bfloat16), pltpu.SemaphoreType.DMA],
        input_output_aliases=aliases,
        compiler_params=pltpu.CompilerParams(vmem_limit_bytes=8 << 20),
        name="finish",
    )(*operands)


def ring(value, axis, distance):
    count = lax.axis_size(axis)
    return lax.ppermute(value, axis, [(s, (s + distance) % count) for s in range(count)])


def pass_on(value, distance):
    count = lax.axis_size("seq")
    return lax.ppermute(value, "seq", [(s, s + distance) for s in range(distance, count - distance)])


def swap(value):
    count = lax.axis_size("head")
    return lax.ppermute(value, "head", [(h, h ^ 1) for h in range(count)])


def tile_of(width):
    return max(t for t in range(128, 1024, 128) if width % t == 0 and (t % 256 == 0 or width % 256))


def on_device(queries, keys, values, out_weight):
    rows = queries.shape[0]
    heads = lax.axis_size("head")
    seq_count = lax.axis_size("seq")
    place = lax.axis_index("seq").astype(jnp.int32)[None]
    me = lax.axis_index("head")
    chips = heads // CORES
    part = rows // heads
    kv_local = keys.shape[1] // HEAD_SIZE
    reaches = [1 << level for level in range(seq_count.bit_length() - 1)]
    f32, bf16 = jnp.float32, jnp.bfloat16

    k_now, v_now = ring(keys, "seq", 1), ring(values, "seq", 1)

    chip, core = me // CORES, me % CORES
    owners = []
    for step in range(1, chips + 1):
        base = ((chip + step) % chips) * CORES
        owners += [base + 1 - core, base + core]
    q = jnp.concatenate([lax.dynamic_slice_in_dim(queries, owner * part, part, 0) for owner in owners], axis=0)
    pos = jnp.concatenate([owner * part + jnp.arange(part, dtype=jnp.int32) for owner in owners])
    pos = jnp.concatenate([pos] * GROUP)[None]
    q = in_vmem(q)

    width = out_weight.shape[1]
    tile = tile_of(width)
    tiles = width // tile
    bounds = [0] + [tile * t for t in range(1, tiles, 2)] + [tile * (tiles - 1), width]
    bounds = sorted(set(bounds))
    chunks = list(zip(bounds[:-1], bounds[1:]))
    far_parts = 2 * (chips - 1)
    border = bounds[len(bounds) // 2]
    halves = [(0, border), (border, width)]

    line = (kv_local, 1, GROUP * rows)
    block = (kv_local, HEAD_SIZE, GROUP * rows)
    state = [(line, f32), (line, f32), (block, f32)]
    *carried, left = call(local_kernel, state, place, pos, q, keys, values, scalars=1, load=(out_weight, halves[0]))
    right = None
    for distance in reaches[:-1]:
        k_here, v_here = k_now, v_now
        k_now = pass_on(k_here, distance)
        v_now = pass_on(v_here, distance)
        carried = call(
            functools.partial(middle_kernel, distance),
            state,
            place,
            q,
            k_here,
            v_here,
            *carried,
            scalars=1,
            load=(out_weight, halves[1]) if right is None else None,
        )
        if right is None:
            *carried, right = carried
    weights, scaled = call(
        functools.partial(last_scores_kernel, reaches[-1]),
        [((kv_local, rows, GROUP * rows), bf16), (block, f32)],
        place,
        q,
        k_now,
        *carried,
        scalars=1,
    )

    def weight_of(columns):
        side = int(columns[0] >= border)
        return (left, right)[side], (columns[0] - halves[side][0], columns[1] - halves[side][0])

    def parts_of(count, columns):
        return [((part, columns[1] - columns[0]), bf16)] * count

    weight, inner = weight_of(chunks[0])
    att, *first_far = call(
        functools.partial(last_values_kernel, inner),
        [(queries.shape, bf16)] + parts_of(far_parts, chunks[0]),
        weights,
        scaled,
        v_now,
        weight,
    )
    arrived = []
    for index, columns in enumerate(chunks):
        far = first_far
        if index:
            weight, inner = weight_of(columns)
            kernel = functools.partial(project_kernel, 0, inner)
            far = call(kernel, parts_of(far_parts, columns), att, weight)
        here = []
        for step in range(1, chips):
            theirs, mine = far[2 * step - 2], far[2 * step - 1]
            got = swap(theirs)
            both = (mine.astype(f32) + got.astype(f32)).astype(bf16)
            here.append(ring(both, "head", step * CORES))
        arrived.append(here)
    whole = (0, width)
    theirs, mine = call(functools.partial(project_whole_kernel, far_parts * part), parts_of(2, whole), att, left, right)
    got = swap(theirs)
    out = None
    for columns, here in zip(chunks, arrived):
        out = finish(columns, width, mine, got, here, out)
    return out


def solution(mesh):
    in_specs = (
        P(("grp", "seq"), "head"),
        P(("grp", "seq"), "head"),
        P(("grp", "seq"), "head"),
        P("head", None),
    )
    out_specs = P(("grp", "seq", "head"), None)

    return jax.shard_map(on_device, mesh=mesh, in_specs=in_specs, out_specs=out_specs, check_vma=False)
```

```python
import functools
import math

import jax
import jax.numpy as jnp
from jax import lax
from jax.experimental import pallas as pl
from jax.experimental.pallas import tpu as pltpu
from jax.sharding import PartitionSpec as P

QUERY_HEADS = 32
KEY_VALUE_HEADS = 16
HEAD_SIZE = 128
GROUP = QUERY_HEADS // KEY_VALUE_HEADS
CORES = 2

SCALE2 = 168.0**-0.5 * math.log2(math.e)


VMEM = pl.BlockSpec(memory_space=pltpu.VMEM)
SMEM = pl.BlockSpec(memory_space=pltpu.SMEM)


def in_vmem(value):
    return pltpu.with_memory_space_constraint(value, pltpu.VMEM)


def loading(kernel, *refs):
    source, (out_ref, sems), refs = refs[0], refs[-2:], refs[1:-2]
    count = sems.shape[0]
    rows = source.shape[0] // count
    copies = []
    for i in range(count):
        block = pl.ds(i * rows, rows)
        copies.append(pltpu.make_async_copy(source.at[block], out_ref.at[block], sems.at[i]))
        copies[-1].start()
    kernel(*refs)
    for copy in copies:
        copy.wait()


def call(kernel, outs, *operands, scalars=0, load=None):
    operands = [value if i < scalars else in_vmem(value) for i, value in enumerate(operands)]
    specs = [SMEM] * scalars + [VMEM] * (len(operands) - scalars)
    outs = [pltpu.VMEM(shape, dtype) for shape, dtype in outs]
    scratch = []
    if load is not None:
        kernel = functools.partial(loading, kernel)
        operands = [pltpu.with_memory_space_constraint(load, pltpu.HBM)] + operands
        specs = [pl.BlockSpec(memory_space=pltpu.HBM)] + specs
        outs.append(pltpu.VMEM(load.shape, load.dtype))
        scratch = [pltpu.SemaphoreType.DMA((4,))]
    return pl.pallas_call(
        kernel,
        in_specs=specs,
        out_specs=[VMEM] * len(outs),
        out_shape=outs,
        scratch_shapes=scratch,
        compiler_params=pltpu.CompilerParams(vmem_limit_bytes=20 << 20),
    )(*operands)


def stacked(q_ref, i):
    first = i * GROUP
    return jnp.concatenate(
        [q_ref[:, (first + g) * HEAD_SIZE : (first + g + 1) * HEAD_SIZE] for g in range(GROUP)], axis=0
    )


def head_of(ref, i):
    return ref[:, i * HEAD_SIZE : (i + 1) * HEAD_SIZE]


def scores_of(k, q):
    return lax.dot_general(k, q, (((1,), (1,)), ((), ())), preferred_element_type=jnp.float32) * SCALE2


def weigh(v, p):
    return lax.dot_general(v, p, (((0,), (0,)), ((), ())), preferred_element_type=jnp.float32)


def thirds(value):
    high = value.astype(jnp.bfloat16).astype(jnp.float32)
    middle = (value - high).astype(jnp.bfloat16).astype(jnp.float32)
    return [high, middle, value - high - middle]


PACKED = HEAD_SIZE + 16


def put_heads(att_ref, i, o):
    rows = att_ref.shape[0]
    o = o.T.astype(jnp.bfloat16)
    for g in range(GROUP):
        head = i * GROUP + g
        att_ref[:, head * HEAD_SIZE : (head + 1) * HEAD_SIZE] = o[g * rows : (g + 1) * rows]


def local_part(pos_ref, q_ref, k_ref, v_ref, i):
    s = scores_of(head_of(k_ref, i), stacked(q_ref, i))
    s = jnp.where(pos_ref[...] >= lax.broadcasted_iota(jnp.int32, s.shape, 0), s, -jnp.inf)
    top = jnp.max(s, axis=0, keepdims=True)
    p = jnp.exp2(s - top)
    return top, jnp.sum(p, axis=0, keepdims=True), weigh(head_of(v_ref, i), p.astype(jnp.bfloat16))


def local_kernel(sets, place_ref, k_ref, v_ref, *refs):
    inputs, outputs = refs[: 2 * sets], refs[2 * sets :]
    top_ref, total_ref, o_ref = outputs[:3]
    for i in range(o_ref.shape[0]):
        top_ref[i], total_ref[i], o_ref[i] = local_part(*inputs[:2], k_ref, v_ref, i)
        if sets == 2:
            pack_ref, att_ref = outputs[3:]
            top, total, o = local_part(*inputs[2:], k_ref, v_ref, i)
            pack_ref[i, 0:HEAD_SIZE] = o.astype(jnp.bfloat16)
            lines = thirds(top) + thirds(total)
            lines.append(jnp.zeros((PACKED - HEAD_SIZE - len(lines), top.shape[1]), jnp.float32))
            pack_ref[i, HEAD_SIZE:PACKED] = jnp.concatenate(lines, axis=0).astype(jnp.bfloat16)
            put_heads(att_ref, i, o * (1.0 / total))


def early_kernel(chips, distances, columns, place_ref, q_ref, *refs):
    count = len(distances)
    k_refs, v_refs = refs[:count], refs[count : 2 * count]
    pack_ref, weight_ref, att_ref, theirs_ref, mine_ref = refs[2 * count :]
    for i in range(pack_ref.shape[0]):
        q = stacked(q_ref, i)
        extra = pack_ref[i, HEAD_SIZE:PACKED].astype(jnp.float32)
        top = extra[0:1] + extra[1:2] + extra[2:3]
        total = extra[3:4] + extra[4:5] + extra[5:6]
        parts = [
            scores_of(head_of(k_ref, i), q) + jnp.where(place_ref[0] + 1 >= distance, 0.0, -jnp.inf)
            for distance, k_ref in zip(distances, k_refs)
        ]
        new_top = functools.reduce(jnp.maximum, [top] + [jnp.max(s, axis=0, keepdims=True) for s in parts])
        keep = jnp.exp2(top - new_top)
        total = total * keep
        o = pack_ref[i, 0:HEAD_SIZE].astype(jnp.float32) * keep
        for s, v_ref in zip(parts, v_refs):
            p = jnp.exp2(s - new_top)
            total = total + jnp.sum(p, axis=0, keepdims=True)
            o = o + weigh(head_of(v_ref, i), p.astype(jnp.bfloat16))
        put_heads(att_ref, i, o * (1.0 / total))
    put_pairs(chips, att_ref[...], weight_ref, columns, theirs_ref, mine_ref)


def put_pairs(chips, att, weight_ref, columns, theirs_ref, mine_ref):
    product = jnp.dot(att, weight_ref[:, columns[0] : columns[1]], preferred_element_type=jnp.float32)
    product = product.astype(jnp.bfloat16)
    part = att.shape[0] // (2 * chips)
    for chip in range(chips):
        block = slice(chip * part, (chip + 1) * part)
        theirs_ref[block, :] = product[2 * chip * part : (2 * chip + 1) * part]
        mine_ref[block, :] = product[(2 * chip + 1) * part : (2 * chip + 2) * part]


def own_kernel(chips, place_ref, att_ref, weight_ref, theirs_ref, mine_ref):
    @pl.when(place_ref[0] == 0)
    def _():
        put_pairs(chips, att_ref[...], weight_ref, (0, weight_ref.shape[1]), theirs_ref, mine_ref)


def pairs_kernel(chips, columns, att_ref, weight_ref, theirs_ref, mine_ref):
    put_pairs(chips, att_ref[...], weight_ref, columns, theirs_ref, mine_ref)


def seen(place_ref, distance):
    return jnp.where(place_ref[0] >= distance, 0.0, -jnp.inf).astype(jnp.float32)


def middle_kernel(distance, place_ref, q_ref, k_ref, v_ref, top_ref, total_ref, o_ref, top_out, total_out, o_out):
    for i in range(o_ref.shape[0]):
        s = scores_of(head_of(k_ref, i), stacked(q_ref, i)) + seen(place_ref, distance)
        old = top_ref[i]
        top = jnp.maximum(old, jnp.max(s, axis=0, keepdims=True))
        p = jnp.exp2(s - top)
        keep = jnp.exp2(old - top)
        top_out[i] = top
        total_out[i] = total_ref[i] * keep + jnp.sum(p, axis=0, keepdims=True)
        o_out[i] = o_ref[i] * keep + weigh(head_of(v_ref, i), p.astype(jnp.bfloat16))


def last_scores_kernel(distance, place_ref, q_ref, k_ref, top_ref, total_ref, o_ref, w_out, o_out):
    for i in range(o_ref.shape[0]):
        s = scores_of(head_of(k_ref, i), stacked(q_ref, i)) + seen(place_ref, distance)
        old = top_ref[i]
        top = jnp.maximum(old, jnp.max(s, axis=0, keepdims=True))
        p = jnp.exp2(s - top)
        keep = jnp.exp2(old - top)
        inverse = 1.0 / (total_ref[i] * keep + jnp.sum(p, axis=0, keepdims=True))
        w_out[i] = (p * inverse).astype(jnp.bfloat16)
        o_out[i] = o_ref[i] * (keep * inverse)


def put_product(att, w_ref, columns, out_refs):
    product = jnp.dot(att, w_ref[:, columns[0] : columns[1]], preferred_element_type=jnp.float32)
    part = out_refs[0].shape[0]
    for i, out_ref in enumerate(out_refs):
        out_ref[...] = product[i * part : (i + 1) * part].astype(jnp.bfloat16)


def last_values_kernel(columns, w_ref, o_ref, v_ref, weight_ref, att_ref, *out_refs):
    for i in range(o_ref.shape[0]):
        put_heads(att_ref, i, o_ref[i] + weigh(head_of(v_ref, i), w_ref[i]))
    far = len(out_refs) * out_refs[0].shape[0]
    put_product(att_ref[0:far, :], weight_ref, columns, out_refs)


def project_kernel(first, columns, att_ref, weight_ref, *out_refs):
    count = len(out_refs) * out_refs[0].shape[0]
    put_product(att_ref[first : first + count, :], weight_ref, columns, out_refs)


def finish_kernel(columns, first, mine_ref, got_ref, *refs):
    far_refs, (out_ref, staged, sem) = refs[: len(refs) - 3], refs[len(refs) - 3 :]
    if not first:
        far_refs = far_refs[:-1]
    total = mine_ref[:, columns[0] : columns[1]].astype(jnp.float32)
    total = total + got_ref[:, columns[0] : columns[1]].astype(jnp.float32)
    for far_ref in far_refs:
        total = total + far_ref[...].astype(jnp.float32)
    staged[...] = total.astype(jnp.bfloat16)
    target = out_ref.at[0 : staged.shape[0], columns[0] : columns[1]]
    copy = pltpu.make_async_copy(staged, target, sem)
    copy.start()
    copy.wait()


def place_moved_kernel(place_ref, own_ref, back_ref, _, out_ref, sem):
    target = out_ref.at[out_ref.shape[0] - own_ref.shape[0] : out_ref.shape[0]]

    @pl.when(place_ref[0] == 0)
    def _own():
        copy = pltpu.make_async_copy(own_ref, target, sem)
        copy.start()
        copy.wait()

    @pl.when(place_ref[0] != 0)
    def _back():
        copy = pltpu.make_async_copy(back_ref, target, sem)
        copy.start()
        copy.wait()


def write(kernel, out_shape, scratch, out, *operands, scalars=0):
    operands = [value if i < scalars else in_vmem(value) for i, value in enumerate(operands)]
    specs = [SMEM] * scalars + [VMEM] * (len(operands) - scalars)
    aliases = {}
    if out is not None:
        aliases = {len(operands): 0}
        operands.append(out)
        specs.append(pl.BlockSpec(memory_space=pltpu.HBM))
    return pl.pallas_call(
        kernel,
        in_specs=specs,
        out_specs=pl.BlockSpec(memory_space=pltpu.HBM),
        out_shape=jax.ShapeDtypeStruct(out_shape, jnp.bfloat16),
        scratch_shapes=scratch + [pltpu.SemaphoreType.DMA],
        input_output_aliases=aliases,
        compiler_params=pltpu.CompilerParams(vmem_limit_bytes=8 << 20),
    )(*operands)


def ring(value, axis, distance):
    count = lax.axis_size(axis)
    return lax.ppermute(value, axis, [(s, (s + distance) % count) for s in range(count)])


def pass_on(value, distance):
    count = lax.axis_size("seq")
    return lax.ppermute(value, "seq", [(s, s + distance) for s in range(distance, count - distance)])


def swap(value):
    count = lax.axis_size("head")
    return lax.ppermute(value, "head", [(h, h ^ 1) for h in range(count)])


def tile_of(width):
    return max(t for t in range(128, 1024, 128) if width % t == 0 and (t % 256 == 0 or width % 256))


def on_device(queries, keys, values, out_weight):
    rows, depth = queries.shape
    width = out_weight.shape[1]
    heads = lax.axis_size("head")
    seq_count = lax.axis_size("seq")
    place = lax.axis_index("seq").astype(jnp.int32)[None]
    me = lax.axis_index("head")
    chips = heads // CORES
    part = rows // heads
    kv_local = keys.shape[1] // HEAD_SIZE
    reaches = [1 << level for level in range(seq_count.bit_length() - 1)]
    f32, bf16 = jnp.float32, jnp.bfloat16

    moved = part // 3 if reaches == [1, 2] and part % 48 == 0 else 0
    kept = part - moved
    parts = 2 * chips

    k_now, v_now = ring(keys, "seq", 1), ring(values, "seq", 1)

    chip, core = me // CORES, me % CORES
    owners = []
    for step in range(1, chips + 1):
        base = ((chip + step) % chips) * CORES
        owners += [base + 1 - core, base + core]

    def rows_from(first, count):
        starts = [owner * part + first for owner in owners]
        q = jnp.concatenate([lax.dynamic_slice_in_dim(queries, start, count, 0) for start in starts], axis=0)
        pos = jnp.concatenate([start + jnp.arange(count, dtype=jnp.int32) for start in starts])
        return jnp.concatenate([pos] * GROUP)[None], in_vmem(q)

    sets = [rows_from(0, kept)]
    lanes = GROUP * kept * parts
    line, block = (kv_local, 1, lanes), (kv_local, HEAD_SIZE, lanes)
    state = [(line, f32), (line, f32), (block, f32)]
    back_pairs = [(s, s - 1) for s in range(1, seq_count)]
    extra = []
    if moved:
        sets.append(rows_from(kept, moved))
        q_moved = lax.ppermute(sets[1][1], "seq", back_pairs)
        extra = [((kv_local, PACKED, GROUP * moved * parts), bf16), ((moved * parts, depth), bf16)]
    q = sets[0][1]
    outs = call(
        functools.partial(local_kernel, len(sets)),
        state + extra,
        place,
        keys,
        values,
        *[value for pair in sets for value in pair],
        scalars=1,
        load=out_weight,
    )
    carried, weight = outs[:3], outs[-1]
    if moved:
        pack_moved = lax.ppermute(outs[3], "seq", back_pairs)
        pair_outs = [((moved * chips, width), bf16)] * 2
        own_parts = call(functools.partial(own_kernel, chips), pair_outs, place, outs[4], weight, scalars=1)

    def settle(theirs, mine, everywhere):
        axes = "head" if everywhere else ("seq", "head")
        got = lax.ppermute(theirs, axes, [(h, h ^ 1) for h in range(heads)])
        both = mine.astype(f32) + got.astype(f32)
        total = both[(chips - 1) * moved :]
        for step in range(1, chips):
            piece = both[(step - 1) * moved : step * moved].astype(bf16)
            moves = [(h, (h + step * CORES) % heads) for h in range(heads)]
            total = total + lax.ppermute(piece, axes, moves).astype(f32)
        return total.astype(bf16)

    if moved:
        own_rows = settle(*own_parts, False)

    tile = tile_of(width)
    tiles = width // tile
    back = None
    for distance in reaches[:-1]:
        k_here, v_here = k_now, v_now
        k_now = pass_on(k_here, distance)
        v_now = pass_on(v_here, distance)
        if moved:
            border = tile * (tiles // 2)
            halves = [(0, border), (border, width)]

            def pair_shapes(columns):
                return [((moved * chips, columns[1] - columns[0]), bf16)] * 2

            att_moved, *early_parts = call(
                functools.partial(early_kernel, chips, reaches, halves[0]),
                [((moved * parts, depth), bf16)] + pair_shapes(halves[0]),
                place,
                q_moved,
                keys,
                k_here,
                values,
                v_here,
                pack_moved,
                weight,
                scalars=1,
            )
            late_parts = call(
                functools.partial(pairs_kernel, chips, halves[1]), pair_shapes(halves[1]), att_moved, weight
            )
            done = [settle(*early_parts, True), settle(*late_parts, True)]
            back = lax.ppermute(jnp.concatenate(done, axis=1), "seq", [(s, s + 1) for s in range(seq_count - 1)])
        carried = call(functools.partial(middle_kernel, distance), state, place, q, k_here, v_here, *carried, scalars=1)
    weights, scaled = call(
        functools.partial(last_scores_kernel, reaches[-1]),
        [((kv_local, rows, lanes), bf16), (block, f32)],
        place,
        q,
        k_now,
        *carried,
        scalars=1,
    )

    bounds = [0] + [tile * t for t in range(1, tiles, 2)] + [tile * (tiles - 1), width]
    bounds = sorted(set(bounds))
    chunks = list(zip(bounds[:-1], bounds[1:]))
    far_parts = parts - 2

    def parts_of(count, columns):
        return [((kept, columns[1] - columns[0]), bf16)] * count

    att, *first_far = call(
        functools.partial(last_values_kernel, chunks[0]),
        [((kept * parts, depth), bf16)] + parts_of(far_parts, chunks[0]),
        weights,
        scaled,
        v_now,
        weight,
    )
    arrived = []
    for index, columns in enumerate(chunks):
        far = first_far
        if index:
            kernel = functools.partial(project_kernel, 0, columns)
            far = call(kernel, parts_of(far_parts, columns), att, weight)
        here = []
        for step in range(1, chips):
            theirs, mine = far[2 * step - 2], far[2 * step - 1]
            got = swap(theirs)
            both = (mine.astype(f32) + got.astype(f32)).astype(bf16)
            here.append(ring(both, "head", step * CORES))
        arrived.append(here)
    whole = (0, width)
    theirs, mine = call(functools.partial(project_kernel, far_parts * kept, whole), parts_of(2, whole), att, weight)
    got = swap(theirs)
    out = None
    for index, (columns, here) in enumerate(zip(chunks, arrived)):
        if moved and index == max(1, len(chunks) - 2):
            out = write(place_moved_kernel, (part, width), [], out, place, own_rows, back, scalars=1)
        out = write(
            functools.partial(finish_kernel, columns, out is None),
            (part, width),
            [pltpu.VMEM((kept, columns[1] - columns[0]), bf16)],
            out,
            mine,
            got,
            *here,
        )
    return out


def solution(mesh):
    in_specs = (
        P(("grp", "seq"), "head"),
        P(("grp", "seq"), "head"),
        P(("grp", "seq"), "head"),
        P("head", None),
    )
    out_specs = P(("grp", "seq", "head"), None)

    return jax.shard_map(on_device, mesh=mesh, in_specs=in_specs, out_specs=out_specs, check_vma=False)
```

```python
import functools
import math

import jax
import jax.numpy as jnp
from jax import lax
from jax.experimental import pallas as pl
from jax.experimental.pallas import tpu as pltpu
from jax.sharding import PartitionSpec as P

QUERY_HEADS = 32
KEY_VALUE_HEADS = 16
HEAD_SIZE = 128
GROUP = QUERY_HEADS // KEY_VALUE_HEADS
CORES = 2

SCALE2 = 168.0**-0.5 * math.log2(math.e)


VMEM = pl.BlockSpec(memory_space=pltpu.VMEM)
SMEM = pl.BlockSpec(memory_space=pltpu.SMEM)


def in_vmem(value):
    return pltpu.with_memory_space_constraint(value, pltpu.VMEM)


def loading(kernel, *refs):
    source, (out_ref, sems), refs = refs[0], refs[-2:], refs[1:-2]
    count = sems.shape[0]
    rows = source.shape[0] // count
    copies = []
    for i in range(count):
        block = pl.ds(i * rows, rows)
        copies.append(pltpu.make_async_copy(source.at[block], out_ref.at[block], sems.at[i]))
        copies[-1].start()

    @pl.when(refs[0][0] >= 0)
    def _compute():
        kernel(*refs)

    for copy in copies:
        copy.wait()


def call(kernel, outs, *operands, scalars=0, load=None, scratch=()):
    operands = [value if i < scalars else in_vmem(value) for i, value in enumerate(operands)]
    specs = [SMEM] * scalars + [VMEM] * (len(operands) - scalars)
    outs = [pltpu.VMEM(shape, dtype) for shape, dtype in outs]
    scratch = list(scratch)
    if load is not None:
        kernel = functools.partial(loading, kernel)
        operands = [pltpu.with_memory_space_constraint(load, pltpu.HBM)] + operands
        specs = [pl.BlockSpec(memory_space=pltpu.HBM)] + specs
        outs.append(pltpu.VMEM(load.shape, load.dtype))
        scratch = [pltpu.SemaphoreType.DMA((4,))]
    return pl.pallas_call(
        kernel,
        in_specs=specs,
        out_specs=[VMEM] * len(outs),
        out_shape=outs,
        scratch_shapes=scratch,
        compiler_params=pltpu.CompilerParams(vmem_limit_bytes=20 << 20),
    )(*operands)


def stacked(q_ref, i):
    first = i * GROUP
    return jnp.concatenate(
        [q_ref[:, (first + g) * HEAD_SIZE : (first + g + 1) * HEAD_SIZE] for g in range(GROUP)], axis=0
    )


def head_of(ref, i):
    return ref[:, i * HEAD_SIZE : (i + 1) * HEAD_SIZE]


def scores_of(k, q):
    return lax.dot_general(k, q, (((1,), (1,)), ((), ())), preferred_element_type=jnp.float32) * SCALE2


def weigh(v, p):
    return lax.dot_general(v, p, (((0,), (0,)), ((), ())), preferred_element_type=jnp.float32)


def thirds(value):
    high = value.astype(jnp.bfloat16).astype(jnp.float32)
    middle = (value - high).astype(jnp.bfloat16).astype(jnp.float32)
    return [high, middle, value - high - middle]


LINES = HEAD_SIZE + 16
PACKED = LINES + HEAD_SIZE


def put_heads(att_ref, i, o):
    rows = att_ref.shape[0]
    o = o.T.astype(jnp.bfloat16)
    for g in range(GROUP):
        head = i * GROUP + g
        att_ref[:, head * HEAD_SIZE : (head + 1) * HEAD_SIZE] = o[g * rows : (g + 1) * rows]


def local_part(pos_ref, q_ref, k_ref, v_ref, i):
    s = scores_of(head_of(k_ref, i), stacked(q_ref, i))
    s = jnp.where(pos_ref[...] >= lax.broadcasted_iota(jnp.int32, s.shape, 0), s, -jnp.inf)
    top = jnp.max(s, axis=0, keepdims=True)
    p = jnp.exp2(s - top)
    return top, jnp.sum(p, axis=0, keepdims=True), weigh(head_of(v_ref, i), p.astype(jnp.bfloat16))


def local_kernel(sets, place_ref, k_ref, v_ref, *refs):
    inputs, outputs = refs[: 2 * sets], refs[2 * sets :]
    top_ref, total_ref, o_ref = outputs[:3]
    for i in range(o_ref.shape[0]):
        top_ref[i], total_ref[i], o_ref[i] = local_part(*inputs[:2], k_ref, v_ref, i)
        if sets == 2:
            pack_ref, att_ref = outputs[3:]
            top, total, o = local_part(*inputs[2:], k_ref, v_ref, i)
            pack_ref[i, 0:HEAD_SIZE] = o.astype(jnp.bfloat16)
            lines = thirds(top) + thirds(total)
            lines.append(jnp.zeros((LINES - HEAD_SIZE - len(lines), top.shape[1]), jnp.float32))
            pack_ref[i, HEAD_SIZE:LINES] = jnp.concatenate(lines, axis=0).astype(jnp.bfloat16)
            pack_ref[i, LINES:PACKED] = stacked(inputs[3], i).astype(jnp.float32).T.astype(jnp.bfloat16)
            put_heads(att_ref, i, o * (1.0 / total))


def early_kernel(chips, distances, place_ref, *refs):
    count = len(distances)
    k_refs, v_refs = refs[:count], refs[count : 2 * count]
    pack_ref, weight_ref, theirs_ref, mine_ref, att_ref = refs[2 * count :]
    for i in range(pack_ref.shape[0]):
        q = pack_ref[i, LINES:PACKED]
        extra = pack_ref[i, HEAD_SIZE:LINES].astype(jnp.float32)
        top = extra[0:1] + extra[1:2] + extra[2:3]
        total = extra[3:4] + extra[4:5] + extra[5:6]
        parts = [
            jnp.dot(head_of(k_ref, i), q, preferred_element_type=jnp.float32) * SCALE2
            + jnp.where(place_ref[0] + 1 >= distance, 0.0, -jnp.inf)
            for distance, k_ref in zip(distances, k_refs)
        ]
        new_top = functools.reduce(jnp.maximum, [top] + [jnp.max(s, axis=0, keepdims=True) for s in parts])
        keep = jnp.exp2(top - new_top)
        total = total * keep
        o = pack_ref[i, 0:HEAD_SIZE].astype(jnp.float32) * keep
        for s, v_ref in zip(parts, v_refs):
            p = jnp.exp2(s - new_top)
            total = total + jnp.sum(p, axis=0, keepdims=True)
            o = o + weigh(head_of(v_ref, i), p.astype(jnp.bfloat16))
        put_heads(att_ref, i, o * (1.0 / total))
    put_pairs(chips, att_ref[...], weight_ref, theirs_ref, mine_ref)


def put_pairs(chips, att, weight_ref, theirs_ref, mine_ref):
    product = jnp.dot(att, weight_ref[...], preferred_element_type=jnp.float32)
    product = product.astype(jnp.bfloat16)
    part = att.shape[0] // (2 * chips)
    for chip in range(chips):
        block = slice(chip * part, (chip + 1) * part)
        theirs_ref[block, :] = product[2 * chip * part : (2 * chip + 1) * part]
        mine_ref[block, :] = product[(2 * chip + 1) * part : (2 * chip + 2) * part]


def own_kernel(chips, place_ref, att_ref, weight_ref, theirs_ref, mine_ref):
    @pl.when(place_ref[0] == 0)
    def _():
        put_pairs(chips, att_ref[...], weight_ref, theirs_ref, mine_ref)


def seen(place_ref, distance):
    return jnp.where(place_ref[0] >= distance, 0.0, -jnp.inf).astype(jnp.float32)


def middle_kernel(distance, place_ref, q_ref, k_ref, v_ref, top_ref, total_ref, o_ref, top_out, total_out, o_out):
    for i in range(o_ref.shape[0]):
        s = scores_of(head_of(k_ref, i), stacked(q_ref, i)) + seen(place_ref, distance)
        old = top_ref[i]
        top = jnp.maximum(old, jnp.max(s, axis=0, keepdims=True))
        p = jnp.exp2(s - top)
        keep = jnp.exp2(old - top)
        top_out[i] = top
        total_out[i] = total_ref[i] * keep + jnp.sum(p, axis=0, keepdims=True)
        o_out[i] = o_ref[i] * keep + weigh(head_of(v_ref, i), p.astype(jnp.bfloat16))


def last_scores_kernel(distance, place_ref, q_ref, k_ref, top_ref, total_ref, o_ref, w_out, o_out):
    for i in range(o_ref.shape[0]):
        s = scores_of(head_of(k_ref, i), stacked(q_ref, i)) + seen(place_ref, distance)
        old = top_ref[i]
        top = jnp.maximum(old, jnp.max(s, axis=0, keepdims=True))
        p = jnp.exp2(s - top)
        keep = jnp.exp2(old - top)
        inverse = 1.0 / (total_ref[i] * keep + jnp.sum(p, axis=0, keepdims=True))
        w_out[i] = (p * inverse).astype(jnp.bfloat16)
        o_out[i] = o_ref[i] * (keep * inverse)


def put_product(att, w_ref, columns, out_refs):
    product = jnp.dot(att, w_ref[:, columns[0] : columns[1]], preferred_element_type=jnp.float32)
    part = out_refs[0].shape[0]
    for i, out_ref in enumerate(out_refs):
        out_ref[...] = product[i * part : (i + 1) * part].astype(jnp.bfloat16)


def last_values_kernel(columns, w_ref, o_ref, v_ref, weight_ref, att_ref, *out_refs):
    for i in range(o_ref.shape[0]):
        put_heads(att_ref, i, o_ref[i] + weigh(head_of(v_ref, i), w_ref[i]))
    far = len(out_refs) * out_refs[0].shape[0]
    put_product(att_ref[0:far, :], weight_ref, columns, out_refs)


def project_kernel(first, columns, att_ref, weight_ref, *out_refs):
    count = len(out_refs) * out_refs[0].shape[0]
    put_product(att_ref[first : first + count, :], weight_ref, columns, out_refs)


def finish_kernel(ranges, steps, first, place_ref, mine_ref, got_ref, *refs):
    far_refs, refs = refs[: len(ranges) * steps], list(refs[len(ranges) * steps :])
    sem, staged = refs.pop(), [refs.pop() for _ in ranges][::-1]
    out_ref = refs.pop()
    if not first:
        refs.pop()
    target = None
    if refs:
        own_ref, back_ref = refs
        target = out_ref.at[out_ref.shape[0] - own_ref.shape[0] : out_ref.shape[0]]

        @pl.when(place_ref[0] == 0)
        def _own():
            pltpu.make_async_copy(own_ref, target, sem.at[len(ranges)]).start()

        @pl.when(place_ref[0] != 0)
        def _back():
            pltpu.make_async_copy(back_ref, target, sem.at[len(ranges)]).start()

    copies = []
    for index, columns in enumerate(ranges):
        span = slice(columns[0], columns[1])
        total = mine_ref[:, span].astype(jnp.float32) + got_ref[:, span].astype(jnp.float32)
        for far_ref in far_refs[index * steps : (index + 1) * steps]:
            total = total + far_ref[...].astype(jnp.float32)
        staged[index][...] = total.astype(jnp.bfloat16)
        copies.append(
            pltpu.make_async_copy(staged[index], out_ref.at[0 : mine_ref.shape[0], span], sem.at[index])
        )
        copies[-1].start()
    for copy in copies:
        copy.wait()
    if target is not None:
        pltpu.make_async_copy(back_ref, target, sem.at[len(ranges)]).wait()


def write(kernel, out_shape, scratch, out, *operands, scalars=0):
    operands = [value if i < scalars else in_vmem(value) for i, value in enumerate(operands)]
    specs = [SMEM] * scalars + [VMEM] * (len(operands) - scalars)
    aliases = {}
    if out is not None:
        aliases = {len(operands): 0}
        operands.append(out)
        specs.append(pl.BlockSpec(memory_space=pltpu.HBM))
    return pl.pallas_call(
        kernel,
        in_specs=specs,
        out_specs=pl.BlockSpec(memory_space=pltpu.HBM),
        out_shape=jax.ShapeDtypeStruct(out_shape, jnp.bfloat16),
        scratch_shapes=scratch,
        input_output_aliases=aliases,
        compiler_params=pltpu.CompilerParams(vmem_limit_bytes=8 << 20),
    )(*operands)


def ring(value, axis, distance):
    count = lax.axis_size(axis)
    return lax.ppermute(value, axis, [(s, (s + distance) % count) for s in range(count)])


def pass_on(value, distance):
    count = lax.axis_size("seq")
    return lax.ppermute(value, "seq", [(s, s + distance) for s in range(distance, count - distance)])


def swap(value):
    count = lax.axis_size("head")
    return lax.ppermute(value, "head", [(h, h ^ 1) for h in range(count)])


def tile_of(width):
    return max(t for t in range(128, 1024, 128) if width % t == 0 and (t % 256 == 0 or width % 256))


def on_device(queries, keys, values, out_weight):
    rows, depth = queries.shape
    width = out_weight.shape[1]
    heads = lax.axis_size("head")
    seq_count = lax.axis_size("seq")
    place = lax.axis_index("seq").astype(jnp.int32)[None]
    me = lax.axis_index("head")
    chips = heads // CORES
    part = rows // heads
    kv_local = keys.shape[1] // HEAD_SIZE
    reaches = [1 << level for level in range(seq_count.bit_length() - 1)]
    f32, bf16 = jnp.float32, jnp.bfloat16

    moved = part // 3 if reaches == [1, 2] and part % 48 == 0 else 0
    kept = part - moved
    parts = 2 * chips

    onward = [(s, s + 1) for s in range(seq_count - 1)]
    k_now, v_now = ring(keys, "seq", 1), lax.ppermute(values, "seq", onward)

    chip, core = me // CORES, me % CORES
    owners = []
    for step in range(1, chips + 1):
        base = ((chip + step) % chips) * CORES
        owners += [base + 1 - core, base + core]

    def rows_from(first, count):
        starts = [owner * part + first for owner in owners]
        q = jnp.concatenate([lax.dynamic_slice_in_dim(queries, start, count, 0) for start in starts], axis=0)
        pos = jnp.concatenate([start + jnp.arange(count, dtype=jnp.int32) for start in starts])
        return jnp.concatenate([pos] * GROUP)[None], in_vmem(q)

    sets = [rows_from(0, kept)]
    lanes = GROUP * kept * parts
    line, block = (kv_local, 1, lanes), (kv_local, HEAD_SIZE, lanes)
    state = [(line, f32), (line, f32), (block, f32)]
    extra = []
    if moved:
        sets.append(rows_from(kept, moved))
        extra = [((kv_local, PACKED, GROUP * moved * parts), bf16), ((moved * parts, depth), bf16)]
    q = sets[0][1]
    outs = call(
        functools.partial(local_kernel, len(sets)),
        state + extra,
        place,
        keys,
        values,
        *[value for pair in sets for value in pair],
        scalars=1,
        load=out_weight,
    )
    carried, weight = outs[:3], outs[-1]
    if moved:
        pack = lax.ppermute(outs[3], "seq", [(s, s - 1) for s in range(1, seq_count)])
        pair_outs = [((moved * chips, width), bf16)] * 2
        own_parts = call(functools.partial(own_kernel, chips), pair_outs, place, outs[4], weight, scalars=1)

    def settle(theirs, mine, everywhere):
        axes = "head" if everywhere else ("seq", "head")
        got = lax.ppermute(theirs, axes, [(h, h ^ 1) for h in range(heads)])
        both = mine.astype(f32) + got.astype(f32)
        total = both[(chips - 1) * moved :]
        for step in range(1, chips):
            piece = both[(step - 1) * moved : step * moved].astype(bf16)
            moves = [(h, (h + step * CORES) % heads) for h in range(heads)]
            total = total + lax.ppermute(piece, axes, moves).astype(f32)
        return total.astype(bf16)

    if moved:
        own_rows = settle(*own_parts, False)

    tile = tile_of(width)
    tiles = width // tile
    back = None
    for distance in reaches[:-1]:
        k_here, v_here = k_now, v_now
        k_now = pass_on(k_here, distance)
        v_now = pass_on(v_here, distance)
        if moved:
            early_parts = call(
                functools.partial(early_kernel, chips, reaches),
                pair_outs,
                place,
                keys,
                k_here,
                values,
                v_here,
                pack,
                weight,
                scalars=1,
                scratch=[pltpu.VMEM((moved * parts, depth), bf16)],
            )
            back = lax.ppermute(settle(*early_parts, True), "seq", onward)
        carried = call(functools.partial(middle_kernel, distance), state, place, q, k_here, v_here, *carried, scalars=1)
    weights, scaled = call(
        functools.partial(last_scores_kernel, reaches[-1]),
        [((kv_local, rows, lanes), bf16), (block, f32)],
        place,
        q,
        k_now,
        *carried,
        scalars=1,
    )

    bounds = sorted({0, tile, tile * ((tiles + 1) // 2), width})
    chunks = list(zip(bounds[:-1], bounds[1:]))
    far_parts = parts - 2

    def parts_of(count, columns):
        return [((kept, columns[1] - columns[0]), bf16)] * count

    att, *first_far = call(
        functools.partial(last_values_kernel, chunks[0]),
        [((kept * parts, depth), bf16)] + parts_of(far_parts, chunks[0]),
        weights,
        scaled,
        v_now,
        weight,
    )
    arrived = []
    for index, columns in enumerate(chunks):
        far = first_far
        if index:
            kernel = functools.partial(project_kernel, 0, columns)
            far = call(kernel, parts_of(far_parts, columns), att, weight)
        here = []
        for step in range(1, chips):
            theirs, mine = far[2 * step - 2], far[2 * step - 1]
            got = swap(theirs)
            both = (mine.astype(f32) + got.astype(f32)).astype(bf16)
            here.append(ring(both, "head", step * CORES))
        arrived.append(here)
    whole = (0, width)
    theirs, mine = call(functools.partial(project_kernel, far_parts * kept, whole), parts_of(2, whole), att, weight)
    got = swap(theirs)
    out = None
    for group in (range(len(chunks) - 1), range(len(chunks) - 1, len(chunks))):
        ranges = [chunks[i] for i in group]
        last = group.stop == len(chunks)
        out = write(
            functools.partial(finish_kernel, ranges, chips - 1, out is None),
            (part, width),
            [pltpu.VMEM((kept, c[1] - c[0]), bf16) for c in ranges] + [pltpu.SemaphoreType.DMA((len(ranges) + 1,))],
            out,
            place,
            mine,
            got,
            *[value for i in group for value in arrived[i]],
            *([own_rows, back] if moved and last else []),
            scalars=1,
        )
    return out


def solution(mesh):
    in_specs = (
        P(("grp", "seq"), "head"),
        P(("grp", "seq"), "head"),
        P(("grp", "seq"), "head"),
        P("head", None),
    )
    out_specs = P(("grp", "seq", "head"), None)

    return jax.shard_map(on_device, mesh=mesh, in_specs=in_specs, out_specs=out_specs, check_vma=False)
```

```python
import functools
import math

import jax
import jax.numpy as jnp
from jax import lax
from jax.experimental import pallas as pl
from jax.experimental.pallas import tpu as pltpu
from jax.sharding import PartitionSpec as P

QUERY_HEADS = 32
KEY_VALUE_HEADS = 16
HEAD_SIZE = 128
GROUP = QUERY_HEADS // KEY_VALUE_HEADS
CORES = 2

SCALE2 = 168.0**-0.5 * math.log2(math.e)


VMEM = pl.BlockSpec(memory_space=pltpu.VMEM)
SMEM = pl.BlockSpec(memory_space=pltpu.SMEM)


def in_vmem(value):
    return pltpu.with_memory_space_constraint(value, pltpu.VMEM)


def loading(kernel, *refs):
    source, (out_ref, sems), refs = refs[0], refs[-2:], refs[1:-2]
    count = sems.shape[0]
    rows = source.shape[0] // count
    copies = []
    for i in range(count):
        block = pl.ds(i * rows, rows)
        copies.append(pltpu.make_async_copy(source.at[block], out_ref.at[block], sems.at[i]))
        copies[-1].start()

    @pl.when(refs[0][0] >= 0)
    def _compute():
        kernel(*refs)

    for copy in copies:
        copy.wait()


def call(kernel, outs, *operands, scalars=0, load=None, scratch=()):
    operands = [value if i < scalars else in_vmem(value) for i, value in enumerate(operands)]
    specs = [SMEM] * scalars + [VMEM] * (len(operands) - scalars)
    outs = [pltpu.VMEM(shape, dtype) for shape, dtype in outs]
    scratch = list(scratch)
    if load is not None:
        kernel = functools.partial(loading, kernel)
        operands = [pltpu.with_memory_space_constraint(load, pltpu.HBM)] + operands
        specs = [pl.BlockSpec(memory_space=pltpu.HBM)] + specs
        outs.append(pltpu.VMEM(load.shape, load.dtype))
        scratch = [pltpu.SemaphoreType.DMA((4,))]
    return pl.pallas_call(
        kernel,
        in_specs=specs,
        out_specs=[VMEM] * len(outs),
        out_shape=outs,
        scratch_shapes=scratch,
        compiler_params=pltpu.CompilerParams(vmem_limit_bytes=20 << 20),
    )(*operands)


def stacked(q_ref, i):
    first = i * GROUP
    return jnp.concatenate(
        [q_ref[:, (first + g) * HEAD_SIZE : (first + g + 1) * HEAD_SIZE] for g in range(GROUP)], axis=0
    )


def head_of(ref, i):
    return ref[:, i * HEAD_SIZE : (i + 1) * HEAD_SIZE]


def scores_of(k, q):
    return lax.dot_general(k, q, (((1,), (1,)), ((), ())), preferred_element_type=jnp.float32) * SCALE2


def weigh(v, p):
    return lax.dot_general(v, p, (((0,), (0,)), ((), ())), preferred_element_type=jnp.float32)


def thirds(value):
    high = value.astype(jnp.bfloat16).astype(jnp.float32)
    middle = (value - high).astype(jnp.bfloat16).astype(jnp.float32)
    return [high, middle, value - high - middle]


LINES = HEAD_SIZE + 16
PACKED = LINES + HEAD_SIZE


def put_heads(att_ref, i, o):
    rows = att_ref.shape[0]
    o = o.T.astype(jnp.bfloat16)
    for g in range(GROUP):
        head = i * GROUP + g
        att_ref[:, head * HEAD_SIZE : (head + 1) * HEAD_SIZE] = o[g * rows : (g + 1) * rows]


def local_part(pos_ref, q_ref, k_ref, v_ref, i):
    s = scores_of(head_of(k_ref, i), stacked(q_ref, i))
    s = jnp.where(pos_ref[...] >= lax.broadcasted_iota(jnp.int32, s.shape, 0), s, -jnp.inf)
    top = jnp.max(s, axis=0, keepdims=True)
    p = jnp.exp2(s - top)
    return top, jnp.sum(p, axis=0, keepdims=True), weigh(head_of(v_ref, i), p.astype(jnp.bfloat16))


def local_kernel(place_ref, k_ref, v_ref, pos_ref, q_ref, top_ref, total_ref, o_ref):
    for i in range(o_ref.shape[0]):
        top_ref[i], total_ref[i], o_ref[i] = local_part(pos_ref, q_ref, k_ref, v_ref, i)


def moving_kernel(k_ref, v_ref, pos_ref, q_ref, pack_ref, att_ref):
    for i in range(pack_ref.shape[0]):
        top, total, o = local_part(pos_ref, q_ref, k_ref, v_ref, i)
        pack_ref[i, 0:HEAD_SIZE] = o.astype(jnp.bfloat16)
        lines = thirds(top) + thirds(total)
        lines.append(jnp.zeros((LINES - HEAD_SIZE - len(lines), top.shape[1]), jnp.float32))
        pack_ref[i, HEAD_SIZE:LINES] = jnp.concatenate(lines, axis=0).astype(jnp.bfloat16)
        pack_ref[i, LINES:PACKED] = stacked(q_ref, i).astype(jnp.float32).T.astype(jnp.bfloat16)
        put_heads(att_ref, i, o * (1.0 / total))


def early_kernel(chips, distances, place_ref, *refs):
    count = len(distances)
    k_refs, v_refs = refs[:count], refs[count : 2 * count]
    pack_ref, weight_ref, theirs_ref, mine_ref, att_ref = refs[2 * count :]
    for i in range(pack_ref.shape[0]):
        q = pack_ref[i, LINES:PACKED]
        extra = pack_ref[i, HEAD_SIZE:LINES].astype(jnp.float32)
        top = extra[0:1] + extra[1:2] + extra[2:3]
        total = extra[3:4] + extra[4:5] + extra[5:6]
        parts = [
            jnp.dot(head_of(k_ref, i), q, preferred_element_type=jnp.float32) * SCALE2
            + jnp.where(place_ref[0] + 1 >= distance, 0.0, -jnp.inf)
            for distance, k_ref in zip(distances, k_refs)
        ]
        new_top = functools.reduce(jnp.maximum, [top] + [jnp.max(s, axis=0, keepdims=True) for s in parts])
        keep = jnp.exp2(top - new_top)
        total = total * keep
        o = pack_ref[i, 0:HEAD_SIZE].astype(jnp.float32) * keep
        for s, v_ref in zip(parts, v_refs):
            p = jnp.exp2(s - new_top)
            total = total + jnp.sum(p, axis=0, keepdims=True)
            o = o + weigh(head_of(v_ref, i), p.astype(jnp.bfloat16))
        put_heads(att_ref, i, o * (1.0 / total))
    put_pairs(chips, att_ref[...], weight_ref, theirs_ref, mine_ref)


def put_pairs(chips, att, weight_ref, theirs_ref, mine_ref):
    product = jnp.dot(att, weight_ref[...], preferred_element_type=jnp.float32)
    product = product.astype(jnp.bfloat16)
    part = att.shape[0] // (2 * chips)
    for chip in range(chips):
        block = slice(chip * part, (chip + 1) * part)
        theirs_ref[block, :] = product[2 * chip * part : (2 * chip + 1) * part]
        mine_ref[block, :] = product[(2 * chip + 1) * part : (2 * chip + 2) * part]


def own_kernel(chips, place_ref, att_ref, weight_ref, theirs_ref, mine_ref):
    @pl.when(place_ref[0] == 0)
    def _():
        put_pairs(chips, att_ref[...], weight_ref, theirs_ref, mine_ref)


def seen(place_ref, distance):
    return jnp.where(place_ref[0] >= distance, 0.0, -jnp.inf).astype(jnp.float32)


def middle_kernel(distance, place_ref, q_ref, k_ref, v_ref, top_ref, total_ref, o_ref, top_out, total_out, o_out):
    for i in range(o_ref.shape[0]):
        s = scores_of(head_of(k_ref, i), stacked(q_ref, i)) + seen(place_ref, distance)
        old = top_ref[i]
        top = jnp.maximum(old, jnp.max(s, axis=0, keepdims=True))
        p = jnp.exp2(s - top)
        keep = jnp.exp2(old - top)
        top_out[i] = top
        total_out[i] = total_ref[i] * keep + jnp.sum(p, axis=0, keepdims=True)
        o_out[i] = o_ref[i] * keep + weigh(head_of(v_ref, i), p.astype(jnp.bfloat16))


def last_scores_kernel(distance, place_ref, q_ref, k_ref, top_ref, total_ref, o_ref, w_out, o_out):
    for i in range(o_ref.shape[0]):
        s = scores_of(head_of(k_ref, i), stacked(q_ref, i)) + seen(place_ref, distance)
        old = top_ref[i]
        top = jnp.maximum(old, jnp.max(s, axis=0, keepdims=True))
        p = jnp.exp2(s - top)
        keep = jnp.exp2(old - top)
        inverse = 1.0 / (total_ref[i] * keep + jnp.sum(p, axis=0, keepdims=True))
        w_out[i] = (p * inverse).astype(jnp.bfloat16)
        o_out[i] = o_ref[i] * (keep * inverse)


def put_product(att, w_ref, columns, out_refs):
    product = jnp.dot(att, w_ref[:, columns[0] : columns[1]], preferred_element_type=jnp.float32)
    part = out_refs[0].shape[0]
    for i, out_ref in enumerate(out_refs):
        out_ref[...] = product[i * part : (i + 1) * part].astype(jnp.bfloat16)


def last_values_kernel(columns, w_ref, o_ref, v_ref, weight_ref, att_ref, *out_refs):
    for i in range(o_ref.shape[0]):
        put_heads(att_ref, i, o_ref[i] + weigh(head_of(v_ref, i), w_ref[i]))
    far = len(out_refs) * out_refs[0].shape[0]
    put_product(att_ref[0:far, :], weight_ref, columns, out_refs)


def project_kernel(first, columns, att_ref, weight_ref, *out_refs):
    count = len(out_refs) * out_refs[0].shape[0]
    put_product(att_ref[first : first + count, :], weight_ref, columns, out_refs)


def finish_kernel(ranges, steps, first, place_ref, mine_ref, got_ref, *refs):
    far_refs, refs = refs[: len(ranges) * steps], list(refs[len(ranges) * steps :])
    sem, staged = refs.pop(), [refs.pop() for _ in ranges][::-1]
    out_ref = refs.pop()
    if not first:
        refs.pop()
    target = None
    if refs:
        own_ref, back_ref = refs
        target = out_ref.at[out_ref.shape[0] - own_ref.shape[0] : out_ref.shape[0]]

        @pl.when(place_ref[0] == 0)
        def _own():
            pltpu.make_async_copy(own_ref, target, sem.at[len(ranges)]).start()

        @pl.when(place_ref[0] != 0)
        def _back():
            pltpu.make_async_copy(back_ref, target, sem.at[len(ranges)]).start()

    copies = []
    for index, columns in enumerate(ranges):
        span = slice(columns[0], columns[1])
        total = mine_ref[:, span].astype(jnp.float32) + got_ref[:, span].astype(jnp.float32)
        for far_ref in far_refs[index * steps : (index + 1) * steps]:
            total = total + far_ref[...].astype(jnp.float32)
        staged[index][...] = total.astype(jnp.bfloat16)
        copies.append(
            pltpu.make_async_copy(staged[index], out_ref.at[0 : mine_ref.shape[0], span], sem.at[index])
        )
        copies[-1].start()
    for copy in copies:
        copy.wait()
    if target is not None:
        pltpu.make_async_copy(back_ref, target, sem.at[len(ranges)]).wait()


def write(kernel, out_shape, scratch, out, *operands, scalars=0):
    operands = [value if i < scalars else in_vmem(value) for i, value in enumerate(operands)]
    specs = [SMEM] * scalars + [VMEM] * (len(operands) - scalars)
    aliases = {}
    if out is not None:
        aliases = {len(operands): 0}
        operands.append(out)
        specs.append(pl.BlockSpec(memory_space=pltpu.HBM))
    return pl.pallas_call(
        kernel,
        in_specs=specs,
        out_specs=pl.BlockSpec(memory_space=pltpu.HBM),
        out_shape=jax.ShapeDtypeStruct(out_shape, jnp.bfloat16),
        scratch_shapes=scratch,
        input_output_aliases=aliases,
        compiler_params=pltpu.CompilerParams(vmem_limit_bytes=8 << 20),
    )(*operands)


def ring(value, axis, distance):
    count = lax.axis_size(axis)
    return lax.ppermute(value, axis, [(s, (s + distance) % count) for s in range(count)])


def pass_on(value, distance):
    count = lax.axis_size("seq")
    return lax.ppermute(value, "seq", [(s, s + distance) for s in range(distance, count - distance)])


def swap(value):
    count = lax.axis_size("head")
    return lax.ppermute(value, "head", [(h, h ^ 1) for h in range(count)])


def tile_of(width):
    return max(t for t in range(128, 1024, 128) if width % t == 0 and (t % 256 == 0 or width % 256))


def on_device(queries, keys, values, out_weight):
    rows, depth = queries.shape
    width = out_weight.shape[1]
    heads = lax.axis_size("head")
    seq_count = lax.axis_size("seq")
    place = lax.axis_index("seq").astype(jnp.int32)[None]
    me = lax.axis_index("head")
    chips = heads // CORES
    part = rows // heads
    kv_local = keys.shape[1] // HEAD_SIZE
    reaches = [1 << level for level in range(seq_count.bit_length() - 1)]
    f32, bf16 = jnp.float32, jnp.bfloat16

    moved = part // 3 if reaches == [1, 2] and part % 48 == 0 else 0
    kept = part - moved
    parts = 2 * chips

    onward = [(s, s + 1) for s in range(seq_count - 1)]
    k_now, v_now = ring(keys, "seq", 1), lax.ppermute(values, "seq", onward)

    chip, core = me // CORES, me % CORES
    owners = []
    for step in range(1, chips + 1):
        base = ((chip + step) % chips) * CORES
        owners += [base + 1 - core, base + core]

    def rows_from(first, count):
        starts = [owner * part + first for owner in owners]
        q = jnp.concatenate([lax.dynamic_slice_in_dim(queries, start, count, 0) for start in starts], axis=0)
        pos = jnp.concatenate([start + jnp.arange(count, dtype=jnp.int32) for start in starts])
        return jnp.concatenate([pos] * GROUP)[None], in_vmem(q)

    if moved:
        pack, att_own = call(
            moving_kernel,
            [((kv_local, PACKED, GROUP * moved * parts), bf16), ((moved * parts, depth), bf16)],
            keys,
            values,
            *rows_from(kept, moved),
        )
        pack = lax.ppermute(pack, "seq", [(s, s - 1) for s in range(1, seq_count)])
    lanes = GROUP * kept * parts
    line, block = (kv_local, 1, lanes), (kv_local, HEAD_SIZE, lanes)
    state = [(line, f32), (line, f32), (block, f32)]
    pos, q = rows_from(0, kept)
    *carried, weight = call(local_kernel, state, place, keys, values, pos, q, scalars=1, load=out_weight)
    if moved:
        pair_outs = [((moved * chips, width), bf16)] * 2
        own_parts = call(functools.partial(own_kernel, chips), pair_outs, place, att_own, weight, scalars=1)

    def settle(theirs, mine, everywhere):
        axes = "head" if everywhere else ("seq", "head")
        got = lax.ppermute(theirs, axes, [(h, h ^ 1) for h in range(heads)])
        both = mine.astype(f32) + got.astype(f32)
        total = both[(chips - 1) * moved :]
        for step in range(1, chips):
            piece = both[(step - 1) * moved : step * moved].astype(bf16)
            moves = [(h, (h + step * CORES) % heads) for h in range(heads)]
            total = total + lax.ppermute(piece, axes, moves).astype(f32)
        return total.astype(bf16)

    if moved:
        own_rows = settle(*own_parts, False)

    tile = tile_of(width)
    tiles = width // tile
    back = None
    for distance in reaches[:-1]:
        k_here, v_here = k_now, v_now
        k_now = pass_on(k_here, distance)
        v_now = pass_on(v_here, distance)
        if moved:
            early_parts = call(
                functools.partial(early_kernel, chips, reaches),
                pair_outs,
                place,
                keys,
                k_here,
                values,
                v_here,
                pack,
                weight,
                scalars=1,
                scratch=[pltpu.VMEM((moved * parts, depth), bf16)],
            )
            back = lax.ppermute(settle(*early_parts, True), "seq", onward)
        carried = call(functools.partial(middle_kernel, distance), state, place, q, k_here, v_here, *carried, scalars=1)
    weights, scaled = call(
        functools.partial(last_scores_kernel, reaches[-1]),
        [((kv_local, rows, lanes), bf16), (block, f32)],
        place,
        q,
        k_now,
        *carried,
        scalars=1,
    )

    bounds = sorted({0, tile, tile * ((tiles + 1) // 2), width})
    chunks = list(zip(bounds[:-1], bounds[1:]))
    far_parts = parts - 2

    def parts_of(count, columns):
        return [((kept, columns[1] - columns[0]), bf16)] * count

    att, *first_far = call(
        functools.partial(last_values_kernel, chunks[0]),
        [((kept * parts, depth), bf16)] + parts_of(far_parts, chunks[0]),
        weights,
        scaled,
        v_now,
        weight,
    )
    arrived = []
    for index, columns in enumerate(chunks):
        far = first_far
        if index:
            kernel = functools.partial(project_kernel, 0, columns)
            far = call(kernel, parts_of(far_parts, columns), att, weight)
        here = []
        for step in range(1, chips):
            theirs, mine = far[2 * step - 2], far[2 * step - 1]
            got = swap(theirs)
            both = (mine.astype(f32) + got.astype(f32)).astype(bf16)
            here.append(ring(both, "head", step * CORES))
        arrived.append(here)
    whole = (0, width)
    theirs, mine = call(functools.partial(project_kernel, far_parts * kept, whole), parts_of(2, whole), att, weight)
    got = swap(theirs)
    out = None
    for group in (range(len(chunks) - 1), range(len(chunks) - 1, len(chunks))):
        ranges = [chunks[i] for i in group]
        last = group.stop == len(chunks)
        out = write(
            functools.partial(finish_kernel, ranges, chips - 1, out is None),
            (part, width),
            [pltpu.VMEM((kept, c[1] - c[0]), bf16) for c in ranges] + [pltpu.SemaphoreType.DMA((len(ranges) + 1,))],
            out,
            place,
            mine,
            got,
            *[value for i in group for value in arrived[i]],
            *([own_rows, back] if moved and last else []),
            scalars=1,
        )
    return out


def solution(mesh):
    in_specs = (
        P(("grp", "seq"), "head"),
        P(("grp", "seq"), "head"),
        P(("grp", "seq"), "head"),
        P("head", None),
    )
    out_specs = P(("grp", "seq", "head"), None)

    return jax.shard_map(on_device, mesh=mesh, in_specs=in_specs, out_specs=out_specs, check_vma=False)
```

```python
import functools
import math

import jax
import jax.numpy as jnp
from jax import lax
from jax.experimental import pallas as pl
from jax.experimental.pallas import tpu as pltpu
from jax.sharding import PartitionSpec as P

QUERY_HEADS = 32
KEY_VALUE_HEADS = 16
HEAD_SIZE = 128
GROUP = QUERY_HEADS // KEY_VALUE_HEADS
CORES = 2

SCALE2 = 168.0**-0.5 * math.log2(math.e)


VMEM = pl.BlockSpec(memory_space=pltpu.VMEM)
SMEM = pl.BlockSpec(memory_space=pltpu.SMEM)


def in_vmem(value):
    return pltpu.with_memory_space_constraint(value, pltpu.VMEM)


def bring(source_ref, first, out_ref, sems):
    pieces = sems.shape[0]
    rows = out_ref.shape[0] // pieces
    copies = []
    for i in range(pieces):
        block = pl.ds(i * rows, rows)
        copies.append(
            pltpu.make_async_copy(source_ref.at[pl.ds(first + i * rows, rows)], out_ref.at[block], sems.at[i])
        )
        copies[-1].start()
    return copies


def loading(kernel, first, source_ref, *refs):
    copies = bring(source_ref, first, *refs[-2:])

    @pl.when(refs[0][0] >= 0)
    def _compute():
        kernel(*refs[:-2])

    for copy in copies:
        copy.wait()


def call(kernel, outs, *operands, scalars=0, load=None):
    operands = [value if i < scalars else in_vmem(value) for i, value in enumerate(operands)]
    specs = [SMEM] * scalars + [VMEM] * (len(operands) - scalars)
    outs = [pltpu.VMEM(shape, dtype) for shape, dtype in outs]
    scratch = []
    if load is not None:
        source, first, count = load
        kernel = functools.partial(kernel, first)
        operands = [pltpu.with_memory_space_constraint(source, pltpu.HBM)] + operands
        specs = [pl.BlockSpec(memory_space=pltpu.HBM)] + specs
        outs.append(pltpu.VMEM((count, source.shape[1]), source.dtype))
        scratch.append(pltpu.SemaphoreType.DMA((4,)))
    return pl.pallas_call(
        kernel,
        in_specs=specs,
        out_specs=[VMEM] * len(outs),
        out_shape=outs,
        scratch_shapes=scratch,
        compiler_params=pltpu.CompilerParams(vmem_limit_bytes=20 << 20),
    )(*operands)


def stacked(q_ref, i):
    first = i * GROUP
    return jnp.concatenate(
        [q_ref[:, (first + g) * HEAD_SIZE : (first + g + 1) * HEAD_SIZE] for g in range(GROUP)], axis=0
    )


def head_of(ref, i):
    return ref[:, i * HEAD_SIZE : (i + 1) * HEAD_SIZE]


def scores_of(k, q):
    return lax.dot_general(k, q, (((1,), (1,)), ((), ())), preferred_element_type=jnp.float32) * SCALE2


def weigh(v, p):
    return lax.dot_general(v, p, (((0,), (0,)), ((), ())), preferred_element_type=jnp.float32)


def thirds(value):
    high = value.astype(jnp.bfloat16).astype(jnp.float32)
    middle = (value - high).astype(jnp.bfloat16).astype(jnp.float32)
    return [high, middle, value - high - middle]


LINES = HEAD_SIZE + 16
PACKED = LINES + HEAD_SIZE


def put_heads(att_ref, i, o):
    rows = att_ref.shape[0]
    o = o.T.astype(jnp.bfloat16)
    for g in range(GROUP):
        head = i * GROUP + g
        att_ref[:, head * HEAD_SIZE : (head + 1) * HEAD_SIZE] = o[g * rows : (g + 1) * rows]


def local_part(pos_ref, q_ref, k_ref, v_ref, i):
    s = scores_of(head_of(k_ref, i), stacked(q_ref, i))
    s = jnp.where(pos_ref[...] >= lax.broadcasted_iota(jnp.int32, s.shape, 0), s, -jnp.inf)
    top = jnp.max(s, axis=0, keepdims=True)
    p = jnp.exp2(s - top)
    return top, jnp.sum(p, axis=0, keepdims=True), weigh(head_of(v_ref, i), p.astype(jnp.bfloat16))


def local_kernel(place_ref, k_ref, v_ref, pos_ref, q_ref, top_ref, total_ref, o_ref):
    for i in range(o_ref.shape[0]):
        top_ref[i], total_ref[i], o_ref[i] = local_part(pos_ref, q_ref, k_ref, v_ref, i)


def moving_kernel(place_ref, k_ref, v_ref, pos_ref, q_ref, pack_ref, att_ref):
    for i in range(pack_ref.shape[0]):
        top, total, o = local_part(pos_ref, q_ref, k_ref, v_ref, i)
        pack_ref[i, 0:HEAD_SIZE] = o.astype(jnp.bfloat16)
        lines = thirds(top) + thirds(total)
        lines.append(jnp.zeros((LINES - HEAD_SIZE - len(lines), top.shape[1]), jnp.float32))
        pack_ref[i, HEAD_SIZE:LINES] = jnp.concatenate(lines, axis=0).astype(jnp.bfloat16)
        pack_ref[i, LINES:PACKED] = stacked(q_ref, i).astype(jnp.float32).T.astype(jnp.bfloat16)
        put_heads(att_ref, i, o * (1.0 / total))


def early_kernel(chips, distances, columns, place_ref, *refs):
    count = len(distances)
    k_refs, v_refs = refs[:count], refs[count : 2 * count]
    pack_ref, *weight_refs, att_ref, theirs_ref, mine_ref = refs[2 * count :]
    for i in range(pack_ref.shape[0]):
        q = pack_ref[i, LINES:PACKED]
        extra = pack_ref[i, HEAD_SIZE:LINES].astype(jnp.float32)
        top = extra[0:1] + extra[1:2] + extra[2:3]
        total = extra[3:4] + extra[4:5] + extra[5:6]
        parts = [
            jnp.dot(head_of(k_ref, i), q, preferred_element_type=jnp.float32) * SCALE2
            + jnp.where(place_ref[0] + 1 >= distance, 0.0, -jnp.inf)
            for distance, k_ref in zip(distances, k_refs)
        ]
        new_top = functools.reduce(jnp.maximum, [top] + [jnp.max(s, axis=0, keepdims=True) for s in parts])
        keep = jnp.exp2(top - new_top)
        total = total * keep
        o = pack_ref[i, 0:HEAD_SIZE].astype(jnp.float32) * keep
        for s, v_ref in zip(parts, v_refs):
            p = jnp.exp2(s - new_top)
            total = total + jnp.sum(p, axis=0, keepdims=True)
            o = o + weigh(head_of(v_ref, i), p.astype(jnp.bfloat16))
        put_heads(att_ref, i, o * (1.0 / total))
    put_pairs(chips, att_ref[...], weight_refs, columns, theirs_ref, mine_ref)


def product_of(att, weight_refs, columns):
    total, first = None, 0
    for weight_ref in weight_refs:
        last = first + weight_ref.shape[0]
        piece = jnp.dot(
            att[:, first:last], weight_ref[:, columns[0] : columns[1]], preferred_element_type=jnp.float32
        )
        total, first = piece if total is None else total + piece, last
    return total


def put_pairs(chips, att, weight_refs, columns, theirs_ref, mine_ref):
    product = product_of(att, weight_refs, columns).astype(jnp.bfloat16)
    part = att.shape[0] // (2 * chips)
    for chip in range(chips):
        block = slice(chip * part, (chip + 1) * part)
        theirs_ref[block, :] = product[2 * chip * part : (2 * chip + 1) * part]
        mine_ref[block, :] = product[(2 * chip + 1) * part : (2 * chip + 2) * part]


def own_kernel(chips, first, source_ref, place_ref, att_ref, top_ref, theirs_ref, mine_ref, rest_ref, sems):
    for copy in bring(source_ref, first, rest_ref, sems):
        copy.wait()

    @pl.when(place_ref[0] == 0)
    def _project():
        put_pairs(chips, att_ref[...], [top_ref, rest_ref], (0, rest_ref.shape[1]), theirs_ref, mine_ref)


def pairs_kernel(chips, columns, att_ref, *refs):
    *weight_refs, theirs_ref, mine_ref = refs
    put_pairs(chips, att_ref[...], weight_refs, columns, theirs_ref, mine_ref)


def seen(place_ref, distance):
    return jnp.where(place_ref[0] >= distance, 0.0, -jnp.inf).astype(jnp.float32)


def middle_kernel(distance, place_ref, q_ref, k_ref, v_ref, top_ref, total_ref, o_ref, top_out, total_out, o_out):
    for i in range(o_ref.shape[0]):
        s = scores_of(head_of(k_ref, i), stacked(q_ref, i)) + seen(place_ref, distance)
        old = top_ref[i]
        top = jnp.maximum(old, jnp.max(s, axis=0, keepdims=True))
        p = jnp.exp2(s - top)
        keep = jnp.exp2(old - top)
        top_out[i] = top
        total_out[i] = total_ref[i] * keep + jnp.sum(p, axis=0, keepdims=True)
        o_out[i] = o_ref[i] * keep + weigh(head_of(v_ref, i), p.astype(jnp.bfloat16))


def last_scores_kernel(distance, place_ref, q_ref, k_ref, top_ref, total_ref, o_ref, w_out, o_out):
    for i in range(o_ref.shape[0]):
        s = scores_of(head_of(k_ref, i), stacked(q_ref, i)) + seen(place_ref, distance)
        old = top_ref[i]
        top = jnp.maximum(old, jnp.max(s, axis=0, keepdims=True))
        p = jnp.exp2(s - top)
        keep = jnp.exp2(old - top)
        inverse = 1.0 / (total_ref[i] * keep + jnp.sum(p, axis=0, keepdims=True))
        w_out[i] = (p * inverse).astype(jnp.bfloat16)
        o_out[i] = o_ref[i] * (keep * inverse)


def put_product(att, weight_refs, columns, out_refs):
    product = product_of(att, weight_refs, columns)
    part = out_refs[0].shape[0]
    for i, out_ref in enumerate(out_refs):
        out_ref[...] = product[i * part : (i + 1) * part].astype(jnp.bfloat16)


def last_values_kernel(pieces, columns, w_ref, o_ref, v_ref, *refs):
    weight_refs, (att_ref, *out_refs) = refs[:pieces], refs[pieces:]
    for i in range(o_ref.shape[0]):
        put_heads(att_ref, i, o_ref[i] + weigh(head_of(v_ref, i), w_ref[i]))
    far = len(out_refs) * out_refs[0].shape[0]
    put_product(att_ref[0:far, :], weight_refs, columns, out_refs)


def project_kernel(pieces, first, columns, att_ref, *refs):
    weight_refs, out_refs = refs[:pieces], refs[pieces:]
    count = len(out_refs) * out_refs[0].shape[0]
    put_product(att_ref[first : first + count, :], weight_refs, columns, out_refs)


def finish_kernel(ranges, steps, first, place_ref, mine_ref, got_ref, *refs):
    far_refs, refs = refs[: len(ranges) * steps], list(refs[len(ranges) * steps :])
    sem, staged = refs.pop(), [refs.pop() for _ in ranges][::-1]
    out_ref = refs.pop()
    if not first:
        refs.pop()
    target = None
    if refs:
        own_ref, back_ref = refs
        target = out_ref.at[out_ref.shape[0] - own_ref.shape[0] : out_ref.shape[0]]

        @pl.when(place_ref[0] == 0)
        def _own():
            pltpu.make_async_copy(own_ref, target, sem.at[len(ranges)]).start()

        @pl.when(place_ref[0] != 0)
        def _back():
            pltpu.make_async_copy(back_ref, target, sem.at[len(ranges)]).start()

    copies = []
    for index, columns in enumerate(ranges):
        span = slice(columns[0], columns[1])
        total = mine_ref[:, span].astype(jnp.float32) + got_ref[:, span].astype(jnp.float32)
        for far_ref in far_refs[index * steps : (index + 1) * steps]:
            total = total + far_ref[...].astype(jnp.float32)
        staged[index][...] = total.astype(jnp.bfloat16)
        copies.append(
            pltpu.make_async_copy(staged[index], out_ref.at[0 : mine_ref.shape[0], span], sem.at[index])
        )
        copies[-1].start()
    for copy in copies:
        copy.wait()
    if target is not None:
        pltpu.make_async_copy(back_ref, target, sem.at[len(ranges)]).wait()


def write(kernel, out_shape, scratch, out, *operands, scalars=0):
    operands = [value if i < scalars else in_vmem(value) for i, value in enumerate(operands)]
    specs = [SMEM] * scalars + [VMEM] * (len(operands) - scalars)
    aliases = {}
    if out is not None:
        aliases = {len(operands): 0}
        operands.append(out)
        specs.append(pl.BlockSpec(memory_space=pltpu.HBM))
    return pl.pallas_call(
        kernel,
        in_specs=specs,
        out_specs=pl.BlockSpec(memory_space=pltpu.HBM),
        out_shape=jax.ShapeDtypeStruct(out_shape, jnp.bfloat16),
        scratch_shapes=scratch,
        input_output_aliases=aliases,
        compiler_params=pltpu.CompilerParams(vmem_limit_bytes=8 << 20),
    )(*operands)


def ring(value, axis, distance):
    count = lax.axis_size(axis)
    return lax.ppermute(value, axis, [(s, (s + distance) % count) for s in range(count)])


def pass_on(value, distance):
    count = lax.axis_size("seq")
    return lax.ppermute(value, "seq", [(s, s + distance) for s in range(distance, count - distance)])


def swap(value):
    count = lax.axis_size("head")
    return lax.ppermute(value, "head", [(h, h ^ 1) for h in range(count)])


def tile_of(width):
    return max(t for t in range(128, 1024, 128) if width % t == 0 and (t % 256 == 0 or width % 256))


def on_device(queries, keys, values, out_weight):
    rows, depth = queries.shape
    width = out_weight.shape[1]
    heads = lax.axis_size("head")
    seq_count = lax.axis_size("seq")
    place = lax.axis_index("seq").astype(jnp.int32)[None]
    me = lax.axis_index("head")
    chips = heads // CORES
    part = rows // heads
    kv_local = keys.shape[1] // HEAD_SIZE
    reaches = [1 << level for level in range(seq_count.bit_length() - 1)]
    f32, bf16 = jnp.float32, jnp.bfloat16

    moved = part // 3 if reaches == [1, 2] and part % 48 == 0 else 0
    kept = part - moved
    parts = 2 * chips

    onward = [(s, s + 1) for s in range(seq_count - 1)]
    k_now, v_now = ring(keys, "seq", 1), lax.ppermute(values, "seq", onward)

    chip, core = me // CORES, me % CORES
    owners = []
    for step in range(1, chips + 1):
        base = ((chip + step) % chips) * CORES
        owners += [base + 1 - core, base + core]

    def rows_from(first, count):
        starts = [owner * part + first for owner in owners]
        q = jnp.concatenate([lax.dynamic_slice_in_dim(queries, start, count, 0) for start in starts], axis=0)
        pos = jnp.concatenate([start + jnp.arange(count, dtype=jnp.int32) for start in starts])
        return jnp.concatenate([pos] * GROUP)[None], in_vmem(q)

    if moved:
        pack, att_own = call(
            moving_kernel,
            [((kv_local, PACKED, GROUP * moved * parts), bf16), ((moved * parts, depth), bf16)],
            place,
            keys,
            values,
            *rows_from(kept, moved),
            scalars=1,
        )
        pack = lax.ppermute(pack, "seq", [(s, s - 1) for s in range(1, seq_count)])
    lanes = GROUP * kept * parts
    line, block = (kv_local, 1, lanes), (kv_local, HEAD_SIZE, lanes)
    state = [(line, f32), (line, f32), (block, f32)]
    pos, q = rows_from(0, kept)
    count = depth // 2 if moved else depth
    kernel = functools.partial(loading, local_kernel)
    *carried, top = call(kernel, state, place, keys, values, pos, q, scalars=1, load=(out_weight, 0, count))
    weights = [top]
    if moved:
        pair_outs = [((moved * chips, width), bf16)] * 2
        kernel = functools.partial(own_kernel, chips)
        *own_parts, rest = call(
            kernel, pair_outs, place, att_own, top, scalars=1, load=(out_weight, count, depth - count)
        )
        weights.append(rest)

    def settle(theirs, mine, everywhere):
        axes = "head" if everywhere else ("seq", "head")
        got = lax.ppermute(theirs, axes, [(h, h ^ 1) for h in range(heads)])
        both = mine.astype(f32) + got.astype(f32)
        total = both[(chips - 1) * moved :]
        for step in range(1, chips):
            piece = both[(step - 1) * moved : step * moved].astype(bf16)
            moves = [(h, (h + step * CORES) % heads) for h in range(heads)]
            total = total + lax.ppermute(piece, axes, moves).astype(f32)
        return total.astype(bf16)

    if moved:
        own_rows = settle(*own_parts, False)

    tile = tile_of(width)
    tiles = width // tile
    back = None
    for distance in reaches[:-1]:
        k_here, v_here = k_now, v_now
        k_now = pass_on(k_here, distance)
        v_now = pass_on(v_here, distance)
        if moved:
            border = tile * (tiles // 2)
            halves = [(0, border), (border, width)]
            shapes = [[((moved * chips, c[1] - c[0]), bf16)] * 2 for c in halves]
            att_moved, *early_parts = call(
                functools.partial(early_kernel, chips, reaches, halves[0]),
                [((moved * parts, depth), bf16)] + shapes[0],
                place,
                keys,
                k_here,
                values,
                v_here,
                pack,
                *weights,
                scalars=1,
            )
            late_parts = call(functools.partial(pairs_kernel, chips, halves[1]), shapes[1], att_moved, *weights)
            done = [settle(*early_parts, True), settle(*late_parts, True)]
            back = lax.ppermute(jnp.concatenate(done, axis=1), "seq", onward)
        carried = call(functools.partial(middle_kernel, distance), state, place, q, k_here, v_here, *carried, scalars=1)
    probs, scaled = call(
        functools.partial(last_scores_kernel, reaches[-1]),
        [((kv_local, rows, lanes), bf16), (block, f32)],
        place,
        q,
        k_now,
        *carried,
        scalars=1,
    )

    bounds = sorted({0, tile, tile * ((tiles + 1) // 2), width})
    chunks = list(zip(bounds[:-1], bounds[1:]))
    far_parts = parts - 2

    def parts_of(count, columns):
        return [((kept, columns[1] - columns[0]), bf16)] * count

    att, *first_far = call(
        functools.partial(last_values_kernel, len(weights), chunks[0]),
        [((kept * parts, depth), bf16)] + parts_of(far_parts, chunks[0]),
        probs,
        scaled,
        v_now,
        *weights,
    )
    arrived = []
    for index, columns in enumerate(chunks):
        far = first_far
        if index:
            kernel = functools.partial(project_kernel, len(weights), 0, columns)
            far = call(kernel, parts_of(far_parts, columns), att, *weights)
        here = []
        for step in range(1, chips):
            theirs, mine = far[2 * step - 2], far[2 * step - 1]
            got = swap(theirs)
            both = (mine.astype(f32) + got.astype(f32)).astype(bf16)
            here.append(ring(both, "head", step * CORES))
        arrived.append(here)
    whole = (0, width)
    kernel = functools.partial(project_kernel, len(weights), far_parts * kept, whole)
    theirs, mine = call(kernel, parts_of(2, whole), att, *weights)
    got = swap(theirs)
    out = None
    for group in (range(len(chunks) - 1), range(len(chunks) - 1, len(chunks))):
        ranges = [chunks[i] for i in group]
        last = group.stop == len(chunks)
        out = write(
            functools.partial(finish_kernel, ranges, chips - 1, out is None),
            (part, width),
            [pltpu.VMEM((kept, c[1] - c[0]), bf16) for c in ranges] + [pltpu.SemaphoreType.DMA((len(ranges) + 1,))],
            out,
            place,
            mine,
            got,
            *[value for i in group for value in arrived[i]],
            *([own_rows, back] if moved and last else []),
            scalars=1,
        )
    return out


def solution(mesh):
    in_specs = (
        P(("grp", "seq"), "head"),
        P(("grp", "seq"), "head"),
        P(("grp", "seq"), "head"),
        P("head", None),
    )
    out_specs = P(("grp", "seq", "head"), None)

    return jax.shard_map(on_device, mesh=mesh, in_specs=in_specs, out_specs=out_specs, check_vma=False)
```

```python
import functools
import math

import jax
import jax.numpy as jnp
from jax import lax
from jax.experimental import pallas as pl
from jax.experimental.pallas import tpu as pltpu
from jax.sharding import PartitionSpec as P

QUERY_HEADS = 32
KEY_VALUE_HEADS = 16
HEAD_SIZE = 128
GROUP = QUERY_HEADS // KEY_VALUE_HEADS
CORES = 2

SCALE2 = 168.0**-0.5 * math.log2(math.e)


VMEM = pl.BlockSpec(memory_space=pltpu.VMEM)
SMEM = pl.BlockSpec(memory_space=pltpu.SMEM)


def in_vmem(value):
    return pltpu.with_memory_space_constraint(value, pltpu.VMEM)


def bring(source_ref, first, out_ref, sems):
    pieces = sems.shape[0]
    rows = out_ref.shape[0] // pieces
    copies = []
    for i in range(pieces):
        block = pl.ds(i * rows, rows)
        copies.append(
            pltpu.make_async_copy(source_ref.at[pl.ds(first + i * rows, rows)], out_ref.at[block], sems.at[i])
        )
        copies[-1].start()
    return copies


def loading(kernel, first, source_ref, *refs):
    copies = bring(source_ref, first, *refs[-2:])

    @pl.when(refs[0][0] >= 0)
    def _compute():
        kernel(*refs[:-2])

    for copy in copies:
        copy.wait()


def call(kernel, outs, *operands, scalars=0, load=None, scratch=()):
    operands = [value if i < scalars else in_vmem(value) for i, value in enumerate(operands)]
    specs = [SMEM] * scalars + [VMEM] * (len(operands) - scalars)
    outs = [pltpu.VMEM(shape, dtype) for shape, dtype in outs]
    scratch = list(scratch)
    if load is not None:
        source, first, count = load
        kernel = functools.partial(kernel, first)
        operands = [pltpu.with_memory_space_constraint(source, pltpu.HBM)] + operands
        specs = [pl.BlockSpec(memory_space=pltpu.HBM)] + specs
        outs.append(pltpu.VMEM((count, source.shape[1]), source.dtype))
        scratch.append(pltpu.SemaphoreType.DMA((4,)))
    return pl.pallas_call(
        kernel,
        in_specs=specs,
        out_specs=[VMEM] * len(outs),
        out_shape=outs,
        scratch_shapes=scratch,
        compiler_params=pltpu.CompilerParams(vmem_limit_bytes=20 << 20),
    )(*operands)


def stacked(q_ref, i):
    first = i * GROUP
    return jnp.concatenate(
        [q_ref[:, (first + g) * HEAD_SIZE : (first + g + 1) * HEAD_SIZE] for g in range(GROUP)], axis=0
    )


def head_of(ref, i):
    return ref[:, i * HEAD_SIZE : (i + 1) * HEAD_SIZE]


def scores_of(k, q):
    return lax.dot_general(k, q, (((1,), (1,)), ((), ())), preferred_element_type=jnp.float32) * SCALE2


def weigh(v, p):
    return lax.dot_general(v, p, (((0,), (0,)), ((), ())), preferred_element_type=jnp.float32)


def thirds(value):
    high = value.astype(jnp.bfloat16).astype(jnp.float32)
    middle = (value - high).astype(jnp.bfloat16).astype(jnp.float32)
    return [high, middle, value - high - middle]


LINES = HEAD_SIZE + 16
PACKED = LINES + HEAD_SIZE


def put_heads(att_ref, i, o):
    rows = att_ref.shape[0]
    o = o.T.astype(jnp.bfloat16)
    for g in range(GROUP):
        head = i * GROUP + g
        att_ref[:, head * HEAD_SIZE : (head + 1) * HEAD_SIZE] = o[g * rows : (g + 1) * rows]


def local_part(pos_ref, q_ref, k_ref, v_ref, i):
    s = scores_of(head_of(k_ref, i), stacked(q_ref, i))
    s = jnp.where(pos_ref[...] >= lax.broadcasted_iota(jnp.int32, s.shape, 0), s, -jnp.inf)
    top = jnp.max(s, axis=0, keepdims=True)
    p = jnp.exp2(s - top)
    return top, jnp.sum(p, axis=0, keepdims=True), weigh(head_of(v_ref, i), p.astype(jnp.bfloat16))


def local_kernel(place_ref, k_ref, v_ref, pos_ref, q_ref, top_ref, total_ref, o_ref):
    for i in range(o_ref.shape[0]):
        top_ref[i], total_ref[i], o_ref[i] = local_part(pos_ref, q_ref, k_ref, v_ref, i)


def moving_kernel(place_ref, k_ref, v_ref, pos_ref, q_ref, pack_ref, att_ref):
    for i in range(pack_ref.shape[0]):
        top, total, o = local_part(pos_ref, q_ref, k_ref, v_ref, i)
        pack_ref[i, 0:HEAD_SIZE] = o.astype(jnp.bfloat16)
        lines = thirds(top) + thirds(total)
        lines.append(jnp.zeros((LINES - HEAD_SIZE - len(lines), top.shape[1]), jnp.float32))
        pack_ref[i, HEAD_SIZE:LINES] = jnp.concatenate(lines, axis=0).astype(jnp.bfloat16)
        pack_ref[i, LINES:PACKED] = stacked(q_ref, i).astype(jnp.float32).T.astype(jnp.bfloat16)
        put_heads(att_ref, i, o * (1.0 / total))


def early_kernel(chips, distances, columns, place_ref, *refs):
    count = len(distances)
    k_refs, v_refs = refs[:count], refs[count : 2 * count]
    pack_ref, *weight_refs, att_ref, theirs_ref, mine_ref = refs[2 * count :]
    for i in range(pack_ref.shape[0]):
        q = pack_ref[i, LINES:PACKED]
        extra = pack_ref[i, HEAD_SIZE:LINES].astype(jnp.float32)
        top = extra[0:1] + extra[1:2] + extra[2:3]
        total = extra[3:4] + extra[4:5] + extra[5:6]
        parts = [
            jnp.dot(head_of(k_ref, i), q, preferred_element_type=jnp.float32) * SCALE2
            + jnp.where(place_ref[0] + 1 >= distance, 0.0, -jnp.inf)
            for distance, k_ref in zip(distances, k_refs)
        ]
        new_top = functools.reduce(jnp.maximum, [top] + [jnp.max(s, axis=0, keepdims=True) for s in parts])
        keep = jnp.exp2(top - new_top)
        total = total * keep
        o = pack_ref[i, 0:HEAD_SIZE].astype(jnp.float32) * keep
        for s, v_ref in zip(parts, v_refs):
            p = jnp.exp2(s - new_top)
            total = total + jnp.sum(p, axis=0, keepdims=True)
            o = o + weigh(head_of(v_ref, i), p.astype(jnp.bfloat16))
        put_heads(att_ref, i, o * (1.0 / total))
    put_pairs(chips, product_of(att_ref[...], weight_refs, columns), theirs_ref, mine_ref)


def product_of(att, weight_refs, columns):
    total, first = None, 0
    for weight_ref in weight_refs:
        last = first + weight_ref.shape[0]
        piece = jnp.dot(
            att[:, first:last], weight_ref[:, columns[0] : columns[1]], preferred_element_type=jnp.float32
        )
        total, first = piece if total is None else total + piece, last
    return total


def put_pairs(chips, product, theirs_ref, mine_ref):
    product = product.astype(jnp.bfloat16)
    part = product.shape[0] // (2 * chips)
    for chip in range(chips):
        block = slice(chip * part, (chip + 1) * part)
        theirs_ref[block, :] = product[2 * chip * part : (2 * chip + 1) * part]
        mine_ref[block, :] = product[(2 * chip + 1) * part : (2 * chip + 2) * part]


def own_kernel(chips, first, source_ref, place_ref, att_ref, top_ref, *refs):
    theirs_ref, mine_ref, rest_ref, total, sems = refs
    columns = (0, rest_ref.shape[1])
    copies = bring(source_ref, first, rest_ref, sems)

    @pl.when(place_ref[0] == 0)
    def _top():
        total[...] = product_of(att_ref[:, 0:first], [top_ref], columns)

    for copy in copies:
        copy.wait()

    @pl.when(place_ref[0] == 0)
    def _rest():
        rest = product_of(att_ref[:, first : att_ref.shape[1]], [rest_ref], columns)
        put_pairs(chips, total[...] + rest, theirs_ref, mine_ref)


def pairs_kernel(chips, columns, att_ref, *refs):
    *weight_refs, theirs_ref, mine_ref = refs
    put_pairs(chips, product_of(att_ref[...], weight_refs, columns), theirs_ref, mine_ref)


def seen(place_ref, distance):
    return jnp.where(place_ref[0] >= distance, 0.0, -jnp.inf).astype(jnp.float32)


def middle_kernel(distance, place_ref, q_ref, k_ref, v_ref, top_ref, total_ref, o_ref, top_out, total_out, o_out):
    for i in range(o_ref.shape[0]):
        s = scores_of(head_of(k_ref, i), stacked(q_ref, i)) + seen(place_ref, distance)
        old = top_ref[i]
        top = jnp.maximum(old, jnp.max(s, axis=0, keepdims=True))
        p = jnp.exp2(s - top)
        keep = jnp.exp2(old - top)
        top_out[i] = top
        total_out[i] = total_ref[i] * keep + jnp.sum(p, axis=0, keepdims=True)
        o_out[i] = o_ref[i] * keep + weigh(head_of(v_ref, i), p.astype(jnp.bfloat16))


def last_scores_kernel(distance, place_ref, q_ref, k_ref, top_ref, total_ref, o_ref, w_out, o_out):
    for i in range(o_ref.shape[0]):
        s = scores_of(head_of(k_ref, i), stacked(q_ref, i)) + seen(place_ref, distance)
        old = top_ref[i]
        top = jnp.maximum(old, jnp.max(s, axis=0, keepdims=True))
        p = jnp.exp2(s - top)
        keep = jnp.exp2(old - top)
        inverse = 1.0 / (total_ref[i] * keep + jnp.sum(p, axis=0, keepdims=True))
        w_out[i] = (p * inverse).astype(jnp.bfloat16)
        o_out[i] = o_ref[i] * (keep * inverse)


def put_product(att, weight_refs, columns, out_refs):
    product = product_of(att, weight_refs, columns)
    part = out_refs[0].shape[0]
    for i, out_ref in enumerate(out_refs):
        out_ref[...] = product[i * part : (i + 1) * part].astype(jnp.bfloat16)


def put_values(att_ref, first, w_ref, o_ref, v_ref):
    rows, every = att_ref.shape[0], o_ref.shape[2] // GROUP
    spans = [slice(g * every + first, g * every + first + rows) for g in range(GROUP)]
    for i in range(o_ref.shape[0]):
        w = jnp.concatenate([w_ref[i, :, span] for span in spans], axis=1)
        o = jnp.concatenate([o_ref[i, :, span] for span in spans], axis=1)
        put_heads(att_ref, i, o + weigh(head_of(v_ref, i), w))


def last_values_kernel(pieces, columns, w_ref, o_ref, v_ref, *refs):
    weight_refs, (att_ref, *out_refs) = refs[:pieces], refs[pieces:]
    put_values(att_ref, 0, w_ref, o_ref, v_ref)
    far = len(out_refs) * out_refs[0].shape[0]
    put_product(att_ref[0:far, :], weight_refs, columns, out_refs)


def near_kernel(pieces, first, columns, w_ref, o_ref, v_ref, *refs):
    weight_refs, (theirs_ref, mine_ref, att_ref) = refs[:pieces], refs[pieces:]
    put_values(att_ref, first, w_ref, o_ref, v_ref)
    put_product(att_ref[...], weight_refs, columns, [theirs_ref, mine_ref])


def project_kernel(pieces, first, columns, att_ref, *refs):
    weight_refs, out_refs = refs[:pieces], refs[pieces:]
    count = len(out_refs) * out_refs[0].shape[0]
    put_product(att_ref[first : first + count, :], weight_refs, columns, out_refs)


def finish_kernel(ranges, steps, first, place_ref, mine_ref, got_ref, *refs):
    far_refs, refs = refs[: len(ranges) * steps], list(refs[len(ranges) * steps :])
    sem, staged = refs.pop(), [refs.pop() for _ in ranges][::-1]
    out_ref = refs.pop()
    if not first:
        refs.pop()
    target = None
    if refs:
        own_ref, back_ref = refs
        target = out_ref.at[out_ref.shape[0] - own_ref.shape[0] : out_ref.shape[0]]

        @pl.when(place_ref[0] == 0)
        def _own():
            pltpu.make_async_copy(own_ref, target, sem.at[len(ranges)]).start()

        @pl.when(place_ref[0] != 0)
        def _back():
            pltpu.make_async_copy(back_ref, target, sem.at[len(ranges)]).start()

    copies = []
    for index, columns in enumerate(ranges):
        span = slice(columns[0], columns[1])
        total = mine_ref[:, span].astype(jnp.float32) + got_ref[:, span].astype(jnp.float32)
        for far_ref in far_refs[index * steps : (index + 1) * steps]:
            total = total + far_ref[...].astype(jnp.float32)
        staged[index][...] = total.astype(jnp.bfloat16)
        copies.append(
            pltpu.make_async_copy(staged[index], out_ref.at[0 : mine_ref.shape[0], span], sem.at[index])
        )
        copies[-1].start()
    for copy in copies:
        copy.wait()
    if target is not None:
        pltpu.make_async_copy(back_ref, target, sem.at[len(ranges)]).wait()


def write(kernel, out_shape, scratch, out, *operands, scalars=0):
    operands = [value if i < scalars else in_vmem(value) for i, value in enumerate(operands)]
    specs = [SMEM] * scalars + [VMEM] * (len(operands) - scalars)
    aliases = {}
    if out is not None:
        aliases = {len(operands): 0}
        operands.append(out)
        specs.append(pl.BlockSpec(memory_space=pltpu.HBM))
    return pl.pallas_call(
        kernel,
        in_specs=specs,
        out_specs=pl.BlockSpec(memory_space=pltpu.HBM),
        out_shape=jax.ShapeDtypeStruct(out_shape, jnp.bfloat16),
        scratch_shapes=scratch,
        input_output_aliases=aliases,
        compiler_params=pltpu.CompilerParams(vmem_limit_bytes=8 << 20),
    )(*operands)


def ring(value, axis, distance):
    count = lax.axis_size(axis)
    return lax.ppermute(value, axis, [(s, (s + distance) % count) for s in range(count)])


def pass_on(value, distance):
    count = lax.axis_size("seq")
    return lax.ppermute(value, "seq", [(s, s + distance) for s in range(distance, count - distance)])


def swap(value):
    count = lax.axis_size("head")
    return lax.ppermute(value, "head", [(h, h ^ 1) for h in range(count)])


def tile_of(width):
    return max(t for t in range(128, 1024, 128) if width % t == 0 and (t % 256 == 0 or width % 256))


def on_device(queries, keys, values, out_weight):
    rows, depth = queries.shape
    width = out_weight.shape[1]
    heads = lax.axis_size("head")
    seq_count = lax.axis_size("seq")
    place = lax.axis_index("seq").astype(jnp.int32)[None]
    me = lax.axis_index("head")
    chips = heads // CORES
    part = rows // heads
    kv_local = keys.shape[1] // HEAD_SIZE
    reaches = [1 << level for level in range(seq_count.bit_length() - 1)]
    f32, bf16 = jnp.float32, jnp.bfloat16

    moved = part // 3 if reaches == [1, 2] and part % 48 == 0 else 0
    kept = part - moved
    parts = 2 * chips

    onward = [(s, s + 1) for s in range(seq_count - 1)]
    k_now, v_now = ring(keys, "seq", 1), lax.ppermute(values, "seq", onward)

    chip, core = me // CORES, me % CORES
    owners = []
    for step in range(1, chips + 1):
        base = ((chip + step) % chips) * CORES
        owners += [base + 1 - core, base + core]

    def rows_from(first, count):
        starts = [owner * part + first for owner in owners]
        q = jnp.concatenate([lax.dynamic_slice_in_dim(queries, start, count, 0) for start in starts], axis=0)
        pos = jnp.concatenate([start + jnp.arange(count, dtype=jnp.int32) for start in starts])
        return jnp.concatenate([pos] * GROUP)[None], in_vmem(q)

    if moved:
        pack, att_own = call(
            moving_kernel,
            [((kv_local, PACKED, GROUP * moved * parts), bf16), ((moved * parts, depth), bf16)],
            place,
            keys,
            values,
            *rows_from(kept, moved),
            scalars=1,
        )
        pack = lax.ppermute(pack, "seq", [(s, s - 1) for s in range(1, seq_count)])
    lanes = GROUP * kept * parts
    line, block = (kv_local, 1, lanes), (kv_local, HEAD_SIZE, lanes)
    state = [(line, f32), (line, f32), (block, f32)]
    pos, q = rows_from(0, kept)
    count = depth // 2 if moved else depth
    kernel = functools.partial(loading, local_kernel)
    *carried, top = call(kernel, state, place, keys, values, pos, q, scalars=1, load=(out_weight, 0, count))
    weights = [top]
    if moved:
        pair_outs = [((moved * chips, width), bf16)] * 2
        kernel = functools.partial(own_kernel, chips)
        *own_parts, rest = call(
            kernel,
            pair_outs,
            place,
            att_own,
            top,
            scalars=1,
            load=(out_weight, count, depth - count),
            scratch=[pltpu.VMEM((moved * parts, width), f32)],
        )
        weights.append(rest)

    def settle(theirs, mine, everywhere):
        axes = "head" if everywhere else ("seq", "head")
        got = swap(theirs)
        both = mine.astype(f32) + got.astype(f32)
        total = both[(chips - 1) * moved :]
        for step in range(1, chips):
            piece = both[(step - 1) * moved : step * moved].astype(bf16)
            moves = [(h, (h + step * CORES) % heads) for h in range(heads)]
            total = total + lax.ppermute(piece, axes, moves).astype(f32)
        return total.astype(bf16)

    if moved:
        own_rows = settle(*own_parts, False)

    tile = tile_of(width)
    tiles = width // tile
    back = None
    for distance in reaches[:-1]:
        k_here, v_here = k_now, v_now
        k_now = pass_on(k_here, distance)
        v_now = pass_on(v_here, distance)
        if moved:
            border = tile * (tiles // 2)
            halves = [(0, border), (border, width)]
            shapes = [[((moved * chips, c[1] - c[0]), bf16)] * 2 for c in halves]
            att_moved, *early_parts = call(
                functools.partial(early_kernel, chips, reaches, halves[0]),
                [((moved * parts, depth), bf16)] + shapes[0],
                place,
                keys,
                k_here,
                values,
                v_here,
                pack,
                *weights,
                scalars=1,
            )
            late_parts = call(functools.partial(pairs_kernel, chips, halves[1]), shapes[1], att_moved, *weights)
            done = [settle(*early_parts, True), settle(*late_parts, True)]
            back = lax.ppermute(jnp.concatenate(done, axis=1), "seq", onward)
        carried = call(functools.partial(middle_kernel, distance), state, place, q, k_here, v_here, *carried, scalars=1)
    probs, scaled = call(
        functools.partial(last_scores_kernel, reaches[-1]),
        [((kv_local, rows, lanes), bf16), (block, f32)],
        place,
        q,
        k_now,
        *carried,
        scalars=1,
    )

    bounds = sorted({0, tile, tile * max(1, tiles - 2), width})
    chunks = list(zip(bounds[:-1], bounds[1:]))
    far_parts = parts - 2

    def parts_of(count, columns):
        return [((kept, columns[1] - columns[0]), bf16)] * count

    apart = (far_parts * kept) % 128 == 0 and (2 * kept) % 128 == 0
    first_rows = (far_parts if apart else parts) * kept
    att, *first_far = call(
        functools.partial(last_values_kernel, len(weights), chunks[0]),
        [((first_rows, depth), bf16)] + parts_of(far_parts, chunks[0]),
        probs,
        scaled,
        v_now,
        *weights,
    )
    arrived = []
    for index, columns in enumerate(chunks):
        far = first_far
        if index:
            kernel = functools.partial(project_kernel, len(weights), 0, columns)
            far = call(kernel, parts_of(far_parts, columns), att, *weights)
        here = []
        for step in range(1, chips):
            theirs, mine = far[2 * step - 2], far[2 * step - 1]
            got = swap(theirs)
            both = (mine.astype(f32) + got.astype(f32)).astype(bf16)
            here.append(ring(both, "head", step * CORES))
        arrived.append(here)
    whole = (0, width)
    shapes = parts_of(2, whole)
    if apart:
        kernel = functools.partial(near_kernel, len(weights), far_parts * kept, whole)
        att_near = [pltpu.VMEM((2 * kept, depth), bf16)]
        theirs, mine = call(kernel, shapes, probs, scaled, v_now, *weights, scratch=att_near)
    else:
        kernel = functools.partial(project_kernel, len(weights), far_parts * kept, whole)
        theirs, mine = call(kernel, shapes, att, *weights)
    got = swap(theirs)
    out = None
    for group in (range(len(chunks) - 1), range(len(chunks) - 1, len(chunks))):
        ranges = [chunks[i] for i in group]
        last = group.stop == len(chunks)
        out = write(
            functools.partial(finish_kernel, ranges, chips - 1, out is None),
            (part, width),
            [pltpu.VMEM((kept, c[1] - c[0]), bf16) for c in ranges] + [pltpu.SemaphoreType.DMA((len(ranges) + 1,))],
            out,
            place,
            mine,
            got,
            *[value for i in group for value in arrived[i]],
            *([own_rows, back] if moved and last else []),
            scalars=1,
        )
    return out


def solution(mesh):
    in_specs = (
        P(("grp", "seq"), "head"),
        P(("grp", "seq"), "head"),
        P(("grp", "seq"), "head"),
        P("head", None),
    )
    out_specs = P(("grp", "seq", "head"), None)

    return jax.shard_map(on_device, mesh=mesh, in_specs=in_specs, out_specs=out_specs, check_vma=False)
```

```python
import functools
import math

import jax
import jax.numpy as jnp
from jax import lax
from jax.experimental import pallas as pl
from jax.experimental.pallas import tpu as pltpu
from jax.sharding import PartitionSpec as P

QUERY_HEADS = 32
KEY_VALUE_HEADS = 16
HEAD_SIZE = 128
GROUP = QUERY_HEADS // KEY_VALUE_HEADS
CORES = 2

SCALE2 = 168.0**-0.5 * math.log2(math.e)


VMEM = pl.BlockSpec(memory_space=pltpu.VMEM)
SMEM = pl.BlockSpec(memory_space=pltpu.SMEM)


def in_vmem(value):
    return pltpu.with_memory_space_constraint(value, pltpu.VMEM)


def bring(source_ref, first, out_ref, sems):
    pieces = sems.shape[0]
    rows = out_ref.shape[0] // pieces
    copies = []
    for i in range(pieces):
        block = pl.ds(i * rows, rows)
        copies.append(
            pltpu.make_async_copy(source_ref.at[pl.ds(first + i * rows, rows)], out_ref.at[block], sems.at[i])
        )
        copies[-1].start()
    return copies


def loading(kernel, first, source_ref, *refs):
    copies = bring(source_ref, first, *refs[-2:])

    @pl.when(refs[0][0] >= 0)
    def _compute():
        kernel(*refs[:-2])

    for copy in copies:
        copy.wait()


def call(kernel, outs, *operands, scalars=0, load=None, scratch=()):
    operands = [value if i < scalars else in_vmem(value) for i, value in enumerate(operands)]
    specs = [SMEM] * scalars + [VMEM] * (len(operands) - scalars)
    outs = [pltpu.VMEM(shape, dtype) for shape, dtype in outs]
    scratch = list(scratch)
    if load is not None:
        source, first, count = load
        kernel = functools.partial(kernel, first)
        operands = [pltpu.with_memory_space_constraint(source, pltpu.HBM)] + operands
        specs = [pl.BlockSpec(memory_space=pltpu.HBM)] + specs
        outs.append(pltpu.VMEM((count, source.shape[1]), source.dtype))
        scratch.append(pltpu.SemaphoreType.DMA((4,)))
    return pl.pallas_call(
        kernel,
        in_specs=specs,
        out_specs=[VMEM] * len(outs),
        out_shape=outs,
        scratch_shapes=scratch,
        compiler_params=pltpu.CompilerParams(vmem_limit_bytes=20 << 20),
    )(*operands)


def stacked(q_ref, i):
    first = i * GROUP
    return jnp.concatenate(
        [q_ref[:, (first + g) * HEAD_SIZE : (first + g + 1) * HEAD_SIZE] for g in range(GROUP)], axis=0
    )


def head_of(ref, i):
    return ref[:, i * HEAD_SIZE : (i + 1) * HEAD_SIZE]


def scores_of(k, q):
    return lax.dot_general(k, q, (((1,), (1,)), ((), ())), preferred_element_type=jnp.float32) * SCALE2


def weigh(v, p):
    return lax.dot_general(v, p, (((0,), (0,)), ((), ())), preferred_element_type=jnp.float32)


def thirds(value):
    high = value.astype(jnp.bfloat16).astype(jnp.float32)
    middle = (value - high).astype(jnp.bfloat16).astype(jnp.float32)
    return [high, middle, value - high - middle]


LINES = HEAD_SIZE + 16
PACKED = LINES + HEAD_SIZE


def put_heads(att_ref, i, o):
    rows = att_ref.shape[0]
    o = o.T.astype(jnp.bfloat16)
    for g in range(GROUP):
        head = i * GROUP + g
        att_ref[:, head * HEAD_SIZE : (head + 1) * HEAD_SIZE] = o[g * rows : (g + 1) * rows]


def local_part(pos, q, k_ref, v_ref, i):
    s = scores_of(head_of(k_ref, i), q)
    s = jnp.where(pos >= lax.broadcasted_iota(jnp.int32, s.shape, 0), s, -jnp.inf)
    top = jnp.max(s, axis=0, keepdims=True)
    p = jnp.exp2(s - top)
    return top, jnp.sum(p, axis=0, keepdims=True), weigh(head_of(v_ref, i), p.astype(jnp.bfloat16))


def local_kernel(place_ref, k_ref, v_ref, pos_ref, q_ref, top_ref, total_ref, o_ref):
    for i in range(o_ref.shape[0]):
        top_ref[i], total_ref[i], o_ref[i] = local_part(pos_ref[...], stacked(q_ref, i), k_ref, v_ref, i)


def moving_kernel(part, moved, q_ref, k_ref, v_ref, pack_ref, att_ref):
    starts = range(part - moved, q_ref.shape[0], part)
    count = moved * len(starts)
    lane = lax.broadcasted_iota(jnp.int32, (1, GROUP * count), 1)
    pos = jnp.zeros_like(lane)
    for g in range(GROUP):
        for index, start in enumerate(starts):
            first = g * count + index * moved
            pos = jnp.where(lane >= first, lane - first + start, pos)
    for i in range(pack_ref.shape[0]):
        q = jnp.concatenate(
            [
                q_ref[start : start + moved, head * HEAD_SIZE : (head + 1) * HEAD_SIZE]
                for head in range(i * GROUP, (i + 1) * GROUP)
                for start in starts
            ],
            axis=0,
        )
        top, total, o = local_part(pos, q, k_ref, v_ref, i)
        pack_ref[i, 0:HEAD_SIZE] = o.astype(jnp.bfloat16)
        lines = thirds(top) + thirds(total)
        lines.append(jnp.zeros((LINES - HEAD_SIZE - len(lines), top.shape[1]), jnp.float32))
        pack_ref[i, HEAD_SIZE:LINES] = jnp.concatenate(lines, axis=0).astype(jnp.bfloat16)
        pack_ref[i, LINES:PACKED] = q.astype(jnp.float32).T.astype(jnp.bfloat16)
        put_heads(att_ref, i, o * (1.0 / total))


def ordered(chips, me_ref, att_ref):
    part = att_ref.shape[0] // (CORES * chips)
    chip, core = me_ref[0] // CORES, me_ref[0] % CORES
    blocks = []
    for step in range(1, chips + 1):
        base = ((chip + step) % chips) * CORES
        for owner in (base + 1 - core, base + core):
            blocks.append(att_ref[pl.ds(pl.multiple_of(owner * part, part), part), :])
    return jnp.concatenate(blocks, axis=0)


def early_kernel(chips, distances, columns, place_ref, me_ref, *refs):
    count = len(distances)
    k_refs, v_refs = refs[:count], refs[count : 2 * count]
    pack_ref, *weight_refs, att_ref, theirs_ref, mine_ref = refs[2 * count :]
    for i in range(pack_ref.shape[0]):
        q = pack_ref[i, LINES:PACKED]
        extra = pack_ref[i, HEAD_SIZE:LINES].astype(jnp.float32)
        top = extra[0:1] + extra[1:2] + extra[2:3]
        total = extra[3:4] + extra[4:5] + extra[5:6]
        parts = [
            jnp.dot(head_of(k_ref, i), q, preferred_element_type=jnp.float32) * SCALE2
            + jnp.where(place_ref[0] + 1 >= distance, 0.0, -jnp.inf)
            for distance, k_ref in zip(distances, k_refs)
        ]
        new_top = functools.reduce(jnp.maximum, [top] + [jnp.max(s, axis=0, keepdims=True) for s in parts])
        keep = jnp.exp2(top - new_top)
        total = total * keep
        o = pack_ref[i, 0:HEAD_SIZE].astype(jnp.float32) * keep
        for s, v_ref in zip(parts, v_refs):
            p = jnp.exp2(s - new_top)
            total = total + jnp.sum(p, axis=0, keepdims=True)
            o = o + weigh(head_of(v_ref, i), p.astype(jnp.bfloat16))
        put_heads(att_ref, i, o * (1.0 / total))
    put_pairs(chips, product_of(ordered(chips, me_ref, att_ref), weight_refs, columns), theirs_ref, mine_ref)


def product_of(att, weight_refs, columns):
    total, first = None, 0
    for weight_ref in weight_refs:
        last = first + weight_ref.shape[0]
        piece = jnp.dot(
            att[:, first:last], weight_ref[:, columns[0] : columns[1]], preferred_element_type=jnp.float32
        )
        total, first = piece if total is None else total + piece, last
    return total


def put_pairs(chips, product, theirs_ref, mine_ref):
    product = product.astype(jnp.bfloat16)
    part = product.shape[0] // (2 * chips)
    for chip in range(chips):
        block = slice(chip * part, (chip + 1) * part)
        theirs_ref[block, :] = product[2 * chip * part : (2 * chip + 1) * part]
        mine_ref[block, :] = product[(2 * chip + 1) * part : (2 * chip + 2) * part]


def own_kernel(chips, first, source_ref, place_ref, me_ref, att_ref, top_ref, *refs):
    theirs_ref, mine_ref, rest_ref, total, sems = refs
    columns = (0, rest_ref.shape[1])
    copies = bring(source_ref, first, rest_ref, sems)

    @pl.when(place_ref[0] == 0)
    def _top():
        total[...] = product_of(ordered(chips, me_ref, att_ref.at[:, 0:first]), [top_ref], columns)

    for copy in copies:
        copy.wait()

    @pl.when(place_ref[0] == 0)
    def _rest():
        rest = product_of(ordered(chips, me_ref, att_ref.at[:, first : att_ref.shape[1]]), [rest_ref], columns)
        put_pairs(chips, total[...] + rest, theirs_ref, mine_ref)


def pairs_kernel(chips, columns, me_ref, att_ref, *refs):
    *weight_refs, theirs_ref, mine_ref = refs
    put_pairs(chips, product_of(ordered(chips, me_ref, att_ref), weight_refs, columns), theirs_ref, mine_ref)


def seen(place_ref, distance):
    return jnp.where(place_ref[0] >= distance, 0.0, -jnp.inf).astype(jnp.float32)


def middle_kernel(distance, place_ref, q_ref, k_ref, v_ref, top_ref, total_ref, o_ref, top_out, total_out, o_out):
    for i in range(o_ref.shape[0]):
        s = scores_of(head_of(k_ref, i), stacked(q_ref, i)) + seen(place_ref, distance)
        old = top_ref[i]
        top = jnp.maximum(old, jnp.max(s, axis=0, keepdims=True))
        p = jnp.exp2(s - top)
        keep = jnp.exp2(old - top)
        top_out[i] = top
        total_out[i] = total_ref[i] * keep + jnp.sum(p, axis=0, keepdims=True)
        o_out[i] = o_ref[i] * keep + weigh(head_of(v_ref, i), p.astype(jnp.bfloat16))


def last_scores_kernel(distance, place_ref, q_ref, k_ref, top_ref, total_ref, o_ref, w_out, o_out):
    for i in range(o_ref.shape[0]):
        s = scores_of(head_of(k_ref, i), stacked(q_ref, i)) + seen(place_ref, distance)
        old = top_ref[i]
        top = jnp.maximum(old, jnp.max(s, axis=0, keepdims=True))
        p = jnp.exp2(s - top)
        keep = jnp.exp2(old - top)
        inverse = 1.0 / (total_ref[i] * keep + jnp.sum(p, axis=0, keepdims=True))
        w_out[i] = (p * inverse).astype(jnp.bfloat16)
        o_out[i] = o_ref[i] * (keep * inverse)


def put_product(att, weight_refs, columns, out_refs):
    product = product_of(att, weight_refs, columns)
    part = out_refs[0].shape[0]
    for i, out_ref in enumerate(out_refs):
        out_ref[...] = product[i * part : (i + 1) * part].astype(jnp.bfloat16)


def put_values(att_ref, first, w_ref, o_ref, v_ref):
    rows, every = att_ref.shape[0], o_ref.shape[2] // GROUP
    spans = [slice(g * every + first, g * every + first + rows) for g in range(GROUP)]
    for i in range(o_ref.shape[0]):
        w = jnp.concatenate([w_ref[i, :, span] for span in spans], axis=1)
        o = jnp.concatenate([o_ref[i, :, span] for span in spans], axis=1)
        put_heads(att_ref, i, o + weigh(head_of(v_ref, i), w))


def last_values_kernel(pieces, columns, w_ref, o_ref, v_ref, *refs):
    weight_refs, (att_ref, *out_refs) = refs[:pieces], refs[pieces:]
    put_values(att_ref, 0, w_ref, o_ref, v_ref)
    far = len(out_refs) * out_refs[0].shape[0]
    put_product(att_ref[0:far, :], weight_refs, columns, out_refs)


def near_kernel(pieces, first, columns, w_ref, o_ref, v_ref, *refs):
    weight_refs, (theirs_ref, mine_ref, att_ref) = refs[:pieces], refs[pieces:]
    put_values(att_ref, first, w_ref, o_ref, v_ref)
    put_product(att_ref[...], weight_refs, columns, [theirs_ref, mine_ref])


def project_kernel(pieces, first, columns, att_ref, *refs):
    weight_refs, out_refs = refs[:pieces], refs[pieces:]
    count = len(out_refs) * out_refs[0].shape[0]
    put_product(att_ref[first : first + count, :], weight_refs, columns, out_refs)


def finish_kernel(ranges, steps, first, place_ref, mine_ref, got_ref, *refs):
    far_refs, refs = refs[: len(ranges) * steps], list(refs[len(ranges) * steps :])
    sem, staged = refs.pop(), [refs.pop() for _ in ranges][::-1]
    out_ref = refs.pop()
    if not first:
        refs.pop()
    target = None
    if refs:
        own_ref, back_ref = refs
        target = out_ref.at[out_ref.shape[0] - own_ref.shape[0] : out_ref.shape[0]]

        @pl.when(place_ref[0] == 0)
        def _own():
            pltpu.make_async_copy(own_ref, target, sem.at[len(ranges)]).start()

        @pl.when(place_ref[0] != 0)
        def _back():
            pltpu.make_async_copy(back_ref, target, sem.at[len(ranges)]).start()

    copies = []
    for index, columns in enumerate(ranges):
        span = slice(columns[0], columns[1])
        total = mine_ref[:, span].astype(jnp.float32) + got_ref[:, span].astype(jnp.float32)
        for far_ref in far_refs[index * steps : (index + 1) * steps]:
            total = total + far_ref[...].astype(jnp.float32)
        staged[index][...] = total.astype(jnp.bfloat16)
        copies.append(
            pltpu.make_async_copy(staged[index], out_ref.at[0 : mine_ref.shape[0], span], sem.at[index])
        )
        copies[-1].start()
    for copy in copies:
        copy.wait()
    if target is not None:
        pltpu.make_async_copy(back_ref, target, sem.at[len(ranges)]).wait()


def write(kernel, out_shape, scratch, out, *operands, scalars=0):
    operands = [value if i < scalars else in_vmem(value) for i, value in enumerate(operands)]
    specs = [SMEM] * scalars + [VMEM] * (len(operands) - scalars)
    aliases = {}
    if out is not None:
        aliases = {len(operands): 0}
        operands.append(out)
        specs.append(pl.BlockSpec(memory_space=pltpu.HBM))
    return pl.pallas_call(
        kernel,
        in_specs=specs,
        out_specs=pl.BlockSpec(memory_space=pltpu.HBM),
        out_shape=jax.ShapeDtypeStruct(out_shape, jnp.bfloat16),
        scratch_shapes=scratch,
        input_output_aliases=aliases,
        compiler_params=pltpu.CompilerParams(vmem_limit_bytes=8 << 20),
    )(*operands)


def ring(value, axis, distance):
    count = lax.axis_size(axis)
    return lax.ppermute(value, axis, [(s, (s + distance) % count) for s in range(count)])


def pass_on(value, distance):
    count = lax.axis_size("seq")
    return lax.ppermute(value, "seq", [(s, s + distance) for s in range(distance, count - distance)])


def swap(value):
    count = lax.axis_size("head")
    return lax.ppermute(value, "head", [(h, h ^ 1) for h in range(count)])


def tile_of(width):
    return max(t for t in range(128, 1024, 128) if width % t == 0 and (t % 256 == 0 or width % 256))


def on_device(queries, keys, values, out_weight):
    rows, depth = queries.shape
    width = out_weight.shape[1]
    heads = lax.axis_size("head")
    seq_count = lax.axis_size("seq")
    place = lax.axis_index("seq").astype(jnp.int32)[None]
    me = lax.axis_index("head").astype(jnp.int32)
    chips = heads // CORES
    part = rows // heads
    kv_local = keys.shape[1] // HEAD_SIZE
    reaches = [1 << level for level in range(seq_count.bit_length() - 1)]
    f32, bf16 = jnp.float32, jnp.bfloat16

    moved = part // 3 if reaches == [1, 2] and part % 48 == 0 else 0
    kept = part - moved
    parts = 2 * chips

    onward = [(s, s + 1) for s in range(seq_count - 1)]
    k_now, v_now = ring(keys, "seq", 1), lax.ppermute(values, "seq", onward)

    chip, core = me // CORES, me % CORES
    owners = []
    for step in range(1, chips + 1):
        base = ((chip + step) % chips) * CORES
        owners += [base + 1 - core, base + core]

    if moved:
        pack, att_own = call(
            functools.partial(moving_kernel, part, moved),
            [((kv_local, PACKED, GROUP * moved * parts), bf16), ((moved * parts, depth), bf16)],
            queries,
            keys,
            values,
        )
        pack = lax.ppermute(pack, "seq", [(s, s - 1) for s in range(1, seq_count)])
    lanes = GROUP * kept * parts
    line, block = (kv_local, 1, lanes), (kv_local, HEAD_SIZE, lanes)
    state = [(line, f32), (line, f32), (block, f32)]
    starts = [owner * part for owner in owners]
    q = in_vmem(jnp.concatenate([lax.dynamic_slice_in_dim(queries, start, kept, 0) for start in starts], axis=0))
    pos = jnp.concatenate([start + jnp.arange(kept, dtype=jnp.int32) for start in starts] * GROUP)[None]
    count = depth // 2 if moved else depth
    kernel = functools.partial(loading, local_kernel)
    *carried, top = call(kernel, state, place, keys, values, pos, q, scalars=1, load=(out_weight, 0, count))
    weights = [top]
    if moved:
        pair_outs = [((moved * chips, width), bf16)] * 2
        kernel = functools.partial(own_kernel, chips)
        *own_parts, rest = call(
            kernel,
            pair_outs,
            place,
            me[None],
            att_own,
            top,
            scalars=2,
            load=(out_weight, count, depth - count),
            scratch=[pltpu.VMEM((moved * parts, width), f32)],
        )
        weights.append(rest)

    def settle(theirs, mine, everywhere):
        axes = "head" if everywhere else ("seq", "head")
        got = swap(theirs)
        both = mine.astype(f32) + got.astype(f32)
        total = both[(chips - 1) * moved :]
        for step in range(1, chips):
            piece = both[(step - 1) * moved : step * moved].astype(bf16)
            moves = [(h, (h + step * CORES) % heads) for h in range(heads)]
            total = total + lax.ppermute(piece, axes, moves).astype(f32)
        return total.astype(bf16)

    if moved:
        own_rows = settle(*own_parts, False)

    tile = tile_of(width)
    tiles = width // tile
    back = None
    for distance in reaches[:-1]:
        k_here, v_here = k_now, v_now
        k_now = pass_on(k_here, distance)
        v_now = pass_on(v_here, distance)
        if moved:
            border = tile * (tiles // 2)
            halves = [(0, border), (border, width)]
            shapes = [[((moved * chips, c[1] - c[0]), bf16)] * 2 for c in halves]
            att_moved, *early_parts = call(
                functools.partial(early_kernel, chips, reaches, halves[0]),
                [((moved * parts, depth), bf16)] + shapes[0],
                place,
                me[None],
                keys,
                k_here,
                values,
                v_here,
                pack,
                *weights,
                scalars=2,
            )
            late_parts = call(
                functools.partial(pairs_kernel, chips, halves[1]), shapes[1], me[None], att_moved, *weights, scalars=1
            )
            done = [settle(*early_parts, True), settle(*late_parts, True)]
            back = lax.ppermute(jnp.concatenate(done, axis=1), "seq", onward)
        carried = call(functools.partial(middle_kernel, distance), state, place, q, k_here, v_here, *carried, scalars=1)
    probs, scaled = call(
        functools.partial(last_scores_kernel, reaches[-1]),
        [((kv_local, rows, lanes), bf16), (block, f32)],
        place,
        q,
        k_now,
        *carried,
        scalars=1,
    )

    bounds = sorted({0, tile, tile * max(1, tiles - 2), width})
    chunks = list(zip(bounds[:-1], bounds[1:]))
    far_parts = parts - 2

    def parts_of(count, columns):
        return [((kept, columns[1] - columns[0]), bf16)] * count

    apart = (far_parts * kept) % 128 == 0 and (2 * kept) % 128 == 0
    first_rows = (far_parts if apart else parts) * kept
    att, *first_far = call(
        functools.partial(last_values_kernel, len(weights), chunks[0]),
        [((first_rows, depth), bf16)] + parts_of(far_parts, chunks[0]),
        probs,
        scaled,
        v_now,
        *weights,
    )
    arrived = []
    for index, columns in enumerate(chunks):
        far = first_far
        if index:
            kernel = functools.partial(project_kernel, len(weights), 0, columns)
            far = call(kernel, parts_of(far_parts, columns), att, *weights)
        here = []
        for step in range(1, chips):
            theirs, mine = far[2 * step - 2], far[2 * step - 1]
            got = swap(theirs)
            both = (mine.astype(f32) + got.astype(f32)).astype(bf16)
            here.append(ring(both, "head", step * CORES))
        arrived.append(here)
    whole = (0, width)
    shapes = parts_of(2, whole)
    if apart:
        kernel = functools.partial(near_kernel, len(weights), far_parts * kept, whole)
        att_near = [pltpu.VMEM((2 * kept, depth), bf16)]
        theirs, mine = call(kernel, shapes, probs, scaled, v_now, *weights, scratch=att_near)
    else:
        kernel = functools.partial(project_kernel, len(weights), far_parts * kept, whole)
        theirs, mine = call(kernel, shapes, att, *weights)
    got = swap(theirs)
    out = None
    for group in (range(len(chunks) - 1), range(len(chunks) - 1, len(chunks))):
        ranges = [chunks[i] for i in group]
        last = group.stop == len(chunks)
        out = write(
            functools.partial(finish_kernel, ranges, chips - 1, out is None),
            (part, width),
            [pltpu.VMEM((kept, c[1] - c[0]), bf16) for c in ranges] + [pltpu.SemaphoreType.DMA((len(ranges) + 1,))],
            out,
            place,
            mine,
            got,
            *[value for i in group for value in arrived[i]],
            *([own_rows, back] if moved and last else []),
            scalars=1,
        )
    return out


def solution(mesh):
    in_specs = (
        P(("grp", "seq"), "head"),
        P(("grp", "seq"), "head"),
        P(("grp", "seq"), "head"),
        P("head", None),
    )
    out_specs = P(("grp", "seq", "head"), None)

    return jax.shard_map(on_device, mesh=mesh, in_specs=in_specs, out_specs=out_specs, check_vma=False)
```

```python
import functools
import math

import jax
import jax.numpy as jnp
from jax import lax
from jax.experimental import pallas as pl
from jax.experimental.pallas import tpu as pltpu
from jax.sharding import PartitionSpec as P

QUERY_HEADS = 32
KEY_VALUE_HEADS = 16
HEAD_SIZE = 128
GROUP = QUERY_HEADS // KEY_VALUE_HEADS
CORES = 2

SCALE2 = 168.0**-0.5 * math.log2(math.e)


VMEM = pl.BlockSpec(memory_space=pltpu.VMEM)
SMEM = pl.BlockSpec(memory_space=pltpu.SMEM)


def in_vmem(value):
    return pltpu.with_memory_space_constraint(value, pltpu.VMEM)


def bring(source_ref, first, out_ref, sems):
    pieces = sems.shape[0]
    rows = out_ref.shape[0] // pieces
    copies = []
    for i in range(pieces):
        block = pl.ds(i * rows, rows)
        copies.append(
            pltpu.make_async_copy(source_ref.at[pl.ds(first + i * rows, rows)], out_ref.at[block], sems.at[i])
        )
        copies[-1].start()
    return copies


def loading(kernel, first, source_ref, *refs):
    copies = bring(source_ref, first, *refs[-2:])

    @pl.when(refs[0][0] >= 0)
    def _compute():
        kernel(*refs[:-2])

    for copy in copies:
        copy.wait()


def call(kernel, outs, *operands, scalars=0, load=None, scratch=()):
    operands = [value if i < scalars else in_vmem(value) for i, value in enumerate(operands)]
    specs = [SMEM] * scalars + [VMEM] * (len(operands) - scalars)
    outs = [pltpu.VMEM(shape, dtype) for shape, dtype in outs]
    scratch = list(scratch)
    if load is not None:
        source, first, count = load
        kernel = functools.partial(kernel, first)
        operands = [pltpu.with_memory_space_constraint(source, pltpu.HBM)] + operands
        specs = [pl.BlockSpec(memory_space=pltpu.HBM)] + specs
        outs.append(pltpu.VMEM((count, source.shape[1]), source.dtype))
        scratch.append(pltpu.SemaphoreType.DMA((4,)))
    return pl.pallas_call(
        kernel,
        in_specs=specs,
        out_specs=[VMEM] * len(outs),
        out_shape=outs,
        scratch_shapes=scratch,
        compiler_params=pltpu.CompilerParams(vmem_limit_bytes=20 << 20),
    )(*operands)


def stacked(q_ref, i):
    first = i * GROUP
    return jnp.concatenate(
        [q_ref[:, (first + g) * HEAD_SIZE : (first + g + 1) * HEAD_SIZE] for g in range(GROUP)], axis=0
    )


def head_of(ref, i):
    return ref[:, i * HEAD_SIZE : (i + 1) * HEAD_SIZE]


def scores_of(k, q):
    return lax.dot_general(k, q, (((1,), (1,)), ((), ())), preferred_element_type=jnp.float32) * SCALE2


def weigh(v, p):
    return lax.dot_general(v, p, (((0,), (0,)), ((), ())), preferred_element_type=jnp.float32)


def thirds(value):
    high = value.astype(jnp.bfloat16).astype(jnp.float32)
    middle = (value - high).astype(jnp.bfloat16).astype(jnp.float32)
    return [high, middle, value - high - middle]


LINES = HEAD_SIZE + 16
PACKED = LINES + HEAD_SIZE


def put_heads(att_ref, i, o):
    rows = att_ref.shape[0]
    o = o.T.astype(jnp.bfloat16)
    for g in range(GROUP):
        head = i * GROUP + g
        att_ref[:, head * HEAD_SIZE : (head + 1) * HEAD_SIZE] = o[g * rows : (g + 1) * rows]


def local_part(pos_ref, q_ref, k_ref, v_ref, i):
    s = scores_of(head_of(k_ref, i), stacked(q_ref, i))
    s = jnp.where(pos_ref[...] >= lax.broadcasted_iota(jnp.int32, s.shape, 0), s, -jnp.inf)
    top = jnp.max(s, axis=0, keepdims=True)
    p = jnp.exp2(s - top)
    return top, jnp.sum(p, axis=0, keepdims=True), weigh(head_of(v_ref, i), p.astype(jnp.bfloat16))


def local_kernel(place_ref, k_ref, v_ref, pos_ref, q_ref, top_ref, total_ref, o_ref):
    for i in range(o_ref.shape[0]):
        top_ref[i], total_ref[i], o_ref[i] = local_part(pos_ref, q_ref, k_ref, v_ref, i)


def moving_kernel(place_ref, k_ref, v_ref, pos_ref, q_ref, pack_ref, att_ref):
    for i in range(pack_ref.shape[0]):
        top, total, o = local_part(pos_ref, q_ref, k_ref, v_ref, i)
        pack_ref[i, 0:HEAD_SIZE] = o.astype(jnp.bfloat16)
        lines = thirds(top) + thirds(total)
        lines.append(jnp.zeros((LINES - HEAD_SIZE - len(lines), top.shape[1]), jnp.float32))
        pack_ref[i, HEAD_SIZE:LINES] = jnp.concatenate(lines, axis=0).astype(jnp.bfloat16)
        pack_ref[i, LINES:PACKED] = stacked(q_ref, i).astype(jnp.float32).T.astype(jnp.bfloat16)
        put_heads(att_ref, i, o * (1.0 / total))


def early_kernel(chips, distances, columns, place_ref, *refs):
    count = len(distances)
    k_refs, v_refs = refs[:count], refs[count : 2 * count]
    pack_ref, *weight_refs, att_ref, theirs_ref, mine_ref = refs[2 * count :]
    for i in range(pack_ref.shape[0]):
        q = pack_ref[i, LINES:PACKED]
        extra = pack_ref[i, HEAD_SIZE:LINES].astype(jnp.float32)
        top = extra[0:1] + extra[1:2] + extra[2:3]
        total = extra[3:4] + extra[4:5] + extra[5:6]
        parts = [
            jnp.dot(head_of(k_ref, i), q, preferred_element_type=jnp.float32) * SCALE2
            + jnp.where(place_ref[0] + 1 >= distance, 0.0, -jnp.inf)
            for distance, k_ref in zip(distances, k_refs)
        ]
        new_top = functools.reduce(jnp.maximum, [top] + [jnp.max(s, axis=0, keepdims=True) for s in parts])
        keep = jnp.exp2(top - new_top)
        total = total * keep
        o = pack_ref[i, 0:HEAD_SIZE].astype(jnp.float32) * keep
        for s, v_ref in zip(parts, v_refs):
            p = jnp.exp2(s - new_top)
            total = total + jnp.sum(p, axis=0, keepdims=True)
            o = o + weigh(head_of(v_ref, i), p.astype(jnp.bfloat16))
        put_heads(att_ref, i, o * (1.0 / total))
    put_pairs(chips, product_of(att_ref[...], weight_refs, columns), theirs_ref, mine_ref)


def product_of(att, weight_refs, columns):
    total, first = None, 0
    for weight_ref in weight_refs:
        last = first + weight_ref.shape[0]
        piece = jnp.dot(
            att[:, first:last], weight_ref[:, columns[0] : columns[1]], preferred_element_type=jnp.float32
        )
        total, first = piece if total is None else total + piece, last
    return total


def put_pairs(chips, product, theirs_ref, mine_ref):
    product = product.astype(jnp.bfloat16)
    part = product.shape[0] // (2 * chips)
    for chip in range(chips):
        block = slice(chip * part, (chip + 1) * part)
        theirs_ref[block, :] = product[2 * chip * part : (2 * chip + 1) * part]
        mine_ref[block, :] = product[(2 * chip + 1) * part : (2 * chip + 2) * part]


def own_kernel(chips, first, source_ref, place_ref, att_ref, top_ref, *refs):
    theirs_ref, mine_ref, rest_ref, total, sems = refs
    columns = (0, rest_ref.shape[1])
    copies = bring(source_ref, first, rest_ref, sems)

    @pl.when(place_ref[0] == 0)
    def _top():
        total[...] = product_of(att_ref[:, 0:first], [top_ref], columns)

    for copy in copies:
        copy.wait()

    @pl.when(place_ref[0] == 0)
    def _rest():
        rest = product_of(att_ref[:, first : att_ref.shape[1]], [rest_ref], columns)
        put_pairs(chips, total[...] + rest, theirs_ref, mine_ref)


def pairs_kernel(chips, columns, att_ref, *refs):
    *weight_refs, theirs_ref, mine_ref = refs
    put_pairs(chips, product_of(att_ref[...], weight_refs, columns), theirs_ref, mine_ref)


def seen(place_ref, distance):
    return jnp.where(place_ref[0] >= distance, 0.0, -jnp.inf).astype(jnp.float32)


def middle_kernel(distance, place_ref, q_ref, k_ref, v_ref, top_ref, total_ref, o_ref, top_out, total_out, o_out):
    for i in range(o_ref.shape[0]):
        s = scores_of(head_of(k_ref, i), stacked(q_ref, i)) + seen(place_ref, distance)
        old = top_ref[i]
        top = jnp.maximum(old, jnp.max(s, axis=0, keepdims=True))
        p = jnp.exp2(s - top)
        keep = jnp.exp2(old - top)
        top_out[i] = top
        total_out[i] = total_ref[i] * keep + jnp.sum(p, axis=0, keepdims=True)
        o_out[i] = o_ref[i] * keep + weigh(head_of(v_ref, i), p.astype(jnp.bfloat16))


def last_scores_kernel(distance, place_ref, q_ref, k_ref, top_ref, total_ref, o_ref, w_out, o_out):
    for i in range(o_ref.shape[0]):
        s = scores_of(head_of(k_ref, i), stacked(q_ref, i)) + seen(place_ref, distance)
        old = top_ref[i]
        top = jnp.maximum(old, jnp.max(s, axis=0, keepdims=True))
        p = jnp.exp2(s - top)
        keep = jnp.exp2(old - top)
        inverse = 1.0 / (total_ref[i] * keep + jnp.sum(p, axis=0, keepdims=True))
        w_out[i] = (p * inverse).astype(jnp.bfloat16)
        o_out[i] = o_ref[i] * (keep * inverse)


def put_product(att, weight_refs, columns, out_refs):
    product = product_of(att, weight_refs, columns)
    part = out_refs[0].shape[0]
    for i, out_ref in enumerate(out_refs):
        out_ref[...] = product[i * part : (i + 1) * part].astype(jnp.bfloat16)


def put_values(att_ref, first, w_ref, o_ref, v_ref):
    rows, every = att_ref.shape[0], o_ref.shape[2] // GROUP
    spans = [slice(g * every + first, g * every + first + rows) for g in range(GROUP)]
    for i in range(o_ref.shape[0]):
        w = jnp.concatenate([w_ref[i, :, span] for span in spans], axis=1)
        o = jnp.concatenate([o_ref[i, :, span] for span in spans], axis=1)
        put_heads(att_ref, i, o + weigh(head_of(v_ref, i), w))


def last_values_kernel(pieces, columns, w_ref, o_ref, v_ref, *refs):
    weight_refs, (att_ref, *out_refs) = refs[:pieces], refs[pieces:]
    put_values(att_ref, 0, w_ref, o_ref, v_ref)
    far = len(out_refs) * out_refs[0].shape[0]
    put_product(att_ref[0:far, :], weight_refs, columns, out_refs)


def near_kernel(pieces, first, columns, w_ref, o_ref, v_ref, *refs):
    weight_refs, (theirs_ref, mine_ref, att_ref) = refs[:pieces], refs[pieces:]
    put_values(att_ref, first, w_ref, o_ref, v_ref)
    put_product(att_ref[...], weight_refs, columns, [theirs_ref, mine_ref])


def project_kernel(pieces, first, columns, att_ref, *refs):
    weight_refs, out_refs = refs[:pieces], refs[pieces:]
    count = len(out_refs) * out_refs[0].shape[0]
    put_product(att_ref[first : first + count, :], weight_refs, columns, out_refs)


def finish_kernel(ranges, steps, first, mine_ref, got_ref, *refs):
    far_refs, refs = refs[: len(ranges) * steps], list(refs[len(ranges) * steps :])
    sem, staged = refs.pop(), [refs.pop() for _ in ranges][::-1]
    out_ref = refs.pop()
    if not first:
        refs.pop()
    copies = []
    for index, columns in enumerate(ranges):
        span = slice(columns[0], columns[1])
        total = mine_ref[:, span].astype(jnp.float32) + got_ref[:, span].astype(jnp.float32)
        for far_ref in far_refs[index * steps : (index + 1) * steps]:
            total = total + far_ref[...].astype(jnp.float32)
        staged[index][...] = total.astype(jnp.bfloat16)
        copies.append(
            pltpu.make_async_copy(staged[index], out_ref.at[0 : mine_ref.shape[0], span], sem.at[index])
        )
        copies[-1].start()
    for copy in copies:
        copy.wait()


def place_moved_kernel(place_ref, own_ref, back_ref, _, out_ref, sem):
    target = out_ref.at[out_ref.shape[0] - own_ref.shape[0] : out_ref.shape[0]]

    @pl.when(place_ref[0] == 0)
    def _own():
        copy = pltpu.make_async_copy(own_ref, target, sem)
        copy.start()
        copy.wait()

    @pl.when(place_ref[0] != 0)
    def _back():
        copy = pltpu.make_async_copy(back_ref, target, sem)
        copy.start()
        copy.wait()


def write(kernel, out_shape, scratch, out, *operands, scalars=0):
    operands = [value if i < scalars else in_vmem(value) for i, value in enumerate(operands)]
    specs = [SMEM] * scalars + [VMEM] * (len(operands) - scalars)
    aliases = {}
    if out is not None:
        aliases = {len(operands): 0}
        operands.append(out)
        specs.append(pl.BlockSpec(memory_space=pltpu.HBM))
    return pl.pallas_call(
        kernel,
        in_specs=specs,
        out_specs=pl.BlockSpec(memory_space=pltpu.HBM),
        out_shape=jax.ShapeDtypeStruct(out_shape, jnp.bfloat16),
        scratch_shapes=scratch,
        input_output_aliases=aliases,
        compiler_params=pltpu.CompilerParams(vmem_limit_bytes=8 << 20),
    )(*operands)


def ring(value, axis, distance):
    count = lax.axis_size(axis)
    return lax.ppermute(value, axis, [(s, (s + distance) % count) for s in range(count)])


def pass_on(value, distance):
    count = lax.axis_size("seq")
    return lax.ppermute(value, "seq", [(s, s + distance) for s in range(distance, count - distance)])


def swap(value):
    count = lax.axis_size("head")
    return lax.ppermute(value, "head", [(h, h ^ 1) for h in range(count)])


def tile_of(width):
    return max(t for t in range(128, 1024, 128) if width % t == 0 and (t % 256 == 0 or width % 256))


def on_device(queries, keys, values, out_weight):
    rows, depth = queries.shape
    width = out_weight.shape[1]
    heads = lax.axis_size("head")
    seq_count = lax.axis_size("seq")
    place = lax.axis_index("seq").astype(jnp.int32)[None]
    me = lax.axis_index("head")
    chips = heads // CORES
    part = rows // heads
    kv_local = keys.shape[1] // HEAD_SIZE
    reaches = [1 << level for level in range(seq_count.bit_length() - 1)]
    f32, bf16 = jnp.float32, jnp.bfloat16

    moved = part // 3 if reaches == [1, 2] and part % 48 == 0 else 0
    kept = part - moved
    parts = 2 * chips

    onward = [(s, s + 1) for s in range(seq_count - 1)]
    k_now, v_now = ring(keys, "seq", 1), lax.ppermute(values, "seq", onward)

    chip, core = me // CORES, me % CORES
    owners = []
    for step in range(1, chips + 1):
        base = ((chip + step) % chips) * CORES
        owners += [base + 1 - core, base + core]

    def rows_from(first, count):
        starts = [owner * part + first for owner in owners]
        q = jnp.concatenate([lax.dynamic_slice_in_dim(queries, start, count, 0) for start in starts], axis=0)
        pos = jnp.concatenate([start + jnp.arange(count, dtype=jnp.int32) for start in starts])
        return jnp.concatenate([pos] * GROUP)[None], in_vmem(q)

    if moved:
        pack, att_own = call(
            moving_kernel,
            [((kv_local, PACKED, GROUP * moved * parts), bf16), ((moved * parts, depth), bf16)],
            place,
            keys,
            values,
            *rows_from(kept, moved),
            scalars=1,
        )
        pack = lax.ppermute(pack, "seq", [(s, s - 1) for s in range(1, seq_count)])
    lanes = GROUP * kept * parts
    line, block = (kv_local, 1, lanes), (kv_local, HEAD_SIZE, lanes)
    state = [(line, f32), (line, f32), (block, f32)]
    pos, q = rows_from(0, kept)
    count = 5 * depth // 8 if moved else depth
    kernel = functools.partial(loading, local_kernel)
    *carried, top = call(kernel, state, place, keys, values, pos, q, scalars=1, load=(out_weight, 0, count))
    weights = [top]
    if moved:
        pair_outs = [((moved * chips, width), bf16)] * 2
        kernel = functools.partial(own_kernel, chips)
        *own_parts, rest = call(
            kernel,
            pair_outs,
            place,
            att_own,
            top,
            scalars=1,
            load=(out_weight, count, depth - count),
            scratch=[pltpu.VMEM((moved * parts, width), f32)],
        )
        weights.append(rest)

    def settle(theirs, mine, everywhere):
        axes = "head" if everywhere else ("seq", "head")
        got = swap(theirs)
        both = mine.astype(f32) + got.astype(f32)
        total = both[(chips - 1) * moved :]
        for step in range(1, chips):
            piece = both[(step - 1) * moved : step * moved].astype(bf16)
            moves = [(h, (h + step * CORES) % heads) for h in range(heads)]
            total = total + lax.ppermute(piece, axes, moves).astype(f32)
        return total.astype(bf16)

    if moved:
        own_rows = settle(*own_parts, False)

    tile = tile_of(width)
    tiles = width // tile
    back = None
    for distance in reaches[:-1]:
        k_here, v_here = k_now, v_now
        k_now = pass_on(k_here, distance)
        v_now = pass_on(v_here, distance)
        if moved:
            border = tile * max(1, tiles // 3)
            halves = [(0, border), (border, width)]
            shapes = [[((moved * chips, c[1] - c[0]), bf16)] * 2 for c in halves]
            att_moved, *early_parts = call(
                functools.partial(early_kernel, chips, reaches, halves[0]),
                [((moved * parts, depth), bf16)] + shapes[0],
                place,
                keys,
                k_here,
                values,
                v_here,
                pack,
                *weights,
                scalars=1,
            )
            late_parts = call(functools.partial(pairs_kernel, chips, halves[1]), shapes[1], att_moved, *weights)
            done = [settle(*early_parts, True), settle(*late_parts, True)]
            back = lax.ppermute(jnp.concatenate(done, axis=1), "seq", onward)
        carried = call(functools.partial(middle_kernel, distance), state, place, q, k_here, v_here, *carried, scalars=1)
    probs, scaled = call(
        functools.partial(last_scores_kernel, reaches[-1]),
        [((kv_local, rows, lanes), bf16), (block, f32)],
        place,
        q,
        k_now,
        *carried,
        scalars=1,
    )

    bounds = sorted({0, tile, tile * max(1, tiles - 2), width})
    chunks = list(zip(bounds[:-1], bounds[1:]))
    far_parts = parts - 2

    def parts_of(count, columns):
        return [((kept, columns[1] - columns[0]), bf16)] * count

    apart = (far_parts * kept) % 128 == 0 and (2 * kept) % 128 == 0
    first_rows = (far_parts if apart else parts) * kept
    att, *first_far = call(
        functools.partial(last_values_kernel, len(weights), chunks[0]),
        [((first_rows, depth), bf16)] + parts_of(far_parts, chunks[0]),
        probs,
        scaled,
        v_now,
        *weights,
    )
    arrived = []
    for index, columns in enumerate(chunks):
        far = first_far
        if index:
            kernel = functools.partial(project_kernel, len(weights), 0, columns)
            far = call(kernel, parts_of(far_parts, columns), att, *weights)
        here = []
        for step in range(1, chips):
            theirs, mine = far[2 * step - 2], far[2 * step - 1]
            got = swap(theirs)
            both = (mine.astype(f32) + got.astype(f32)).astype(bf16)
            here.append(ring(both, "head", step * CORES))
        arrived.append(here)
    whole = (0, width)
    shapes = parts_of(2, whole)
    if apart:
        kernel = functools.partial(near_kernel, len(weights), far_parts * kept, whole)
        att_near = [pltpu.VMEM((2 * kept, depth), bf16)]
        theirs, mine = call(kernel, shapes, probs, scaled, v_now, *weights, scratch=att_near)
    else:
        kernel = functools.partial(project_kernel, len(weights), far_parts * kept, whole)
        theirs, mine = call(kernel, shapes, att, *weights)
    got = swap(theirs)
    out = None
    for group in (range(len(chunks) - 1), range(len(chunks) - 1, len(chunks))):
        ranges = [chunks[i] for i in group]
        if moved and out is not None:
            sem = [pltpu.SemaphoreType.DMA]
            out = write(place_moved_kernel, (part, width), sem, out, place, own_rows, back, scalars=1)
        out = write(
            functools.partial(finish_kernel, ranges, chips - 1, out is None),
            (part, width),
            [pltpu.VMEM((kept, c[1] - c[0]), bf16) for c in ranges] + [pltpu.SemaphoreType.DMA((len(ranges),))],
            out,
            mine,
            got,
            *[value for i in group for value in arrived[i]],
        )
    return out


def solution(mesh):
    in_specs = (
        P(("grp", "seq"), "head"),
        P(("grp", "seq"), "head"),
        P(("grp", "seq"), "head"),
        P("head", None),
    )
    out_specs = P(("grp", "seq", "head"), None)

    return jax.shard_map(on_device, mesh=mesh, in_specs=in_specs, out_specs=out_specs, check_vma=False)
```

```python
import functools
import math

import jax
import jax.numpy as jnp
from jax import lax
from jax.experimental import pallas as pl
from jax.experimental.pallas import tpu as pltpu
from jax.sharding import PartitionSpec as P

QUERY_HEADS = 32
KEY_VALUE_HEADS = 16
HEAD_SIZE = 128
GROUP = QUERY_HEADS // KEY_VALUE_HEADS
CORES = 2

SCALE2 = 168.0**-0.5 * math.log2(math.e)


VMEM = pl.BlockSpec(memory_space=pltpu.VMEM)
SMEM = pl.BlockSpec(memory_space=pltpu.SMEM)


def in_vmem(value):
    return pltpu.with_memory_space_constraint(value, pltpu.VMEM)


def bring(source_ref, first, out_ref, sems):
    pieces = sems.shape[0]
    rows = out_ref.shape[0] // pieces
    copies = []
    for i in range(pieces):
        block = pl.ds(i * rows, rows)
        copies.append(
            pltpu.make_async_copy(source_ref.at[pl.ds(first + i * rows, rows)], out_ref.at[block], sems.at[i])
        )
        copies[-1].start()
    return copies


def loading(kernel, first, source_ref, *refs):
    copies = bring(source_ref, first, *refs[-2:])

    @pl.when(refs[0][0] >= 0)
    def _compute():
        kernel(*refs[:-2])

    for copy in copies:
        copy.wait()


def call(kernel, outs, *operands, scalars=0, load=None, scratch=()):
    operands = [value if i < scalars else in_vmem(value) for i, value in enumerate(operands)]
    specs = [SMEM] * scalars + [VMEM] * (len(operands) - scalars)
    outs = [pltpu.VMEM(shape, dtype) for shape, dtype in outs]
    scratch = list(scratch)
    if load is not None:
        source, first, count = load
        kernel = functools.partial(kernel, first)
        operands = [pltpu.with_memory_space_constraint(source, pltpu.HBM)] + operands
        specs = [pl.BlockSpec(memory_space=pltpu.HBM)] + specs
        outs.append(pltpu.VMEM((count, source.shape[1]), source.dtype))
        scratch.append(pltpu.SemaphoreType.DMA((4,)))
    return pl.pallas_call(
        kernel,
        in_specs=specs,
        out_specs=[VMEM] * len(outs),
        out_shape=outs,
        scratch_shapes=scratch,
        compiler_params=pltpu.CompilerParams(vmem_limit_bytes=20 << 20),
    )(*operands)


def stacked(q_ref, i):
    first = i * GROUP
    return jnp.concatenate(
        [q_ref[:, (first + g) * HEAD_SIZE : (first + g + 1) * HEAD_SIZE] for g in range(GROUP)], axis=0
    )


def head_of(ref, i):
    return ref[:, i * HEAD_SIZE : (i + 1) * HEAD_SIZE]


def scores_of(k, q):
    return lax.dot_general(k, q, (((1,), (1,)), ((), ())), preferred_element_type=jnp.float32) * SCALE2


def weigh(v, p):
    return lax.dot_general(v, p, (((0,), (0,)), ((), ())), preferred_element_type=jnp.float32)


def thirds(value):
    high = value.astype(jnp.bfloat16).astype(jnp.float32)
    middle = (value - high).astype(jnp.bfloat16).astype(jnp.float32)
    return [high, middle, value - high - middle]


LINES = HEAD_SIZE + 16
PACKED = LINES + HEAD_SIZE


def put_heads(att_ref, i, o):
    rows = att_ref.shape[0]
    o = o.T.astype(jnp.bfloat16)
    for g in range(GROUP):
        head = i * GROUP + g
        att_ref[:, head * HEAD_SIZE : (head + 1) * HEAD_SIZE] = o[g * rows : (g + 1) * rows]


def local_part(pos_ref, q_ref, k_ref, v_ref, i):
    s = scores_of(head_of(k_ref, i), stacked(q_ref, i))
    s = jnp.where(pos_ref[...] >= lax.broadcasted_iota(jnp.int32, s.shape, 0), s, -jnp.inf)
    top = jnp.max(s, axis=0, keepdims=True)
    p = jnp.exp2(s - top)
    return top, jnp.sum(p, axis=0, keepdims=True), weigh(head_of(v_ref, i), p.astype(jnp.bfloat16))


def local_kernel(place_ref, k_ref, v_ref, pos_ref, q_ref, top_ref, total_ref, o_ref):
    for i in range(o_ref.shape[0]):
        top_ref[i], total_ref[i], o_ref[i] = local_part(pos_ref, q_ref, k_ref, v_ref, i)


def moving_kernel(k_ref, v_ref, pos_ref, q_ref, pack_ref, att_ref):
    for i in range(pack_ref.shape[0]):
        top, total, o = local_part(pos_ref, q_ref, k_ref, v_ref, i)
        pack_ref[i, 0:HEAD_SIZE] = o.astype(jnp.bfloat16)
        lines = thirds(top) + thirds(total)
        lines.append(jnp.zeros((LINES - HEAD_SIZE - len(lines), top.shape[1]), jnp.float32))
        pack_ref[i, HEAD_SIZE:LINES] = jnp.concatenate(lines, axis=0).astype(jnp.bfloat16)
        pack_ref[i, LINES:PACKED] = stacked(q_ref, i).astype(jnp.float32).T.astype(jnp.bfloat16)
        put_heads(att_ref, i, o * (1.0 / total))


def early_kernel(chips, distances, columns, place_ref, *refs):
    count = len(distances)
    k_refs, v_refs = refs[:count], refs[count : 2 * count]
    pack_ref, *weight_refs, att_ref, theirs_ref, mine_ref = refs[2 * count :]
    for i in range(pack_ref.shape[0]):
        q = pack_ref[i, LINES:PACKED]
        extra = pack_ref[i, HEAD_SIZE:LINES].astype(jnp.float32)
        top = extra[0:1] + extra[1:2] + extra[2:3]
        total = extra[3:4] + extra[4:5] + extra[5:6]
        parts = [
            jnp.dot(head_of(k_ref, i), q, preferred_element_type=jnp.float32) * SCALE2
            + jnp.where(place_ref[0] + 1 >= distance, 0.0, -jnp.inf)
            for distance, k_ref in zip(distances, k_refs)
        ]
        new_top = functools.reduce(jnp.maximum, [top] + [jnp.max(s, axis=0, keepdims=True) for s in parts])
        keep = jnp.exp2(top - new_top)
        total = total * keep
        o = pack_ref[i, 0:HEAD_SIZE].astype(jnp.float32) * keep
        for s, v_ref in zip(parts, v_refs):
            p = jnp.exp2(s - new_top)
            total = total + jnp.sum(p, axis=0, keepdims=True)
            o = o + weigh(head_of(v_ref, i), p.astype(jnp.bfloat16))
        put_heads(att_ref, i, o * (1.0 / total))
    put_pairs(chips, product_of(att_ref[...], weight_refs, columns), theirs_ref, mine_ref)


def product_of(att, weight_refs, columns):
    total, first = None, 0
    for weight_ref in weight_refs:
        last = first + weight_ref.shape[0]
        piece = jnp.dot(
            att[:, first:last], weight_ref[:, columns[0] : columns[1]], preferred_element_type=jnp.float32
        )
        total, first = piece if total is None else total + piece, last
    return total


def put_pairs(chips, product, theirs_ref, mine_ref):
    product = product.astype(jnp.bfloat16)
    part = product.shape[0] // (2 * chips)
    for chip in range(chips):
        block = slice(chip * part, (chip + 1) * part)
        theirs_ref[block, :] = product[2 * chip * part : (2 * chip + 1) * part]
        mine_ref[block, :] = product[(2 * chip + 1) * part : (2 * chip + 2) * part]


def own_kernel(chips, first, source_ref, place_ref, att_ref, _, theirs_ref, mine_ref, weight_ref, total, sems):
    columns = (0, weight_ref.shape[1])
    copies = bring(source_ref, first, weight_ref, sems)
    rows = weight_ref.shape[0] // len(copies)
    for i, copy in enumerate(copies):
        copy.wait()

        @pl.when(place_ref[0] == 0)
        def _project():
            block = slice(i * rows, (i + 1) * rows)
            piece = product_of(att_ref[:, block], [weight_ref.at[block, :]], columns)
            if i:
                piece = piece + total[...]
            if i + 1 < len(copies):
                total[...] = piece
            else:
                put_pairs(chips, piece, theirs_ref, mine_ref)


def pairs_kernel(chips, columns, att_ref, *refs):
    *weight_refs, theirs_ref, mine_ref = refs
    put_pairs(chips, product_of(att_ref[...], weight_refs, columns), theirs_ref, mine_ref)


def seen(place_ref, distance):
    return jnp.where(place_ref[0] >= distance, 0.0, -jnp.inf).astype(jnp.float32)


def middle_kernel(distance, place_ref, q_ref, k_ref, v_ref, top_ref, total_ref, o_ref, top_out, total_out, o_out):
    for i in range(o_ref.shape[0]):
        s = scores_of(head_of(k_ref, i), stacked(q_ref, i)) + seen(place_ref, distance)
        old = top_ref[i]
        top = jnp.maximum(old, jnp.max(s, axis=0, keepdims=True))
        p = jnp.exp2(s - top)
        keep = jnp.exp2(old - top)
        top_out[i] = top
        total_out[i] = total_ref[i] * keep + jnp.sum(p, axis=0, keepdims=True)
        o_out[i] = o_ref[i] * keep + weigh(head_of(v_ref, i), p.astype(jnp.bfloat16))


def last_scores_kernel(distance, place_ref, q_ref, k_ref, top_ref, total_ref, o_ref, w_out, o_out):
    for i in range(o_ref.shape[0]):
        s = scores_of(head_of(k_ref, i), stacked(q_ref, i)) + seen(place_ref, distance)
        old = top_ref[i]
        top = jnp.maximum(old, jnp.max(s, axis=0, keepdims=True))
        p = jnp.exp2(s - top)
        keep = jnp.exp2(old - top)
        inverse = 1.0 / (total_ref[i] * keep + jnp.sum(p, axis=0, keepdims=True))
        w_out[i] = (p * inverse).astype(jnp.bfloat16)
        o_out[i] = o_ref[i] * (keep * inverse)


def put_product(att, weight_refs, columns, out_refs):
    product = product_of(att, weight_refs, columns)
    part = out_refs[0].shape[0]
    for i, out_ref in enumerate(out_refs):
        out_ref[...] = product[i * part : (i + 1) * part].astype(jnp.bfloat16)


def put_values(att_ref, first, w_ref, o_ref, v_ref):
    rows, every = att_ref.shape[0], o_ref.shape[2] // GROUP
    spans = [slice(g * every + first, g * every + first + rows) for g in range(GROUP)]
    for i in range(o_ref.shape[0]):
        w = jnp.concatenate([w_ref[i, :, span] for span in spans], axis=1)
        o = jnp.concatenate([o_ref[i, :, span] for span in spans], axis=1)
        put_heads(att_ref, i, o + weigh(head_of(v_ref, i), w))


def last_values_kernel(pieces, columns, w_ref, o_ref, v_ref, *refs):
    weight_refs, (att_ref, *out_refs) = refs[:pieces], refs[pieces:]
    put_values(att_ref, 0, w_ref, o_ref, v_ref)
    far = len(out_refs) * out_refs[0].shape[0]
    put_product(att_ref[0:far, :], weight_refs, columns, out_refs)


def near_kernel(pieces, first, columns, w_ref, o_ref, v_ref, *refs):
    weight_refs, (theirs_ref, mine_ref, att_ref) = refs[:pieces], refs[pieces:]
    put_values(att_ref, first, w_ref, o_ref, v_ref)
    put_product(att_ref[...], weight_refs, columns, [theirs_ref, mine_ref])


def project_kernel(pieces, first, columns, att_ref, *refs):
    weight_refs, out_refs = refs[:pieces], refs[pieces:]
    count = len(out_refs) * out_refs[0].shape[0]
    put_product(att_ref[first : first + count, :], weight_refs, columns, out_refs)


def finish_kernel(ranges, steps, first, place_ref, mine_ref, got_ref, *refs):
    far_refs, refs = refs[: len(ranges) * steps], list(refs[len(ranges) * steps :])
    sem, staged = refs.pop(), [refs.pop() for _ in ranges][::-1]
    out_ref = refs.pop()
    if not first:
        refs.pop()
    target = None
    if refs:
        own_ref, back_ref = refs
        target = out_ref.at[out_ref.shape[0] - own_ref.shape[0] : out_ref.shape[0]]

        @pl.when(place_ref[0] == 0)
        def _own():
            pltpu.make_async_copy(own_ref, target, sem.at[len(ranges)]).start()

        @pl.when(place_ref[0] != 0)
        def _back():
            pltpu.make_async_copy(back_ref, target, sem.at[len(ranges)]).start()

    copies = []
    for index, columns in enumerate(ranges):
        span = slice(columns[0], columns[1])
        total = mine_ref[:, span].astype(jnp.float32) + got_ref[:, span].astype(jnp.float32)
        for far_ref in far_refs[index * steps : (index + 1) * steps]:
            total = total + far_ref[...].astype(jnp.float32)
        staged[index][...] = total.astype(jnp.bfloat16)
        copies.append(
            pltpu.make_async_copy(staged[index], out_ref.at[0 : mine_ref.shape[0], span], sem.at[index])
        )
        copies[-1].start()
    for copy in copies:
        copy.wait()
    if target is not None:
        pltpu.make_async_copy(back_ref, target, sem.at[len(ranges)]).wait()


def write(kernel, out_shape, scratch, out, *operands, scalars=0):
    operands = [value if i < scalars else in_vmem(value) for i, value in enumerate(operands)]
    specs = [SMEM] * scalars + [VMEM] * (len(operands) - scalars)
    aliases = {}
    if out is not None:
        aliases = {len(operands): 0}
        operands.append(out)
        specs.append(pl.BlockSpec(memory_space=pltpu.HBM))
    return pl.pallas_call(
        kernel,
        in_specs=specs,
        out_specs=pl.BlockSpec(memory_space=pltpu.HBM),
        out_shape=jax.ShapeDtypeStruct(out_shape, jnp.bfloat16),
        scratch_shapes=scratch,
        input_output_aliases=aliases,
        compiler_params=pltpu.CompilerParams(vmem_limit_bytes=8 << 20),
    )(*operands)


def ring(value, axis, distance):
    count = lax.axis_size(axis)
    return lax.ppermute(value, axis, [(s, (s + distance) % count) for s in range(count)])


def pass_on(value, distance):
    count = lax.axis_size("seq")
    return lax.ppermute(value, "seq", [(s, s + distance) for s in range(distance, count - distance)])


def swap(value):
    count = lax.axis_size("head")
    return lax.ppermute(value, "head", [(h, h ^ 1) for h in range(count)])


def tile_of(width):
    return max(t for t in range(128, 1024, 128) if width % t == 0 and (t % 256 == 0 or width % 256))


def on_device(queries, keys, values, out_weight):
    rows, depth = queries.shape
    width = out_weight.shape[1]
    heads = lax.axis_size("head")
    seq_count = lax.axis_size("seq")
    place = lax.axis_index("seq").astype(jnp.int32)[None]
    me = lax.axis_index("head")
    chips = heads // CORES
    part = rows // heads
    kv_local = keys.shape[1] // HEAD_SIZE
    reaches = [1 << level for level in range(seq_count.bit_length() - 1)]
    f32, bf16 = jnp.float32, jnp.bfloat16

    moved = part // 3 if reaches == [1, 2] and part % 48 == 0 else 0
    kept = part - moved
    parts = 2 * chips

    onward = [(s, s + 1) for s in range(seq_count - 1)]
    k_now, v_now = ring(keys, "seq", 1), lax.ppermute(values, "seq", onward)

    chip, core = me // CORES, me % CORES
    owners = []
    for step in range(1, chips + 1):
        base = ((chip + step) % chips) * CORES
        owners += [base + 1 - core, base + core]
    owners = [owner.astype(jnp.uint32) for owner in owners]

    def rows_from(first, count):
        starts = [owner * part + first for owner in owners]
        q = jnp.concatenate([lax.dynamic_slice_in_dim(queries, start, count, 0) for start in starts], axis=0)
        pos = jnp.concatenate([start.astype(jnp.int32) + jnp.arange(count, dtype=jnp.int32) for start in starts])
        return jnp.concatenate([pos] * GROUP)[None], in_vmem(q)

    pos, q = rows_from(0, kept)
    if moved:
        pack, att_own = call(
            moving_kernel,
            [((kv_local, PACKED, GROUP * moved * parts), bf16), ((moved * parts, depth), bf16)],
            keys,
            values,
            *rows_from(kept, moved),
        )
        pack = lax.ppermute(pack, "seq", [(s, s - 1) for s in range(1, seq_count)])
        pair_outs = [((moved * chips, width), bf16)] * 2
        *own_parts, weight = call(
            functools.partial(own_kernel, chips),
            pair_outs,
            place,
            att_own,
            pos,
            scalars=1,
            load=(out_weight, 0, depth),
            scratch=[pltpu.VMEM((moved * parts, width), f32)],
        )
    lanes = GROUP * kept * parts
    line, block = (kv_local, 1, lanes), (kv_local, HEAD_SIZE, lanes)
    state = [(line, f32), (line, f32), (block, f32)]
    if moved:
        carried = call(local_kernel, state, place, keys, values, pos, q, scalars=1)
    else:
        kernel = functools.partial(loading, local_kernel)
        load = (out_weight, 0, depth)
        *carried, weight = call(kernel, state, place, keys, values, pos, q, scalars=1, load=load)
    weights = [weight]

    def settle(theirs, mine, everywhere):
        axes = "head" if everywhere else ("seq", "head")
        got = swap(theirs)
        both = mine.astype(f32) + got.astype(f32)
        total = both[(chips - 1) * moved :]
        for step in range(1, chips):
            piece = both[(step - 1) * moved : step * moved].astype(bf16)
            moves = [(h, (h + step * CORES) % heads) for h in range(heads)]
            total = total + lax.ppermute(piece, axes, moves).astype(f32)
        return total.astype(bf16)

    if moved:
        own_rows = settle(*own_parts, False)

    tile = tile_of(width)
    tiles = width // tile
    back = None
    for distance in reaches[:-1]:
        k_here, v_here = k_now, v_now
        k_now = pass_on(k_here, distance)
        v_now = pass_on(v_here, distance)
        if moved:
            border = tile * (tiles // 2)
            halves = [(0, border), (border, width)]
            shapes = [[((moved * chips, c[1] - c[0]), bf16)] * 2 for c in halves]
            att_moved, *early_parts = call(
                functools.partial(early_kernel, chips, reaches, halves[0]),
                [((moved * parts, depth), bf16)] + shapes[0],
                place,
                keys,
                k_here,
                values,
                v_here,
                pack,
                *weights,
                scalars=1,
            )
            late_parts = call(functools.partial(pairs_kernel, chips, halves[1]), shapes[1], att_moved, *weights)
            done = [settle(*early_parts, True), settle(*late_parts, True)]
            back = lax.ppermute(jnp.concatenate(done, axis=1), "seq", onward)
        carried = call(functools.partial(middle_kernel, distance), state, place, q, k_here, v_here, *carried, scalars=1)
    probs, scaled = call(
        functools.partial(last_scores_kernel, reaches[-1]),
        [((kv_local, rows, lanes), bf16), (block, f32)],
        place,
        q,
        k_now,
        *carried,
        scalars=1,
    )

    bounds = sorted({0, tile, tile * max(1, tiles - 2), width})
    chunks = list(zip(bounds[:-1], bounds[1:]))
    far_parts = parts - 2

    def parts_of(count, columns):
        return [((kept, columns[1] - columns[0]), bf16)] * count

    apart = (far_parts * kept) % 128 == 0 and (2 * kept) % 128 == 0
    first_rows = (far_parts if apart else parts) * kept
    att, *first_far = call(
        functools.partial(last_values_kernel, len(weights), chunks[0]),
        [((first_rows, depth), bf16)] + parts_of(far_parts, chunks[0]),
        probs,
        scaled,
        v_now,
        *weights,
    )
    arrived = []
    for index, columns in enumerate(chunks):
        far = first_far
        if index:
            kernel = functools.partial(project_kernel, len(weights), 0, columns)
            far = call(kernel, parts_of(far_parts, columns), att, *weights)
        here = []
        for step in range(1, chips):
            theirs, mine = far[2 * step - 2], far[2 * step - 1]
            got = swap(theirs)
            both = (mine.astype(f32) + got.astype(f32)).astype(bf16)
            here.append(ring(both, "head", step * CORES))
        arrived.append(here)
    whole = (0, width)
    shapes = parts_of(2, whole)
    if apart:
        kernel = functools.partial(near_kernel, len(weights), far_parts * kept, whole)
        att_near = [pltpu.VMEM((2 * kept, depth), bf16)]
        theirs, mine = call(kernel, shapes, probs, scaled, v_now, *weights, scratch=att_near)
    else:
        kernel = functools.partial(project_kernel, len(weights), far_parts * kept, whole)
        theirs, mine = call(kernel, shapes, att, *weights)
    got = swap(theirs)
    out = None
    for group in (range(len(chunks) - 1), range(len(chunks) - 1, len(chunks))):
        ranges = [chunks[i] for i in group]
        last = group.stop == len(chunks)
        out = write(
            functools.partial(finish_kernel, ranges, chips - 1, out is None),
            (part, width),
            [pltpu.VMEM((kept, c[1] - c[0]), bf16) for c in ranges] + [pltpu.SemaphoreType.DMA((len(ranges) + 1,))],
            out,
            place,
            mine,
            got,
            *[value for i in group for value in arrived[i]],
            *([own_rows, back] if moved and last else []),
            scalars=1,
        )
    return out


def solution(mesh):
    in_specs = (
        P(("grp", "seq"), "head"),
        P(("grp", "seq"), "head"),
        P(("grp", "seq"), "head"),
        P("head", None),
    )
    out_specs = P(("grp", "seq", "head"), None)

    return jax.shard_map(on_device, mesh=mesh, in_specs=in_specs, out_specs=out_specs, check_vma=False)
```

```python
import functools
import math

import jax
import jax.numpy as jnp
from jax import lax
from jax.experimental import pallas as pl
from jax.experimental.pallas import tpu as pltpu
from jax.sharding import PartitionSpec as P

QUERY_HEADS = 32
KEY_VALUE_HEADS = 16
HEAD_SIZE = 128
GROUP = QUERY_HEADS // KEY_VALUE_HEADS
CORES = 2

SCALE2 = 168.0**-0.5 * math.log2(math.e)


VMEM = pl.BlockSpec(memory_space=pltpu.VMEM)
SMEM = pl.BlockSpec(memory_space=pltpu.SMEM)


def in_vmem(value):
    return pltpu.with_memory_space_constraint(value, pltpu.VMEM)


def bring(source_ref, first, out_ref, sems):
    pieces = sems.shape[0]
    rows = out_ref.shape[0] // pieces
    copies = []
    for i in range(pieces):
        block = pl.ds(i * rows, rows)
        copies.append(
            pltpu.make_async_copy(source_ref.at[pl.ds(first + i * rows, rows)], out_ref.at[block], sems.at[i])
        )
        copies[-1].start()
    return copies


def loading(kernel, first, source_ref, *refs):
    copies = bring(source_ref, first, *refs[-2:])

    @pl.when(refs[0][0] >= 0)
    def _compute():
        kernel(*refs[:-2])

    for copy in copies:
        copy.wait()


def call(kernel, outs, *operands, scalars=0, load=None, scratch=()):
    operands = [value if i < scalars else in_vmem(value) for i, value in enumerate(operands)]
    specs = [SMEM] * scalars + [VMEM] * (len(operands) - scalars)
    outs = [pltpu.VMEM(shape, dtype) for shape, dtype in outs]
    scratch = list(scratch)
    if load is not None:
        source, first, count = load
        kernel = functools.partial(kernel, first)
        operands = [pltpu.with_memory_space_constraint(source, pltpu.HBM)] + operands
        specs = [pl.BlockSpec(memory_space=pltpu.HBM)] + specs
        outs.append(pltpu.VMEM((count, source.shape[1]), source.dtype))
        scratch.append(pltpu.SemaphoreType.DMA((4,)))
    return pl.pallas_call(
        kernel,
        in_specs=specs,
        out_specs=[VMEM] * len(outs),
        out_shape=outs,
        scratch_shapes=scratch,
        compiler_params=pltpu.CompilerParams(vmem_limit_bytes=20 << 20),
    )(*operands)


def stacked(q_ref, i):
    first = i * GROUP
    return jnp.concatenate(
        [q_ref[:, (first + g) * HEAD_SIZE : (first + g + 1) * HEAD_SIZE] for g in range(GROUP)], axis=0
    )


def head_of(ref, i):
    return ref[:, i * HEAD_SIZE : (i + 1) * HEAD_SIZE]


def scores_of(k, q):
    return lax.dot_general(k, q, (((1,), (1,)), ((), ())), preferred_element_type=jnp.float32) * SCALE2


def weigh(v, p):
    return lax.dot_general(v, p, (((0,), (0,)), ((), ())), preferred_element_type=jnp.float32)


def thirds(value):
    high = value.astype(jnp.bfloat16).astype(jnp.float32)
    middle = (value - high).astype(jnp.bfloat16).astype(jnp.float32)
    return [high, middle, value - high - middle]


LINES = HEAD_SIZE + 16
PACKED = LINES + HEAD_SIZE


def put_heads(att_ref, i, o):
    rows = att_ref.shape[0]
    o = o.T.astype(jnp.bfloat16)
    for g in range(GROUP):
        head = i * GROUP + g
        att_ref[:, head * HEAD_SIZE : (head + 1) * HEAD_SIZE] = o[g * rows : (g + 1) * rows]


def local_part(pos_ref, q_ref, k_ref, v_ref, i):
    s = scores_of(head_of(k_ref, i), stacked(q_ref, i))
    s = jnp.where(pos_ref[...] >= lax.broadcasted_iota(jnp.int32, s.shape, 0), s, -jnp.inf)
    top = jnp.max(s, axis=0, keepdims=True)
    p = jnp.exp2(s - top)
    return top, jnp.sum(p, axis=0, keepdims=True), weigh(head_of(v_ref, i), p.astype(jnp.bfloat16))


def local_kernel(place_ref, k_ref, v_ref, pos_ref, q_ref, top_ref, total_ref, o_ref):
    for i in range(o_ref.shape[0]):
        top_ref[i], total_ref[i], o_ref[i] = local_part(pos_ref, q_ref, k_ref, v_ref, i)


def moving_kernel(place_ref, k_ref, v_ref, pos_ref, q_ref, pack_ref, att_ref, o_ref):
    for i in range(pack_ref.shape[0]):
        top, total, o = local_part(pos_ref, q_ref, k_ref, v_ref, i)
        pack_ref[i, 0:HEAD_SIZE] = o.astype(jnp.bfloat16)
        lines = thirds(top) + thirds(total)
        lines.append(jnp.zeros((LINES - HEAD_SIZE - len(lines), top.shape[1]), jnp.float32))
        pack_ref[i, HEAD_SIZE:LINES] = jnp.concatenate(lines, axis=0).astype(jnp.bfloat16)
        pack_ref[i, LINES:PACKED] = stacked(q_ref, i).astype(jnp.float32).T.astype(jnp.bfloat16)
        o_ref[i] = o * (1.0 / total)

    @pl.when(place_ref[0] == 0)
    def _own():
        for i in range(pack_ref.shape[0]):
            put_heads(att_ref, i, o_ref[i])


def early_kernel(chips, distances, columns, place_ref, *refs):
    count = len(distances)
    k_refs, v_refs = refs[:count], refs[count : 2 * count]
    pack_ref, *weight_refs, att_ref, theirs_ref, mine_ref = refs[2 * count :]
    for i in range(pack_ref.shape[0]):
        q = pack_ref[i, LINES:PACKED]
        extra = pack_ref[i, HEAD_SIZE:LINES].astype(jnp.float32)
        top = extra[0:1] + extra[1:2] + extra[2:3]
        total = extra[3:4] + extra[4:5] + extra[5:6]
        parts = [
            jnp.dot(head_of(k_ref, i), q, preferred_element_type=jnp.float32) * SCALE2
            + jnp.where(place_ref[0] + 1 >= distance, 0.0, -jnp.inf)
            for distance, k_ref in zip(distances, k_refs)
        ]
        new_top = functools.reduce(jnp.maximum, [top] + [jnp.max(s, axis=0, keepdims=True) for s in parts])
        keep = jnp.exp2(top - new_top)
        total = total * keep
        o = pack_ref[i, 0:HEAD_SIZE].astype(jnp.float32) * keep
        for s, v_ref in zip(parts, v_refs):
            p = jnp.exp2(s - new_top)
            total = total + jnp.sum(p, axis=0, keepdims=True)
            o = o + weigh(head_of(v_ref, i), p.astype(jnp.bfloat16))
        put_heads(att_ref, i, o * (1.0 / total))
    put_pairs(chips, product_of(att_ref[...], weight_refs, columns), theirs_ref, mine_ref)


def product_of(att, weight_refs, columns):
    total, first = None, 0
    for weight_ref in weight_refs:
        last = first + weight_ref.shape[0]
        piece = jnp.dot(
            att[:, first:last], weight_ref[:, columns[0] : columns[1]], preferred_element_type=jnp.float32
        )
        total, first = piece if total is None else total + piece, last
    return total


def put_pairs(chips, product, theirs_ref, mine_ref):
    product = product.astype(jnp.bfloat16)
    part = product.shape[0] // (2 * chips)
    for chip in range(chips):
        block = slice(chip * part, (chip + 1) * part)
        theirs_ref[block, :] = product[2 * chip * part : (2 * chip + 1) * part]
        mine_ref[block, :] = product[(2 * chip + 1) * part : (2 * chip + 2) * part]


def own_kernel(chips, first, source_ref, place_ref, att_ref, _, theirs_ref, mine_ref, weight_ref, total, sems):
    columns = (0, weight_ref.shape[1])
    copies = bring(source_ref, first, weight_ref, sems)
    rows = weight_ref.shape[0] // len(copies)
    for i, copy in enumerate(copies):
        copy.wait()

        @pl.when(place_ref[0] == 0)
        def _project():
            block = slice(i * rows, (i + 1) * rows)
            piece = product_of(att_ref[:, block], [weight_ref.at[block, :]], columns)
            if i:
                piece = piece + total[...]
            if i + 1 < len(copies):
                total[...] = piece
            else:
                put_pairs(chips, piece, theirs_ref, mine_ref)


def pairs_kernel(chips, columns, att_ref, *refs):
    *weight_refs, theirs_ref, mine_ref = refs
    put_pairs(chips, product_of(att_ref[...], weight_refs, columns), theirs_ref, mine_ref)


def seen(place_ref, distance):
    return jnp.where(place_ref[0] >= distance, 0.0, -jnp.inf).astype(jnp.float32)


def middle_kernel(distance, place_ref, q_ref, k_ref, v_ref, top_ref, total_ref, o_ref, top_out, total_out, o_out):
    for i in range(o_ref.shape[0]):
        s = scores_of(head_of(k_ref, i), stacked(q_ref, i)) + seen(place_ref, distance)
        old = top_ref[i]
        top = jnp.maximum(old, jnp.max(s, axis=0, keepdims=True))
        p = jnp.exp2(s - top)
        keep = jnp.exp2(old - top)
        top_out[i] = top
        total_out[i] = total_ref[i] * keep + jnp.sum(p, axis=0, keepdims=True)
        o_out[i] = o_ref[i] * keep + weigh(head_of(v_ref, i), p.astype(jnp.bfloat16))


def last_scores_kernel(distance, place_ref, q_ref, k_ref, top_ref, total_ref, o_ref, w_out, o_out):
    for i in range(o_ref.shape[0]):
        s = scores_of(head_of(k_ref, i), stacked(q_ref, i)) + seen(place_ref, distance)
        old = top_ref[i]
        top = jnp.maximum(old, jnp.max(s, axis=0, keepdims=True))
        p = jnp.exp2(s - top)
        keep = jnp.exp2(old - top)
        inverse = 1.0 / (total_ref[i] * keep + jnp.sum(p, axis=0, keepdims=True))
        w_out[i] = (p * inverse).astype(jnp.bfloat16)
        o_out[i] = o_ref[i] * (keep * inverse)


def put_product(att, weight_refs, columns, out_refs):
    product = product_of(att, weight_refs, columns)
    part = out_refs[0].shape[0]
    for i, out_ref in enumerate(out_refs):
        out_ref[...] = product[i * part : (i + 1) * part].astype(jnp.bfloat16)


def put_values(att_ref, first, w_ref, o_ref, v_ref):
    rows, every = att_ref.shape[0], o_ref.shape[2] // GROUP
    spans = [slice(g * every + first, g * every + first + rows) for g in range(GROUP)]
    for i in range(o_ref.shape[0]):
        w = jnp.concatenate([w_ref[i, :, span] for span in spans], axis=1)
        o = jnp.concatenate([o_ref[i, :, span] for span in spans], axis=1)
        put_heads(att_ref, i, o + weigh(head_of(v_ref, i), w))


def last_values_kernel(pieces, columns, w_ref, o_ref, v_ref, *refs):
    weight_refs, (att_ref, *out_refs) = refs[:pieces], refs[pieces:]
    put_values(att_ref, 0, w_ref, o_ref, v_ref)
    far = len(out_refs) * out_refs[0].shape[0]
    put_product(att_ref[0:far, :], weight_refs, columns, out_refs)


def near_kernel(pieces, first, columns, w_ref, o_ref, v_ref, *refs):
    weight_refs, (theirs_ref, mine_ref, att_ref) = refs[:pieces], refs[pieces:]
    put_values(att_ref, first, w_ref, o_ref, v_ref)
    put_product(att_ref[...], weight_refs, columns, [theirs_ref, mine_ref])


def project_kernel(pieces, first, columns, att_ref, *refs):
    weight_refs, out_refs = refs[:pieces], refs[pieces:]
    count = len(out_refs) * out_refs[0].shape[0]
    put_product(att_ref[first : first + count, :], weight_refs, columns, out_refs)


def finish_kernel(ranges, steps, first, place_ref, mine_ref, got_ref, *refs):
    far_refs, refs = refs[: len(ranges) * steps], list(refs[len(ranges) * steps :])
    sem, staged = refs.pop(), [refs.pop() for _ in ranges][::-1]
    out_ref = refs.pop()
    if not first:
        refs.pop()
    target = None
    if refs:
        own_ref, back_ref = refs
        target = out_ref.at[out_ref.shape[0] - own_ref.shape[0] : out_ref.shape[0]]

        @pl.when(place_ref[0] == 0)
        def _own():
            pltpu.make_async_copy(own_ref, target, sem.at[len(ranges)]).start()

        @pl.when(place_ref[0] != 0)
        def _back():
            pltpu.make_async_copy(back_ref, target, sem.at[len(ranges)]).start()

    copies = []
    for index, columns in enumerate(ranges):
        span = slice(columns[0], columns[1])
        total = mine_ref[:, span].astype(jnp.float32) + got_ref[:, span].astype(jnp.float32)
        for far_ref in far_refs[index * steps : (index + 1) * steps]:
            total = total + far_ref[...].astype(jnp.float32)
        staged[index][...] = total.astype(jnp.bfloat16)
        copies.append(
            pltpu.make_async_copy(staged[index], out_ref.at[0 : mine_ref.shape[0], span], sem.at[index])
        )
        copies[-1].start()
    for copy in copies:
        copy.wait()
    if target is not None:
        pltpu.make_async_copy(back_ref, target, sem.at[len(ranges)]).wait()


def write(kernel, out_shape, scratch, out, *operands, scalars=0):
    operands = [value if i < scalars else in_vmem(value) for i, value in enumerate(operands)]
    specs = [SMEM] * scalars + [VMEM] * (len(operands) - scalars)
    aliases = {}
    if out is not None:
        aliases = {len(operands): 0}
        operands.append(out)
        specs.append(pl.BlockSpec(memory_space=pltpu.HBM))
    return pl.pallas_call(
        kernel,
        in_specs=specs,
        out_specs=pl.BlockSpec(memory_space=pltpu.HBM),
        out_shape=jax.ShapeDtypeStruct(out_shape, jnp.bfloat16),
        scratch_shapes=scratch,
        input_output_aliases=aliases,
        compiler_params=pltpu.CompilerParams(vmem_limit_bytes=8 << 20),
    )(*operands)


def ring(value, axis, distance):
    count = lax.axis_size(axis)
    return lax.ppermute(value, axis, [(s, (s + distance) % count) for s in range(count)])


def pass_on(value, distance):
    count = lax.axis_size("seq")
    return lax.ppermute(value, "seq", [(s, s + distance) for s in range(distance, count - distance)])


def swap(value):
    count = lax.axis_size("head")
    return lax.ppermute(value, "head", [(h, h ^ 1) for h in range(count)])


def tile_of(width):
    return max(t for t in range(128, 1024, 128) if width % t == 0 and (t % 256 == 0 or width % 256))


def on_device(queries, keys, values, out_weight):
    rows, depth = queries.shape
    width = out_weight.shape[1]
    heads = lax.axis_size("head")
    seq_count = lax.axis_size("seq")
    place = lax.axis_index("seq").astype(jnp.int32)[None]
    me = lax.axis_index("head")
    chips = heads // CORES
    part = rows // heads
    kv_local = keys.shape[1] // HEAD_SIZE
    reaches = [1 << level for level in range(seq_count.bit_length() - 1)]
    f32, bf16 = jnp.float32, jnp.bfloat16

    moved = part // 3 if reaches == [1, 2] and part % 48 == 0 else 0
    kept = part - moved
    parts = 2 * chips

    onward = [(s, s + 1) for s in range(seq_count - 1)]
    k_now, v_now = ring(keys, "seq", 1), lax.ppermute(values, "seq", onward)

    chip, core = me // CORES, me % CORES
    owners = []
    for step in range(1, chips + 1):
        base = ((chip + step) % chips) * CORES
        owners += [base + 1 - core, base + core]
    owners = [owner.astype(jnp.uint32) for owner in owners]

    def rows_from(first, count):
        starts = [owner * part + first for owner in owners]
        q = jnp.concatenate([lax.dynamic_slice_in_dim(queries, start, count, 0) for start in starts], axis=0)
        pos = jnp.concatenate([start.astype(jnp.int32) + jnp.arange(count, dtype=jnp.int32) for start in starts])
        return jnp.concatenate([pos] * GROUP)[None], in_vmem(q)

    pos, q = rows_from(0, kept)
    if moved:
        pack, att_own = call(
            moving_kernel,
            [((kv_local, PACKED, GROUP * moved * parts), bf16), ((moved * parts, depth), bf16)],
            place,
            keys,
            values,
            *rows_from(kept, moved),
            scalars=1,
            scratch=[pltpu.VMEM((kv_local, HEAD_SIZE, GROUP * moved * parts), f32)],
        )
        pack = lax.ppermute(pack, "seq", [(s, s - 1) for s in range(1, seq_count)])
        pair_outs = [((moved * chips, width), bf16)] * 2
        *own_parts, weight = call(
            functools.partial(own_kernel, chips),
            pair_outs,
            place,
            att_own,
            pos,
            scalars=1,
            load=(out_weight, 0, depth),
            scratch=[pltpu.VMEM((moved * parts, width), f32)],
        )
    lanes = GROUP * kept * parts
    line, block = (kv_local, 1, lanes), (kv_local, HEAD_SIZE, lanes)
    state = [(line, f32), (line, f32), (block, f32)]
    if moved:
        carried = call(local_kernel, state, place, keys, values, pos, q, scalars=1)
    else:
        kernel = functools.partial(loading, local_kernel)
        load = (out_weight, 0, depth)
        *carried, weight = call(kernel, state, place, keys, values, pos, q, scalars=1, load=load)
    weights = [weight]

    def settle(theirs, mine, everywhere):
        axes = "head" if everywhere else ("seq", "head")
        got = swap(theirs)
        both = mine.astype(f32) + got.astype(f32)
        total = both[(chips - 1) * moved :]
        for step in range(1, chips):
            piece = both[(step - 1) * moved : step * moved].astype(bf16)
            moves = [(h, (h + step * CORES) % heads) for h in range(heads)]
            total = total + lax.ppermute(piece, axes, moves).astype(f32)
        return total.astype(bf16)

    if moved:
        own_rows = settle(*own_parts, False)

    tile = tile_of(width)
    tiles = width // tile
    back = None
    for distance in reaches[:-1]:
        k_here, v_here = k_now, v_now
        k_now = pass_on(k_here, distance)
        v_now = pass_on(v_here, distance)
        if moved:
            border = tile * (tiles // 2)
            halves = [(0, border), (border, width)]
            shapes = [[((moved * chips, c[1] - c[0]), bf16)] * 2 for c in halves]
            att_moved, *early_parts = call(
                functools.partial(early_kernel, chips, reaches, halves[0]),
                [((moved * parts, depth), bf16)] + shapes[0],
                place,
                keys,
                k_here,
                values,
                v_here,
                pack,
                *weights,
                scalars=1,
            )
            late_parts = call(functools.partial(pairs_kernel, chips, halves[1]), shapes[1], att_moved, *weights)
            done = [settle(*early_parts, True), settle(*late_parts, True)]
            back = lax.ppermute(jnp.concatenate(done, axis=1), "seq", onward)
        carried = call(functools.partial(middle_kernel, distance), state, place, q, k_here, v_here, *carried, scalars=1)
    probs, scaled = call(
        functools.partial(last_scores_kernel, reaches[-1]),
        [((kv_local, rows, lanes), bf16), (block, f32)],
        place,
        q,
        k_now,
        *carried,
        scalars=1,
    )

    bounds = sorted({0, tile, tile * max(1, tiles - 2), width})
    chunks = list(zip(bounds[:-1], bounds[1:]))
    far_parts = parts - 2

    def parts_of(count, columns):
        return [((kept, columns[1] - columns[0]), bf16)] * count

    apart = (far_parts * kept) % 128 == 0 and (2 * kept) % 128 == 0
    first_rows = (far_parts if apart else parts) * kept
    att, *first_far = call(
        functools.partial(last_values_kernel, len(weights), chunks[0]),
        [((first_rows, depth), bf16)] + parts_of(far_parts, chunks[0]),
        probs,
        scaled,
        v_now,
        *weights,
    )
    arrived = []
    for index, columns in enumerate(chunks):
        far = first_far
        if index:
            kernel = functools.partial(project_kernel, len(weights), 0, columns)
            far = call(kernel, parts_of(far_parts, columns), att, *weights)
        here = []
        for step in range(1, chips):
            theirs, mine = far[2 * step - 2], far[2 * step - 1]
            got = swap(theirs)
            both = (mine.astype(f32) + got.astype(f32)).astype(bf16)
            here.append(ring(both, "head", step * CORES))
        arrived.append(here)
    whole = (0, width)
    shapes = parts_of(2, whole)
    if apart:
        kernel = functools.partial(near_kernel, len(weights), far_parts * kept, whole)
        att_near = [pltpu.VMEM((2 * kept, depth), bf16)]
        theirs, mine = call(kernel, shapes, probs, scaled, v_now, *weights, scratch=att_near)
    else:
        kernel = functools.partial(project_kernel, len(weights), far_parts * kept, whole)
        theirs, mine = call(kernel, shapes, att, *weights)
    got = swap(theirs)
    out = None
    for group in (range(len(chunks) - 1), range(len(chunks) - 1, len(chunks))):
        ranges = [chunks[i] for i in group]
        last = group.stop == len(chunks)
        out = write(
            functools.partial(finish_kernel, ranges, chips - 1, out is None),
            (part, width),
            [pltpu.VMEM((kept, c[1] - c[0]), bf16) for c in ranges] + [pltpu.SemaphoreType.DMA((len(ranges) + 1,))],
            out,
            place,
            mine,
            got,
            *[value for i in group for value in arrived[i]],
            *([own_rows, back] if moved and last else []),
            scalars=1,
        )
    return out


def solution(mesh):
    in_specs = (
        P(("grp", "seq"), "head"),
        P(("grp", "seq"), "head"),
        P(("grp", "seq"), "head"),
        P("head", None),
    )
    out_specs = P(("grp", "seq", "head"), None)

    return jax.shard_map(on_device, mesh=mesh, in_specs=in_specs, out_specs=out_specs, check_vma=False)
```

```python
import functools
import math

import jax
import jax.numpy as jnp
from jax import lax
from jax.experimental import pallas as pl
from jax.experimental.pallas import tpu as pltpu
from jax.sharding import PartitionSpec as P

QUERY_HEADS = 32
KEY_VALUE_HEADS = 16
HEAD_SIZE = 128
GROUP = QUERY_HEADS // KEY_VALUE_HEADS
CORES = 2

SCALE2 = 168.0**-0.5 * math.log2(math.e)


VMEM = pl.BlockSpec(memory_space=pltpu.VMEM)
SMEM = pl.BlockSpec(memory_space=pltpu.SMEM)


def in_vmem(value):
    return pltpu.with_memory_space_constraint(value, pltpu.VMEM)


def bring(source_ref, first, out_ref, sems):
    pieces = sems.shape[0]
    rows = out_ref.shape[0] // pieces
    copies = []
    for i in range(pieces):
        block = pl.ds(i * rows, rows)
        copies.append(
            pltpu.make_async_copy(source_ref.at[pl.ds(first + i * rows, rows)], out_ref.at[block], sems.at[i])
        )
        copies[-1].start()
    return copies


def loading(kernel, first, source_ref, *refs):
    copies = bring(source_ref, first, *refs[-2:])

    @pl.when(refs[0][0] >= 0)
    def _compute():
        kernel(*refs[:-2])

    for copy in copies:
        copy.wait()


def call(kernel, outs, *operands, scalars=0, load=None, scratch=()):
    operands = [value if i < scalars else in_vmem(value) for i, value in enumerate(operands)]
    specs = [SMEM] * scalars + [VMEM] * (len(operands) - scalars)
    outs = [pltpu.VMEM(shape, dtype) for shape, dtype in outs]
    scratch = list(scratch)
    if load is not None:
        source, first, count = load
        kernel = functools.partial(kernel, first)
        operands = [pltpu.with_memory_space_constraint(source, pltpu.HBM)] + operands
        specs = [pl.BlockSpec(memory_space=pltpu.HBM)] + specs
        outs.append(pltpu.VMEM((count, source.shape[1]), source.dtype))
        scratch.append(pltpu.SemaphoreType.DMA((4,)))
    return pl.pallas_call(
        kernel,
        in_specs=specs,
        out_specs=[VMEM] * len(outs),
        out_shape=outs,
        scratch_shapes=scratch,
        compiler_params=pltpu.CompilerParams(vmem_limit_bytes=20 << 20),
    )(*operands)


def stacked(q_ref, i):
    first = i * GROUP
    return jnp.concatenate(
        [q_ref[:, (first + g) * HEAD_SIZE : (first + g + 1) * HEAD_SIZE] for g in range(GROUP)], axis=0
    )


def head_of(ref, i):
    return ref[:, i * HEAD_SIZE : (i + 1) * HEAD_SIZE]


def scores_of(k, q):
    return lax.dot_general(k, q, (((1,), (1,)), ((), ())), preferred_element_type=jnp.float32) * SCALE2


def weigh(v, p):
    return lax.dot_general(v, p, (((0,), (0,)), ((), ())), preferred_element_type=jnp.float32)


def thirds(value):
    high = value.astype(jnp.bfloat16).astype(jnp.float32)
    middle = (value - high).astype(jnp.bfloat16).astype(jnp.float32)
    return [high, middle, value - high - middle]


LINES = 2 * HEAD_SIZE
PACKED = LINES + 8


def put_heads(att_ref, i, o):
    rows = att_ref.shape[0]
    o = o.T.astype(jnp.bfloat16)
    for g in range(GROUP):
        head = i * GROUP + g
        att_ref[:, head * HEAD_SIZE : (head + 1) * HEAD_SIZE] = o[g * rows : (g + 1) * rows]


def local_part(pos_ref, q_ref, k_ref, v_ref, i):
    s = scores_of(head_of(k_ref, i), stacked(q_ref, i))
    s = jnp.where(pos_ref[...] >= lax.broadcasted_iota(jnp.int32, s.shape, 0), s, -jnp.inf)
    top = jnp.max(s, axis=0, keepdims=True)
    p = jnp.exp2(s - top)
    return top, jnp.sum(p, axis=0, keepdims=True), weigh(head_of(v_ref, i), p.astype(jnp.bfloat16))


def local_kernel(place_ref, k_ref, v_ref, pos_ref, q_ref, top_ref, total_ref, o_ref):
    for i in range(o_ref.shape[0]):
        top_ref[i], total_ref[i], o_ref[i] = local_part(pos_ref, q_ref, k_ref, v_ref, i)


def moving_kernel(place_ref, k_ref, v_ref, pos_ref, q_ref, pack_ref, att_ref, o_ref):
    for i in range(pack_ref.shape[0]):
        top, total, o = local_part(pos_ref, q_ref, k_ref, v_ref, i)
        pack_ref[i, 0:HEAD_SIZE] = stacked(q_ref, i).astype(jnp.float32).T.astype(jnp.bfloat16)
        pack_ref[i, HEAD_SIZE:LINES] = o.astype(jnp.bfloat16)
        lines = thirds(top) + thirds(total)
        lines.append(jnp.zeros((PACKED - LINES - len(lines), top.shape[1]), jnp.float32))
        pack_ref[i, LINES:PACKED] = jnp.concatenate(lines, axis=0).astype(jnp.bfloat16)
        o_ref[i] = o * (1.0 / total)

    @pl.when(place_ref[0] == 0)
    def _own():
        for i in range(pack_ref.shape[0]):
            put_heads(att_ref, i, o_ref[i])


def early_kernel(chips, distances, columns, place_ref, *refs):
    count = len(distances)
    k_refs, v_refs = refs[:count], refs[count : 2 * count]
    pack_ref, *weight_refs, att_ref, theirs_ref, mine_ref = refs[2 * count :]
    for i in range(pack_ref.shape[0]):
        q = pack_ref[i, 0:HEAD_SIZE]
        extra = pack_ref[i, LINES:PACKED].astype(jnp.float32)
        top = extra[0:1] + extra[1:2] + extra[2:3]
        total = extra[3:4] + extra[4:5] + extra[5:6]
        parts = [
            jnp.dot(head_of(k_ref, i), q, preferred_element_type=jnp.float32) * SCALE2
            + jnp.where(place_ref[0] + 1 >= distance, 0.0, -jnp.inf)
            for distance, k_ref in zip(distances, k_refs)
        ]
        new_top = functools.reduce(jnp.maximum, [top] + [jnp.max(s, axis=0, keepdims=True) for s in parts])
        keep = jnp.exp2(top - new_top)
        total = total * keep
        o = pack_ref[i, HEAD_SIZE:LINES].astype(jnp.float32) * keep
        for s, v_ref in zip(parts, v_refs):
            p = jnp.exp2(s - new_top)
            total = total + jnp.sum(p, axis=0, keepdims=True)
            o = o + weigh(head_of(v_ref, i), p.astype(jnp.bfloat16))
        put_heads(att_ref, i, o * (1.0 / total))
    put_pairs(chips, product_of(att_ref[...], weight_refs, columns), theirs_ref, mine_ref)


def product_of(att, weight_refs, columns):
    total, first = None, 0
    for weight_ref in weight_refs:
        last = first + weight_ref.shape[0]
        piece = jnp.dot(
            att[:, first:last], weight_ref[:, columns[0] : columns[1]], preferred_element_type=jnp.float32
        )
        total, first = piece if total is None else total + piece, last
    return total


def put_pairs(chips, product, theirs_ref, mine_ref):
    product = product.astype(jnp.bfloat16)
    part = product.shape[0] // (2 * chips)
    for chip in range(chips):
        block = slice(chip * part, (chip + 1) * part)
        theirs_ref[block, :] = product[2 * chip * part : (2 * chip + 1) * part]
        mine_ref[block, :] = product[(2 * chip + 1) * part : (2 * chip + 2) * part]


def own_kernel(chips, first, source_ref, place_ref, att_ref, _, theirs_ref, mine_ref, weight_ref, total, sems):
    columns = (0, weight_ref.shape[1])
    copies = bring(source_ref, first, weight_ref, sems)
    rows = weight_ref.shape[0] // len(copies)
    for i, copy in enumerate(copies):
        copy.wait()

        @pl.when(place_ref[0] == 0)
        def _project():
            block = slice(i * rows, (i + 1) * rows)
            piece = product_of(att_ref[:, block], [weight_ref.at[block, :]], columns)
            if i:
                piece = piece + total[...]
            if i + 1 < len(copies):
                total[...] = piece
            else:
                put_pairs(chips, piece, theirs_ref, mine_ref)


def pairs_kernel(chips, columns, att_ref, *refs):
    *weight_refs, theirs_ref, mine_ref = refs
    put_pairs(chips, product_of(att_ref[...], weight_refs, columns), theirs_ref, mine_ref)


def seen(place_ref, distance):
    return jnp.where(place_ref[0] >= distance, 0.0, -jnp.inf).astype(jnp.float32)


def middle_kernel(distance, place_ref, q_ref, k_ref, v_ref, top_ref, total_ref, o_ref, top_out, total_out, o_out):
    for i in range(o_ref.shape[0]):
        s = scores_of(head_of(k_ref, i), stacked(q_ref, i)) + seen(place_ref, distance)
        old = top_ref[i]
        top = jnp.maximum(old, jnp.max(s, axis=0, keepdims=True))
        p = jnp.exp2(s - top)
        keep = jnp.exp2(old - top)
        top_out[i] = top
        total_out[i] = total_ref[i] * keep + jnp.sum(p, axis=0, keepdims=True)
        o_out[i] = o_ref[i] * keep + weigh(head_of(v_ref, i), p.astype(jnp.bfloat16))


def last_scores_kernel(distance, place_ref, q_ref, k_ref, top_ref, total_ref, o_ref, w_out, o_out):
    for i in range(o_ref.shape[0]):
        s = scores_of(head_of(k_ref, i), stacked(q_ref, i)) + seen(place_ref, distance)
        old = top_ref[i]
        top = jnp.maximum(old, jnp.max(s, axis=0, keepdims=True))
        p = jnp.exp2(s - top)
        keep = jnp.exp2(old - top)
        inverse = 1.0 / (total_ref[i] * keep + jnp.sum(p, axis=0, keepdims=True))
        w_out[i] = (p * inverse).astype(jnp.bfloat16)
        o_out[i] = o_ref[i] * (keep * inverse)


def put_product(att, weight_refs, columns, out_refs):
    product = product_of(att, weight_refs, columns)
    part = out_refs[0].shape[0]
    for i, out_ref in enumerate(out_refs):
        out_ref[...] = product[i * part : (i + 1) * part].astype(jnp.bfloat16)


def put_values(att_ref, first, w_ref, o_ref, v_ref):
    rows, every = att_ref.shape[0], o_ref.shape[2] // GROUP
    spans = [slice(g * every + first, g * every + first + rows) for g in range(GROUP)]
    for i in range(o_ref.shape[0]):
        w = jnp.concatenate([w_ref[i, :, span] for span in spans], axis=1)
        o = jnp.concatenate([o_ref[i, :, span] for span in spans], axis=1)
        put_heads(att_ref, i, o + weigh(head_of(v_ref, i), w))


def last_values_kernel(pieces, columns, w_ref, o_ref, v_ref, *refs):
    weight_refs, (att_ref, *out_refs) = refs[:pieces], refs[pieces:]
    put_values(att_ref, 0, w_ref, o_ref, v_ref)
    far = len(out_refs) * out_refs[0].shape[0]
    put_product(att_ref[0:far, :], weight_refs, columns, out_refs)


def near_kernel(pieces, first, columns, w_ref, o_ref, v_ref, *refs):
    weight_refs, (theirs_ref, mine_ref, att_ref) = refs[:pieces], refs[pieces:]
    put_values(att_ref, first, w_ref, o_ref, v_ref)
    put_product(att_ref[...], weight_refs, columns, [theirs_ref, mine_ref])


def project_kernel(pieces, first, columns, att_ref, *refs):
    weight_refs, out_refs = refs[:pieces], refs[pieces:]
    count = len(out_refs) * out_refs[0].shape[0]
    put_product(att_ref[first : first + count, :], weight_refs, columns, out_refs)


def finish_kernel(ranges, steps, first, place_ref, mine_ref, got_ref, *refs):
    far_refs, refs = refs[: len(ranges) * steps], list(refs[len(ranges) * steps :])
    sem, staged = refs.pop(), [refs.pop() for _ in ranges][::-1]
    out_ref = refs.pop()
    if not first:
        refs.pop()
    target = None
    if refs:
        own_ref, back_ref = refs
        target = out_ref.at[out_ref.shape[0] - own_ref.shape[0] : out_ref.shape[0]]

        @pl.when(place_ref[0] == 0)
        def _own():
            pltpu.make_async_copy(own_ref, target, sem.at[len(ranges)]).start()

        @pl.when(place_ref[0] != 0)
        def _back():
            pltpu.make_async_copy(back_ref, target, sem.at[len(ranges)]).start()

    copies = []
    for index, columns in enumerate(ranges):
        span = slice(columns[0], columns[1])
        total = mine_ref[:, span].astype(jnp.float32) + got_ref[:, span].astype(jnp.float32)
        for far_ref in far_refs[index * steps : (index + 1) * steps]:
            total = total + far_ref[...].astype(jnp.float32)
        staged[index][...] = total.astype(jnp.bfloat16)
        copies.append(
            pltpu.make_async_copy(staged[index], out_ref.at[0 : mine_ref.shape[0], span], sem.at[index])
        )
        copies[-1].start()
    for copy in copies:
        copy.wait()
    if target is not None:
        pltpu.make_async_copy(back_ref, target, sem.at[len(ranges)]).wait()


def write(kernel, out_shape, scratch, out, *operands, scalars=0):
    operands = [value if i < scalars else in_vmem(value) for i, value in enumerate(operands)]
    specs = [SMEM] * scalars + [VMEM] * (len(operands) - scalars)
    aliases = {}
    if out is not None:
        aliases = {len(operands): 0}
        operands.append(out)
        specs.append(pl.BlockSpec(memory_space=pltpu.HBM))
    return pl.pallas_call(
        kernel,
        in_specs=specs,
        out_specs=pl.BlockSpec(memory_space=pltpu.HBM),
        out_shape=jax.ShapeDtypeStruct(out_shape, jnp.bfloat16),
        scratch_shapes=scratch,
        input_output_aliases=aliases,
        compiler_params=pltpu.CompilerParams(vmem_limit_bytes=8 << 20),
    )(*operands)


def ring(value, axis, distance):
    count = lax.axis_size(axis)
    return lax.ppermute(value, axis, [(s, (s + distance) % count) for s in range(count)])


def pass_on(value, distance):
    count = lax.axis_size("seq")
    return lax.ppermute(value, "seq", [(s, s + distance) for s in range(distance, count - distance)])


def swap(value):
    count = lax.axis_size("head")
    return lax.ppermute(value, "head", [(h, h ^ 1) for h in range(count)])


def tile_of(width):
    return max(t for t in range(128, 1024, 128) if width % t == 0 and (t % 256 == 0 or width % 256))


def on_device(queries, keys, values, out_weight):
    rows, depth = queries.shape
    width = out_weight.shape[1]
    heads = lax.axis_size("head")
    seq_count = lax.axis_size("seq")
    place = lax.axis_index("seq").astype(jnp.int32)[None]
    me = lax.axis_index("head")
    chips = heads // CORES
    part = rows // heads
    kv_local = keys.shape[1] // HEAD_SIZE
    reaches = [1 << level for level in range(seq_count.bit_length() - 1)]
    f32, bf16 = jnp.float32, jnp.bfloat16

    moved = part // 3 if reaches == [1, 2] and part % 48 == 0 else 0
    kept = part - moved
    parts = 2 * chips

    onward = [(s, s + 1) for s in range(seq_count - 1)]
    k_now, v_now = ring(keys, "seq", 1), lax.ppermute(values, "seq", onward)

    chip, core = me // CORES, me % CORES
    owners = []
    for step in range(1, chips + 1):
        base = ((chip + step) % chips) * CORES
        owners += [base + 1 - core, base + core]
    owners = [owner.astype(jnp.uint32) for owner in owners]

    def rows_from(first, count):
        starts = [owner * part + first for owner in owners]
        q = jnp.concatenate([lax.dynamic_slice_in_dim(queries, start, count, 0) for start in starts], axis=0)
        pos = jnp.concatenate([start.astype(jnp.int32) + jnp.arange(count, dtype=jnp.int32) for start in starts])
        return jnp.concatenate([pos] * GROUP)[None], in_vmem(q)

    pos, q = rows_from(0, kept)
    if moved:
        pack, att_own = call(
            moving_kernel,
            [((kv_local, PACKED, GROUP * moved * parts), bf16), ((moved * parts, depth), bf16)],
            place,
            keys,
            values,
            *rows_from(kept, moved),
            scalars=1,
            scratch=[pltpu.VMEM((kv_local, HEAD_SIZE, GROUP * moved * parts), f32)],
        )
        pack = lax.ppermute(pack, "seq", [(s, s - 1) for s in range(1, seq_count)])
        pair_outs = [((moved * chips, width), bf16)] * 2
        *own_parts, weight = call(
            functools.partial(own_kernel, chips),
            pair_outs,
            place,
            att_own,
            pos,
            scalars=1,
            load=(out_weight, 0, depth),
            scratch=[pltpu.VMEM((moved * parts, width), f32)],
        )
    lanes = GROUP * kept * parts
    line, block = (kv_local, 1, lanes), (kv_local, HEAD_SIZE, lanes)
    state = [(line, f32), (line, f32), (block, f32)]
    if moved:
        carried = call(local_kernel, state, place, keys, values, pos, q, scalars=1)
    else:
        kernel = functools.partial(loading, local_kernel)
        load = (out_weight, 0, depth)
        *carried, weight = call(kernel, state, place, keys, values, pos, q, scalars=1, load=load)
    weights = [weight]

    def settle(theirs, mine, everywhere):
        axes = "head" if everywhere else ("seq", "head")
        got = swap(theirs)
        both = mine.astype(f32) + got.astype(f32)
        total = both[(chips - 1) * moved :]
        for step in range(1, chips):
            piece = both[(step - 1) * moved : step * moved].astype(bf16)
            moves = [(h, (h + step * CORES) % heads) for h in range(heads)]
            total = total + lax.ppermute(piece, axes, moves).astype(f32)
        return total.astype(bf16)

    if moved:
        own_rows = settle(*own_parts, False)

    tile = tile_of(width)
    tiles = width // tile
    back = None
    for distance in reaches[:-1]:
        k_here, v_here = k_now, v_now
        k_now = pass_on(k_here, distance)
        v_now = pass_on(v_here, distance)
        if moved:
            border = tile * (tiles // 2)
            halves = [(0, border), (border, width)]
            shapes = [[((moved * chips, c[1] - c[0]), bf16)] * 2 for c in halves]
            att_moved, *early_parts = call(
                functools.partial(early_kernel, chips, reaches, halves[0]),
                [((moved * parts, depth), bf16)] + shapes[0],
                place,
                keys,
                k_here,
                values,
                v_here,
                pack,
                *weights,
                scalars=1,
            )
            late_parts = call(functools.partial(pairs_kernel, chips, halves[1]), shapes[1], att_moved, *weights)
            done = [settle(*early_parts, True), settle(*late_parts, True)]
            back = lax.ppermute(jnp.concatenate(done, axis=1), "seq", onward)
        carried = call(functools.partial(middle_kernel, distance), state, place, q, k_here, v_here, *carried, scalars=1)
    probs, scaled = call(
        functools.partial(last_scores_kernel, reaches[-1]),
        [((kv_local, rows, lanes), bf16), (block, f32)],
        place,
        q,
        k_now,
        *carried,
        scalars=1,
    )

    bounds = sorted({0, tile, tile * ((tiles + 1) // 2), width})
    chunks = list(zip(bounds[:-1], bounds[1:]))
    far_parts = parts - 2

    def parts_of(count, columns):
        return [((kept, columns[1] - columns[0]), bf16)] * count

    apart = (far_parts * kept) % 128 == 0 and (2 * kept) % 128 == 0
    first_rows = (far_parts if apart else parts) * kept
    att, *first_far = call(
        functools.partial(last_values_kernel, len(weights), chunks[0]),
        [((first_rows, depth), bf16)] + parts_of(far_parts, chunks[0]),
        probs,
        scaled,
        v_now,
        *weights,
    )
    arrived = []
    for index, columns in enumerate(chunks):
        far = first_far
        if index:
            kernel = functools.partial(project_kernel, len(weights), 0, columns)
            far = call(kernel, parts_of(far_parts, columns), att, *weights)
        here = []
        for step in range(1, chips):
            theirs, mine = far[2 * step - 2], far[2 * step - 1]
            got = swap(theirs)
            both = (mine.astype(f32) + got.astype(f32)).astype(bf16)
            here.append(ring(both, "head", step * CORES))
        arrived.append(here)
    whole = (0, width)
    shapes = parts_of(2, whole)
    if apart:
        kernel = functools.partial(near_kernel, len(weights), far_parts * kept, whole)
        att_near = [pltpu.VMEM((2 * kept, depth), bf16)]
        theirs, mine = call(kernel, shapes, probs, scaled, v_now, *weights, scratch=att_near)
    else:
        kernel = functools.partial(project_kernel, len(weights), far_parts * kept, whole)
        theirs, mine = call(kernel, shapes, att, *weights)
    got = swap(theirs)
    out = None
    for group in (range(len(chunks) - 1), range(len(chunks) - 1, len(chunks))):
        ranges = [chunks[i] for i in group]
        last = group.stop == len(chunks)
        out = write(
            functools.partial(finish_kernel, ranges, chips - 1, out is None),
            (part, width),
            [pltpu.VMEM((kept, c[1] - c[0]), bf16) for c in ranges] + [pltpu.SemaphoreType.DMA((len(ranges) + 1,))],
            out,
            place,
            mine,
            got,
            *[value for i in group for value in arrived[i]],
            *([own_rows, back] if moved and last else []),
            scalars=1,
        )
    return out


def solution(mesh):
    in_specs = (
        P(("grp", "seq"), "head"),
        P(("grp", "seq"), "head"),
        P(("grp", "seq"), "head"),
        P("head", None),
    )
    out_specs = P(("grp", "seq", "head"), None)

    return jax.shard_map(on_device, mesh=mesh, in_specs=in_specs, out_specs=out_specs, check_vma=False)
```
